256 devices in a mesh: dp: 4 (over x), gx: 16 (over y, z_lo, core), gy: 4 (over z_hi).
Axes of the slice: x: 4, y: 4, z: 8 (z_hi: 4, z_lo: 2; z = z_hi * 2 + z_lo), core: 2. Of those that a mesh axis runs over, the one named last changes fastest.
Arguments:
- field_in: bfloat16 [4, 32, 1024, 1024], P('dp', None, 'gx', 'gy'), parts along dimension 0, may hold values from -6 to 6
- spectral_weight: bfloat16 [32, 32, 2, 128, 128], P(None, None, None, ('gx', 'gy')), may hold values from -6 to 6
- conv_weight: bfloat16 [9, 32, 32], replicated, may hold values from -0.375 to 0.375
- conv_bias: float32 [32], replicated, may hold values from -3 to 3
- upstream: bfloat16 [4, 32, 1024, 1024], P('dp', None, 'gx', 'gy'), parts along dimension 0, may hold values from -6 to 6
Outputs:
- activation: float32 [4, 32, 1024, 1024], P('dp', None, 'gx', 'gy'), parts along dimension 0
- field_grad: float32 [4, 32, 1024, 1024], P('dp', None, 'gx', 'gy'), parts along dimension 0
- weight_grad: float32 [128, 32, 2, 128, 128], P('dp', None, None, ('gx', 'gy')), parts along dimension 0
The draws below stay inside these ranges and needn't reach their ends.
There are 4 independent parts, one for each index of `dp`. The reference program is written for one: setup_inputs(seed, part) draws one part's arguments, and reference() takes and returns one part's arrays. A program takes and returns all parts, laid end to end along the dimension named above; an argument that names none is the same for every part. Nothing has to cross between parts.
All inputs are finite; a program needn't handle non-finite values.
Results may differ from the reference program's by a relative error of at most 0.02.
Values may be sent and summed in bfloat16 or wider, within the bound.
No kernel may reach another device: no remote copies, remote signals or barrier semaphores. Data moves between devices by JAX's collectives and lax.ppermute only.
A program may use at most 128 MiB of HBM per device.

```python
import math
import jax
import jax.numpy as jnp
from jax import lax

C = 32
M1 = 128
M2 = 128
LEV = 1
NX = 1024
NY = 1024


def level_of(rng, extent, pieces, least, high):
    loudness = 1.0
    for axis_at, shards_of in pieces:
        draws = jax.random.uniform(jax.random.fold_in(jax.random.fold_in(rng, 6), axis_at), (shards_of,), jnp.float32, least / len(pieces), high / len(pieces))
        loudness = loudness * jnp.repeat(jnp.exp(draws), extent[axis_at] // shards_of).reshape((-1,) + (1,) * (len(extent) - 1 - axis_at))
    return loudness


def scatter_about(key, extent, deviation, reach, pieces=(), kind=jnp.bfloat16):
    values = jax.random.normal(key, extent, jnp.float32) * deviation
    if len(pieces) > 0:
        values = level_of(key, extent, pieces, -0.22, 0.18) * values
    return jnp.clip(values, min=-reach, max=reach).astype(kind)


def setup_inputs(seed: int = 0, part: int = 0) -> dict:
    keys = jax.random.split(jax.random.key(seed), 6)
    own_keys = jax.random.split(jax.random.fold_in(keys[5], part), 6)
    return {
        "field_in": scatter_about(own_keys[0], (LEV, C, NX, NY), 1.0, 6.0, ((2, 16), (3, 4))),
        "spectral_weight": scatter_about(keys[1], (C, C, 2, M1, M2), 1.0, 6.0, ((3, 64),)),
        "conv_weight": scatter_about(keys[2], (9, C, C), (9 * C) ** -0.5, 0.375),
        "conv_bias": scatter_about(keys[3], (C,), 0.5, 3.0, (), jnp.float32),
        "upstream": scatter_about(own_keys[4], (LEV, C, NX, NY), 1.0, 6.0, ((2, 16), (3, 4))),
    }


def kx_values(index, length, kept):
    return jnp.where(index < kept // 2, index, index + (length - kept)).astype(jnp.int32)


def x_table(modes, positions, length):
    product = (modes[:, None] * positions[None, :]) % length
    angle = product.astype(jnp.float32) * (2.0 * math.pi / length)
    return jnp.stack([jnp.cos(angle), -jnp.sin(angle)], axis=1).astype(jnp.bfloat16)


def y_rows(length, kept, weighted):
    modes = jnp.arange(kept, dtype=jnp.int32)
    places = jnp.arange(length, dtype=jnp.int32)
    angle = ((places[:, None] * modes[None, :]) % length).astype(jnp.float32) * (2.0 * math.pi / length)
    cosine = jnp.cos(angle)
    sine = jnp.sin(angle)
    rows = jnp.stack([jnp.stack([cosine, -sine], axis=1), jnp.stack([sine, cosine], axis=1)], axis=0)
    if weighted:
        rows = rows * jnp.where(modes == 0, 1.0, 2.0).astype(jnp.float32)
    return rows


def fdot(form, left, right):
    return jnp.einsum(form, left.astype(jnp.float32), right.astype(jnp.float32), precision=lax.Precision.HIGHEST)


def forward_chain(field, xtab, ytab, factor):
    spec_x = (fdot("msx,lcxy->mslcy", xtab, field) * factor).astype(jnp.bfloat16)
    return fdot("mslcy,sytq->mtlcq", spec_x, ytab).astype(jnp.bfloat16)


def inverse_chain(spec, ytab, xtab, factor):
    over_y = fdot("mtldq,tqpy->mpldy", spec, ytab).astype(jnp.bfloat16)
    return (fdot("mpldy,mpx->ldxy", over_y, xtab) * factor).astype(jnp.bfloat16)


def mix_modes(spec, weight):
    real_s, imag_s = spec[:, 0], spec[:, 1]
    real_w, imag_w = weight[:, :, 0], weight[:, :, 1]
    form = "mlcq,cdmq->mldq"
    real_v = fdot(form, real_s, real_w) - fdot(form, imag_s, imag_w)
    imag_v = fdot(form, real_s, imag_w) + fdot(form, imag_s, real_w)
    return jnp.stack([real_v, imag_v], axis=1).astype(jnp.bfloat16)


def mix_grads(spec, weight, dmixed):
    real_s, imag_s = spec[:, 0], spec[:, 1]
    real_w, imag_w = weight[:, :, 0], weight[:, :, 1]
    real_d, imag_d = dmixed[:, 0], dmixed[:, 1]
    form_w = "mlcq,mldq->cdmq"
    grad_real = fdot(form_w, real_s, real_d) + fdot(form_w, imag_s, imag_d)
    grad_imag = fdot(form_w, real_s, imag_d) - fdot(form_w, imag_s, real_d)
    form_s = "cdmq,mldq->mlcq"
    dreal = fdot(form_s, real_w, real_d) + fdot(form_s, imag_w, imag_d)
    dimag = fdot(form_s, real_w, imag_d) - fdot(form_s, imag_w, real_d)
    grads = jnp.stack([grad_real, grad_imag], axis=2)
    return grads, jnp.stack([dreal, dimag], axis=1).astype(jnp.bfloat16)


def conv_forward(padded, weight, rows, cols):
    total = jnp.zeros((padded.shape[0], weight.shape[1], rows, cols), jnp.float32)
    for row_tap in range(3):
        for col_tap in range(3):
            window = padded[:, :, row_tap:row_tap + rows, col_tap:col_tap + cols]
            total = total + fdot("dc,lcxy->ldxy", weight[3 * row_tap + col_tap], window)
    return total


def conv_backward(padded, weight, rows, cols):
    total = jnp.zeros((padded.shape[0], weight.shape[2], rows, cols), jnp.float32)
    for row_tap in range(3):
        for col_tap in range(3):
            window = padded[:, :, 2 - row_tap:2 - row_tap + rows, 2 - col_tap:2 - col_tap + cols]
            total = total + fdot("dc,ldxy->lcxy", weight[3 * row_tap + col_tap], window)
    return total


def reference(field_in, spectral_weight, conv_weight, conv_bias, upstream):
    scale = 1.0 / (NX * NY)
    modes = kx_values(jnp.arange(M1, dtype=jnp.int32), NX, M1)
    xtab = x_table(modes, jnp.arange(NX, dtype=jnp.int32), NX)
    plain = y_rows(NY, M2, False)
    weighted = y_rows(NY, M2, True)
    fy_table = plain.astype(jnp.bfloat16)
    ay_table = weighted.astype(jnp.bfloat16)
    gy_table = jnp.transpose(weighted, (2, 3, 0, 1)).astype(jnp.bfloat16)
    by_table = jnp.transpose(plain, (2, 3, 0, 1)).astype(jnp.bfloat16)
    spec = forward_chain(field_in, xtab, fy_table, 1.0)
    mixed = mix_modes(spec, spectral_weight)
    spectral = inverse_chain(mixed, gy_table, xtab, scale)
    rim = ((0, 0), (0, 0), (1, 1), (1, 1))
    padded = jnp.pad(field_in, rim)
    local = conv_forward(padded, conv_weight, NX, NY)
    pre = spectral.astype(jnp.float32) + local + conv_bias[None, :, None, None]
    gate = jax.nn.sigmoid(pre)
    activation = pre * gate
    dpre = (upstream.astype(jnp.float32) * gate * (1.0 + pre * (1.0 - gate))).astype(jnp.bfloat16)
    dspec = forward_chain(dpre, xtab, ay_table, scale)
    weight_grad, dmix = mix_grads(spec, spectral_weight, dspec)
    dfield = inverse_chain(dmix, by_table, xtab, 1.0)
    back_local = conv_backward(jnp.pad(dpre, rim), conv_weight, NX, NY)
    field_grad = dfield.astype(jnp.float32) + back_local
    return activation, field_grad, weight_grad
```

```python
import functools
import math

import jax
import jax.numpy as jnp
import numpy as np
from jax import lax
from jax.experimental import pallas as pl
from jax.experimental.pallas import tpu as pltpu
from jax.sharding import PartitionSpec as P

M1 = 128
M2 = 128
BF = jnp.bfloat16
F32 = jnp.float32


def dot(left, right):
    return jnp.dot(left, right, preferred_element_type=F32)


@functools.lru_cache(maxsize=None)
def x_table(length, owners):
    slots = M1 // owners
    order = np.arange(M1).reshape(owners, slots).T.reshape(-1)
    modes = np.where(order < M1 // 2, order, order + length - M1)
    angle = (modes[:, None] * np.arange(length)[None, :] % length) * (2.0 * math.pi / length)
    table = np.concatenate([np.cos(angle), -np.sin(angle)], axis=0)
    return table.astype(np.float32).astype(jnp.bfloat16)


@functools.lru_cache(maxsize=None)
def y_table(length, width):
    angle = (np.arange(width)[:, None] * np.arange(M2)[None, :] % length) * (2.0 * math.pi / length)
    cosine, sine = np.cos(angle), np.sin(angle)
    table = np.concatenate(
        [np.concatenate([cosine, -sine], axis=1), np.concatenate([sine, cosine], axis=1)], axis=0
    )
    return table.astype(np.float32).astype(jnp.bfloat16)


def turn(values, quarter, sign):
    half = values.shape[1] // 2
    lane = lax.broadcasted_iota(jnp.int32, (1, 2 * half), 1)
    second = lane >= half
    q = jnp.where(second, lane - half, lane)
    step = lax.rem(q * quarter, 4)
    one = jnp.where(step == 0, 1.0, jnp.where(step == 2, -1.0, 0.0))
    imag = jnp.where(step == 1, 1.0, jnp.where(step == 3, -1.0, 0.0)) * sign
    swap = jnp.concatenate([values[:, half:], values[:, :half]], axis=1)
    return values * one + swap * jnp.where(second, imag, -imag)


def column_weight(half):
    lane = lax.broadcasted_iota(jnp.int32, (1, 2 * half), 1)
    return jnp.where((lane == 0) | (lane == half), 1.0, 2.0)


def forward_kernel(weighted, factor, block_ref, x_ref, y_ref, out_ref, rows_ref):
    step = pl.program_id(0)
    slots = out_ref.shape[1] // 4
    owners = out_ref.shape[0]
    width = block_ref.shape[3]
    block = block_ref[:, 0].reshape(-1, width)
    spec_x = dot(x_ref[...], block)
    if factor != 1.0:
        spec_x = spec_x * factor
    spec_x = spec_x.astype(BF)
    spec = dot(spec_x[:M1], y_ref[:width]) + dot(spec_x[M1:], y_ref[width:])
    spec = turn(spec, lax.axis_index("gy"), -1.0)
    if weighted:
        spec = spec * column_weight(M2)
    for slot in range(slots):
        for part in range(2):
            rows_ref[(step * slots + slot) * 2 + part] = spec[
                slot * owners : (slot + 1) * owners, part * M2 : (part + 1) * M2
            ]

    @pl.when(step == 1)
    def _():
        out_ref[...] = jnp.transpose(rows_ref[...], (1, 0, 2)).astype(BF)


def to_modes(block, weighted, factor, length_x, length_y, owners):
    strips, channels, width_x, width_y = block.shape
    slots = M1 // owners
    rows = channels * slots * 2
    return pl.pallas_call(
        functools.partial(forward_kernel, weighted, factor),
        grid=(channels,),
        in_specs=[
            pl.BlockSpec((strips, 1, width_x, width_y), lambda c: (0, c, 0, 0)),
            pl.BlockSpec((2 * M1, length_x), lambda c: (0, 0)),
            pl.BlockSpec((2 * width_y, 2 * M2), lambda c: (0, 0)),
        ],
        out_specs=pl.BlockSpec((owners, rows, M2), lambda c: (0, 0, 0)),
        out_shape=jax.ShapeDtypeStruct((owners, rows, M2), BF),
        scratch_shapes=[pltpu.VMEM((rows, owners, M2), F32)],
        name="to_modes",
    )(block, x_table(length_x, owners), y_table(length_y, width_y))


def inverse_kernel(weighted, factor, spec_ref, x_ref, y_ref, out_ref, rows_ref):
    step = pl.program_id(0)
    slots = spec_ref.shape[1] // 4
    width = out_ref.shape[3]

    @pl.when(step == 0)
    def _():
        rows_ref[...] = jnp.transpose(spec_ref[...].astype(F32), (1, 0, 2))

    spec = jnp.concatenate(
        [
            jnp.concatenate(
                [rows_ref[(step * slots + slot) * 2], rows_ref[(step * slots + slot) * 2 + 1]],
                axis=1,
            )
            for slot in range(slots)
        ],
        axis=0,
    )
    spec = turn(spec, lax.axis_index("gy"), 1.0)
    if weighted:
        spec = spec * column_weight(M2)
    over_y = dot(spec.astype(BF), y_ref[...]).astype(BF)
    over_y = jnp.concatenate([over_y[:, :width], over_y[:, width:]], axis=0)
    total = dot(x_ref[...], over_y)
    if factor != 1.0:
        total = total * factor
    out_ref[:, 0] = total.astype(BF).reshape(out_ref.shape[0], out_ref.shape[2], width)


def to_field(spec, weighted, factor, length_x, length_y, strips, width_y):
    owners, rows, _ = spec.shape
    slots = M1 // owners
    channels = rows // slots // 2
    width_x = length_x // strips
    return pl.pallas_call(
        functools.partial(inverse_kernel, weighted, factor),
        grid=(channels,),
        in_specs=[
            pl.BlockSpec((owners, rows, M2), lambda c: (0, 0, 0)),
            pl.BlockSpec((length_x, 2 * M1), lambda c: (0, 0)),
            pl.BlockSpec((2 * M2, 2 * width_y), lambda c: (0, 0)),
        ],
        out_specs=pl.BlockSpec((strips, 1, width_x, width_y), lambda c: (0, c, 0, 0)),
        out_shape=jax.ShapeDtypeStruct((strips, channels, width_x, width_y), BF),
        scratch_shapes=[pltpu.VMEM((rows, owners, M2), F32)],
        name="to_field",
    )(
        spec,
        np.ascontiguousarray(x_table(length_x, owners).T),
        np.ascontiguousarray(y_table(length_y, width_y).T),
    )


CONV_ROWS = 4


def conv_matrix(weight):
    outs, ins = weight.shape[1:]
    band = jnp.transpose(weight.reshape(3, 3, outs, ins), (1, 2, 0, 3)).reshape(3 * outs, 3 * ins)
    return jnp.concatenate(
        [
            jnp.pad(band, ((0, 0), (row * ins, (CONV_ROWS - 1 - row) * ins)))
            for row in range(CONV_ROWS)
        ],
        axis=0,
    )


def conv_kernel(matrix_ref, main_ref, side_ref, out_ref):
    step = pl.program_id(0)
    ins = matrix_ref.shape[1] // (CONV_ROWS + 2)
    outs = out_ref.shape[0]
    tall = out_ref.shape[1]
    width = out_ref.shape[2]
    window = (CONV_ROWS + 2) * ins
    pieces = []
    for part in range(tall // CONV_ROWS):
        start = pl.multiple_of((step * tall + part * CONV_ROWS) * ins, ins)
        main = dot(matrix_ref[...], main_ref[pl.ds(start, window), :])
        side = dot(matrix_ref[...], side_ref[pl.ds(start, window), :])
        taps = jnp.concatenate([main, side], axis=1)
        full = taps.shape[1]
        for row in range(CONV_ROWS):
            base = row * 3 * outs
            low = pltpu.roll(taps[base : base + outs], 1, 1)[:, :width]
            mid = taps[base + outs : base + 2 * outs, :width]
            high = pltpu.roll(taps[base + 2 * outs : base + 3 * outs], full - 1, 1)[:, :width]
            pieces.append(low + mid + high)
    out_ref[...] = jnp.transpose(jnp.stack(pieces, axis=0), (1, 0, 2))


def conv(weight, main, side, rows):
    outs = weight.shape[1]
    width = main.shape[1]
    matrix = conv_matrix(weight)
    tall = 8
    return pl.pallas_call(
        conv_kernel,
        grid=(rows // tall,),
        in_specs=[
            pl.BlockSpec(matrix.shape, lambda k: (0, 0)),
            pl.BlockSpec(main.shape, lambda k: (0, 0)),
            pl.BlockSpec(side.shape, lambda k: (0, 0)),
        ],
        out_specs=pl.BlockSpec((outs, tall, width), lambda k: (0, k, 0)),
        out_shape=jax.ShapeDtypeStruct((outs, rows, width), F32),
        name="conv",
    )(matrix, main, side)


def swap(value, axis, back=False):
    count = lax.axis_size(axis)
    pairs = [(i, i + 1) for i in range(count - 1)]
    if back:
        pairs = [(b, a) for a, b in pairs]
    return lax.ppermute(value, axis, pairs)


def halo(field):
    channels, rows, width = field.shape
    top = swap(field[:, rows - 1], "gx")
    bottom = swap(field[:, 0], "gx", back=True)
    main = jnp.concatenate([top[None], jnp.transpose(field, (1, 0, 2)), bottom[None]], axis=0)
    main = main.reshape((rows + 2) * channels, width)
    pick = np.zeros((2, width), np.float32)
    pick[0, 0] = pick[1, width - 1] = 1.0
    ends = jnp.einsum("ry,ny->rn", pick.astype(BF), main, preferred_element_type=F32).astype(BF)
    right = swap(ends[:1], "gy", back=True)
    left = swap(ends[1:], "gy")
    place = np.zeros((2, 128), np.float32)
    place[0, 0] = place[1, 127] = 1.0
    side = jnp.einsum(
        "rn,rk->nk", jnp.concatenate([right, left]), place.astype(BF), preferred_element_type=F32
    ).astype(BF)
    return main, side


def gather_modes(parts, strips):
    owners, rows, kept = parts.shape
    slots = M1 // owners
    split = parts.reshape(strips, owners // strips, rows // slots // 2, slots, 2, kept)
    total = jnp.sum(split.astype(F32), axis=1).astype(BF)
    return jnp.transpose(total, (2, 3, 0, 1, 4)).reshape(slots, 2, -1, kept)


def spread_modes(spec, strips, pieces):
    slots, _, channels, kept = spec.shape
    split = jnp.transpose(spec.reshape(slots, 2, strips, channels // strips, kept), (2, 3, 0, 1, 4))
    split = jnp.broadcast_to(
        split.reshape(strips, 1, -1, kept), (strips, pieces, 2 * slots * channels // strips, kept)
    )
    return split.reshape(strips * pieces, -1, kept)


def exchange(value, axes):
    return lax.all_to_all(value, axes, split_axis=0, concat_axis=0, tiled=True)


def pdot(form, left, right):
    return jnp.einsum(form, left, right, preferred_element_type=F32)


def mix_modes(spec, weight):
    real_s, imag_s = (spec[:, 0], spec[:, 1])
    real_w, imag_w = (weight[:, :, 0], weight[:, :, 1])
    form = "mcq,cdmq->mdq"
    real_v = pdot(form, real_s, real_w) - pdot(form, imag_s, imag_w)
    imag_v = pdot(form, real_s, imag_w) + pdot(form, imag_s, real_w)
    return jnp.stack([real_v, imag_v], axis=1).astype(BF)


def mix_grads(spec, weight, dmixed):
    real_s, imag_s = (spec[:, 0], spec[:, 1])
    real_w, imag_w = (weight[:, :, 0], weight[:, :, 1])
    real_d, imag_d = (dmixed[:, 0], dmixed[:, 1])
    form_w = "mcq,mdq->cdmq"
    grad_real = pdot(form_w, real_s, real_d) + pdot(form_w, imag_s, imag_d)
    grad_imag = pdot(form_w, real_s, imag_d) - pdot(form_w, imag_s, real_d)
    form_s = "cdmq,mdq->mcq"
    dreal = pdot(form_s, real_w, real_d) + pdot(form_s, imag_w, imag_d)
    dimag = pdot(form_s, real_w, imag_d) - pdot(form_s, imag_w, real_d)
    grads = jnp.stack([grad_real, grad_imag], axis=2)
    return (grads, jnp.stack([dreal, dimag], axis=1).astype(BF))


def body(field_in, spectral_weight, conv_weight, conv_bias, upstream):
    strips, pieces = lax.axis_size("gx"), lax.axis_size("gy")
    owners = strips * pieces
    _, channels, width_x, width_y = field_in.shape
    length_x, length_y = width_x * strips, width_y * pieces
    scale = 1.0 / (length_x * length_y)
    both = ("gx", "gy")
    share = (strips, channels // strips, width_x, width_y)
    whole = (channels, width_x, width_y)

    field = field_in[0]
    block = exchange(field.reshape(share), "gx")
    parts = to_modes(block, False, 1.0, length_x, length_y, owners)
    spec = gather_modes(exchange(parts, both), strips)
    main, side = halo(field)
    local = conv(conv_weight, main, side, width_x)
    mixed = mix_modes(spec, spectral_weight)
    arrived = exchange(spread_modes(mixed, strips, pieces), both)
    back = to_field(arrived, True, scale, length_x, length_y, strips, width_y)
    spectral = exchange(back, "gx").reshape(whole)

    pre = spectral.astype(F32) + local + conv_bias[:, None, None]
    gate = jax.nn.sigmoid(pre)
    activation = pre * gate
    dpre = (upstream[0].astype(F32) * gate * (1.0 + pre * (1.0 - gate))).astype(BF)

    dblock = exchange(dpre.reshape(share), "gx")
    dparts = to_modes(dblock, True, scale, length_x, length_y, owners)
    dspec = gather_modes(exchange(dparts, both), strips)
    dmain, dside = halo(dpre)
    back_local = conv(jnp.transpose(conv_weight[::-1], (0, 2, 1)), dmain, dside, width_x)
    weight_grad, dmix = mix_grads(spec, spectral_weight, dspec)
    darrived = exchange(spread_modes(dmix, strips, pieces), both)
    dback = to_field(darrived, False, 1.0, length_x, length_y, strips, width_y)
    dfield = exchange(dback, "gx").reshape(whole)
    field_grad = dfield.astype(F32) + back_local
    return (activation[None], field_grad[None], weight_grad)


def solution(mesh):
    return jax.shard_map(
        body,
        mesh=mesh,
        in_specs=(
            P("dp", None, "gx", "gy"),
            P(None, None, None, ("gx", "gy"), None),
            P(),
            P(),
            P("dp", None, "gx", "gy"),
        ),
        out_specs=(
            P("dp", None, "gx", "gy"),
            P("dp", None, "gx", "gy"),
            P("dp", None, None, ("gx", "gy"), None),
        ),
        check_vma=False,
    )
```

```python
import functools
import math

import jax
import jax.numpy as jnp
import numpy as np
from jax import lax
from jax.experimental import pallas as pl
from jax.experimental.pallas import tpu as pltpu
from jax.sharding import PartitionSpec as P

M1 = 128
M2 = 128
BF = jnp.bfloat16
F32 = jnp.float32


def dot(left, right):
    return jnp.dot(left, right, preferred_element_type=F32)


@functools.lru_cache(maxsize=None)
def x_table(length, owners):
    slots = M1 // owners
    order = np.arange(M1).reshape(owners, slots).T.reshape(-1)
    modes = np.where(order < M1 // 2, order, order + length - M1)
    angle = (modes[:, None] * np.arange(length)[None, :] % length) * (2.0 * math.pi / length)
    table = np.concatenate([np.cos(angle), -np.sin(angle)], axis=0)
    return table.astype(np.float32).astype(jnp.bfloat16)


@functools.lru_cache(maxsize=None)
def y_table(length, width):
    angle = (np.arange(width)[:, None] * np.arange(M2)[None, :] % length) * (2.0 * math.pi / length)
    cosine, sine = np.cos(angle), np.sin(angle)
    table = np.concatenate(
        [np.concatenate([cosine, -sine], axis=1), np.concatenate([sine, cosine], axis=1)], axis=0
    )
    return table.astype(np.float32).astype(jnp.bfloat16)


def turn(values, quarter, sign):
    half = values.shape[1] // 2
    lane = lax.broadcasted_iota(jnp.int32, (1, 2 * half), 1)
    second = lane >= half
    q = jnp.where(second, lane - half, lane)
    step = lax.rem(q * quarter, 4)
    one = jnp.where(step == 0, 1.0, jnp.where(step == 2, -1.0, 0.0))
    imag = jnp.where(step == 1, 1.0, jnp.where(step == 3, -1.0, 0.0)) * sign
    swap = jnp.concatenate([values[:, half:], values[:, :half]], axis=1)
    return values * one + swap * jnp.where(second, imag, -imag)


def column_weight(half):
    lane = lax.broadcasted_iota(jnp.int32, (1, 2 * half), 1)
    return jnp.where((lane == 0) | (lane == half), 1.0, 2.0)


def resident(value):
    return pltpu.with_memory_space_constraint(value, pltpu.VMEM)


def on_chip(kernel, outs, scratch, name, *values):
    spec = pl.BlockSpec(memory_space=pltpu.VMEM)
    many = isinstance(outs, list)
    return pl.pallas_call(
        kernel,
        in_specs=[spec] * len(values),
        out_specs=[spec] * len(outs) if many else spec,
        out_shape=[pltpu.VMEM(*out) for out in outs] if many else pltpu.VMEM(*outs),
        scratch_shapes=scratch,
        compiler_params=pltpu.CompilerParams(vmem_limit_bytes=48 << 20),
        name=name,
    )(*[resident(value) for value in values])


def forward_kernel(weighted, factor, block_ref, x_ref, y_ref, out_ref, rows_ref):
    owners, rows, _ = out_ref.shape
    _, channels, _, width = block_ref.shape
    slots = M1 // owners
    for channel in range(channels):
        block = block_ref[:, channel].reshape(-1, width)
        spec_x = dot(x_ref[...], block)
        if factor != 1.0:
            spec_x = spec_x * factor
        spec_x = spec_x.astype(BF)
        spec = dot(spec_x[:M1], y_ref[:width]) + dot(spec_x[M1:], y_ref[width:])
        spec = turn(spec, lax.axis_index("gy"), -1.0)
        if weighted:
            spec = spec * column_weight(M2)
        for slot in range(slots):
            for part in range(2):
                rows_ref[(channel * slots + slot) * 2 + part] = spec[
                    slot * owners : (slot + 1) * owners, part * M2 : (part + 1) * M2
                ]
    out_ref[...] = jnp.transpose(rows_ref[...], (1, 0, 2)).astype(BF)


def to_modes(block, weighted, factor, tables, owners):
    rows = block.shape[1] * (M1 // owners) * 2
    return on_chip(
        functools.partial(forward_kernel, weighted, factor),
        ((owners, rows, M2), BF),
        [pltpu.VMEM((rows, owners, M2), F32)],
        "to_modes",
        block,
        tables[0],
        tables[1],
    )


def inverse_kernel(weighted, factor, spec_ref, x_ref, y_ref, out_ref, rows_ref):
    owners = spec_ref.shape[0]
    strips, channels, rows, width = out_ref.shape
    slots = M1 // owners
    rows_ref[...] = jnp.transpose(spec_ref[...].astype(F32), (1, 0, 2))
    for channel in range(channels):
        spec = jnp.concatenate(
            [
                jnp.concatenate(
                    [rows_ref[(channel * slots + slot) * 2 + part] for part in range(2)], axis=1
                )
                for slot in range(slots)
            ],
            axis=0,
        )
        spec = turn(spec, lax.axis_index("gy"), 1.0)
        if weighted:
            spec = spec * column_weight(M2)
        over_y = dot(spec.astype(BF), y_ref[...]).astype(BF)
        over_y = jnp.concatenate([over_y[:, :width], over_y[:, width:]], axis=0)
        total = dot(x_ref[...], over_y)
        if factor != 1.0:
            total = total * factor
        out_ref[:, channel] = total.astype(BF).reshape(strips, rows, width)


def to_field(spec, weighted, factor, tables, shape):
    owners, rows, _ = spec.shape
    return on_chip(
        functools.partial(inverse_kernel, weighted, factor),
        (shape, BF),
        [pltpu.VMEM((rows, owners, M2), F32)],
        "to_field",
        spec,
        tables[2],
        tables[3],
    )


def mix_kernel(sign, parts_ref, weight_ref, out_ref, spec_ref, sum_ref, mixed_ref, place_ref):
    strips, rows, kept = spec_ref.shape
    pieces = parts_ref.shape[0] // strips
    slots, _, ins, outs, _ = weight_ref.shape
    share = ins // strips
    total = jnp.sum(parts_ref[...].reshape(strips, pieces, rows, kept).astype(F32), axis=1).astype(BF)
    spec_ref[...] = total
    sum_ref[...] = total.astype(F32)
    for slot in range(slots):
        real = jnp.zeros((outs, kept), F32)
        imag = jnp.zeros((outs, kept), F32)
        for channel in range(ins):
            strip, row = channel // share, (channel % share * slots + slot) * 2
            real_s = sum_ref[strip, row : row + 1, :]
            imag_s = sum_ref[strip, row + 1 : row + 2, :]
            real_w = weight_ref[slot, 0, channel].astype(F32)
            imag_w = weight_ref[slot, 1, channel].astype(F32)
            if sign > 0:
                real = real + (real_s * real_w - imag_s * imag_w)
                imag = imag + (real_s * imag_w + imag_s * real_w)
            else:
                real = real + (real_s * real_w + imag_s * imag_w)
                imag = imag + (imag_s * real_w - real_s * imag_w)
        mixed_ref[slot * 2] = real
        mixed_ref[slot * 2 + 1] = imag
    share = outs // strips
    for channel in range(share):
        for row in range(2 * slots):
            place_ref[:, channel * 2 * slots + row, :] = mixed_ref[
                row, pl.ds(channel, strips, stride=share), :
            ]
    placed = place_ref[...].astype(BF)
    out_ref[...] = jnp.broadcast_to(placed[:, None], (strips, pieces, rows, kept)).reshape(
        strips * pieces, rows, kept
    )


def mix(parts, weight, sign, strips):
    owners, rows, kept = parts.shape
    slots, _, _, outs, _ = weight.shape
    return on_chip(
        functools.partial(mix_kernel, sign),
        [((owners, rows, kept), BF), ((strips, rows, kept), BF)],
        [
            pltpu.VMEM((strips, rows, kept), F32),
            pltpu.VMEM((2 * slots, outs, kept), F32),
            pltpu.VMEM((strips, rows, kept), F32),
        ],
        "mix",
        parts,
        weight,
    )


def by_mode(rows, slots):
    strips, count, kept = rows.shape
    split = rows.reshape(strips, count // slots // 2, slots, 2, kept)
    return jnp.transpose(split, (2, 3, 0, 1, 4)).reshape(slots, 2, -1, kept)


CONV_ROWS = 4


def conv_matrix(weight):
    outs, ins = weight.shape[1:]
    band = jnp.transpose(weight.reshape(3, 3, outs, ins), (1, 2, 0, 3)).reshape(3 * outs, 3 * ins)
    return jnp.concatenate(
        [
            jnp.pad(band, ((0, 0), (row * ins, (CONV_ROWS - 1 - row) * ins)))
            for row in range(CONV_ROWS)
        ],
        axis=0,
    )


def conv_kernel(matrix_ref, main_ref, side_ref, out_ref):
    ins = matrix_ref.shape[1] // (CONV_ROWS + 2)
    outs, rows, width = out_ref.shape
    window = (CONV_ROWS + 2) * ins
    tall = 2 * CONV_ROWS

    @pl.loop(0, rows // tall)
    def _(step):
        pieces = []
        for part in range(tall // CONV_ROWS):
            start = pl.multiple_of((step * tall + part * CONV_ROWS) * ins, ins)
            main = dot(matrix_ref[...], main_ref[pl.ds(start, window), :])
            side = dot(matrix_ref[...], side_ref[pl.ds(start, window), :])
            taps = jnp.concatenate([main, side], axis=1)
            full = taps.shape[1]
            for row in range(CONV_ROWS):
                base = row * 3 * outs
                low = pltpu.roll(taps[base : base + outs], 1, 1)[:, :width]
                mid = taps[base + outs : base + 2 * outs, :width]
                high = pltpu.roll(taps[base + 2 * outs : base + 3 * outs], full - 1, 1)[:, :width]
                pieces.append(low + mid + high)
        first = pl.multiple_of(step * tall, tall)
        out_ref[:, pl.ds(first, tall), :] = jnp.transpose(jnp.stack(pieces, axis=0), (1, 0, 2))


def conv(matrix, main, side, rows):
    outs = matrix.shape[0] // (3 * CONV_ROWS)
    return on_chip(
        conv_kernel, ((outs, rows, main.shape[1]), F32), [], "conv", matrix, main, side
    )


def swap(value, axis, back=False):
    count = lax.axis_size(axis)
    pairs = [(i, i + 1) for i in range(count - 1)]
    if back:
        pairs = [(b, a) for a, b in pairs]
    return lax.ppermute(value, axis, pairs)


def rows_halo(field):
    channels, rows, width = field.shape
    top = swap(field[:, rows - 1], "gx")
    bottom = swap(field[:, 0], "gx", back=True)
    main = jnp.concatenate([top[None], jnp.transpose(field, (1, 0, 2)), bottom[None]], axis=0)
    main = main.reshape((rows + 2) * channels, width)
    pick = np.zeros((2, width), np.float32)
    pick[0, 0] = pick[1, width - 1] = 1.0
    ends = jnp.einsum("ry,ny->rn", pick.astype(BF), main, preferred_element_type=F32).astype(BF)
    return main, ends


def columns_halo(ends):
    right = swap(ends[:1], "gy", back=True)
    left = swap(ends[1:], "gy")
    place = np.zeros((2, 128), np.float32)
    place[0, 0] = place[1, 127] = 1.0
    return jnp.einsum(
        "rn,rk->nk", jnp.concatenate([right, left]), place.astype(BF), preferred_element_type=F32
    ).astype(BF)


def exchange(value, axes):
    return lax.all_to_all(value, axes, split_axis=0, concat_axis=0, tiled=True)


def pdot(form, left, right):
    return jnp.einsum(form, left, right, preferred_element_type=F32)


def weight_grads(spec, dmixed):
    real_s, imag_s = (spec[:, 0], spec[:, 1])
    real_d, imag_d = (dmixed[:, 0], dmixed[:, 1])
    form_w = "mcq,mdq->cdmq"
    grad_real = pdot(form_w, real_s, real_d) + pdot(form_w, imag_s, imag_d)
    grad_imag = pdot(form_w, real_s, imag_d) - pdot(form_w, imag_s, real_d)
    return jnp.stack([grad_real, grad_imag], axis=2)


def body(field_in, spectral_weight, conv_weight, conv_bias, upstream):
    strips, pieces = lax.axis_size("gx"), lax.axis_size("gy")
    owners = strips * pieces
    _, channels, width_x, width_y = field_in.shape
    length_x, length_y = width_x * strips, width_y * pieces
    scale = 1.0 / (length_x * length_y)
    both = ("gx", "gy")
    share = (strips, channels // strips, width_x, width_y)
    whole = (channels, width_x, width_y)

    table_x, table_y = x_table(length_x, owners), y_table(length_y, width_y)
    tables = [
        jnp.asarray(np.ascontiguousarray(table))
        for table in (table_x, table_y, table_x.T, table_y.T)
    ]
    hold = lax.optimization_barrier

    field = field_in[0]
    matrix = conv_matrix(conv_weight)
    dmatrix = conv_matrix(jnp.transpose(conv_weight[::-1], (0, 2, 1)))
    weight = jnp.transpose(spectral_weight, (3, 2, 0, 1, 4))
    dweight = jnp.transpose(spectral_weight, (3, 2, 1, 0, 4))
    block = exchange(field.reshape(share), "gx")
    main, ends = rows_halo(field)
    block, ends, matrix, dmatrix, weight, dweight = hold(
        (block, ends, matrix, dmatrix, weight, dweight)
    )
    parts = exchange(to_modes(block, False, 1.0, tables, owners), both)
    side = columns_halo(ends)
    parts, side = hold((parts, side))
    mixed, spec = mix(parts, weight, 1, strips)
    arrived = exchange(mixed, both)
    local = conv(matrix, main, side, width_x)
    arrived, local = hold((arrived, local))
    back = to_field(arrived, True, scale, tables, share)
    spectral = exchange(back, "gx").reshape(whole)

    pre = spectral.astype(F32) + local + conv_bias[:, None, None]
    gate = jax.nn.sigmoid(pre)
    activation = pre * gate
    dpre = (upstream[0].astype(F32) * gate * (1.0 + pre * (1.0 - gate))).astype(BF)

    dblock = exchange(dpre.reshape(share), "gx")
    dmain, dends = rows_halo(dpre)
    dblock, dends = hold((dblock, dends))
    dparts = exchange(to_modes(dblock, True, scale, tables, owners), both)
    dside = columns_halo(dends)
    dparts, dside = hold((dparts, dside))
    dmixed, dspec = mix(dparts, dweight, -1, strips)
    darrived = exchange(dmixed, both)
    back_local = conv(dmatrix, dmain, dside, width_x)
    darrived, back_local = hold((darrived, back_local))
    dback = to_field(darrived, False, 1.0, tables, share)
    dfield = exchange(dback, "gx").reshape(whole)
    slots = M1 // owners
    weight_grad = weight_grads(by_mode(spec, slots), by_mode(dspec, slots))
    dfield, weight_grad = hold((dfield, weight_grad))
    field_grad = dfield.astype(F32) + back_local
    return (activation[None], field_grad[None], weight_grad)


def solution(mesh):
    return jax.shard_map(
        body,
        mesh=mesh,
        in_specs=(
            P("dp", None, "gx", "gy"),
            P(None, None, None, ("gx", "gy"), None),
            P(),
            P(),
            P("dp", None, "gx", "gy"),
        ),
        out_specs=(
            P("dp", None, "gx", "gy"),
            P("dp", None, "gx", "gy"),
            P("dp", None, None, ("gx", "gy"), None),
        ),
        check_vma=False,
    )
```

```python
import functools
import math

import jax
import jax.numpy as jnp
import numpy as np
from jax import lax
from jax.experimental import pallas as pl
from jax.experimental.pallas import tpu as pltpu
from jax.sharding import PartitionSpec as P

M1 = 128
M2 = 128
BF = jnp.bfloat16
F32 = jnp.float32


def dot(left, right):
    return jnp.dot(left, right, preferred_element_type=F32)


@functools.lru_cache(maxsize=None)
def x_table(length, owners):
    slots = M1 // owners
    order = np.arange(M1).reshape(owners, slots).T.reshape(-1)
    modes = np.where(order < M1 // 2, order, order + length - M1)
    angle = (modes[:, None] * np.arange(length)[None, :] % length) * (2.0 * math.pi / length)
    table = np.concatenate([np.cos(angle), -np.sin(angle)], axis=0)
    return table.astype(np.float32).astype(jnp.bfloat16)


@functools.lru_cache(maxsize=None)
def y_table(length, width):
    angle = (np.arange(width)[:, None] * np.arange(M2)[None, :] % length) * (2.0 * math.pi / length)
    cosine, sine = np.cos(angle), np.sin(angle)
    table = np.concatenate(
        [np.concatenate([cosine, -sine], axis=1), np.concatenate([sine, cosine], axis=1)], axis=0
    )
    return table.astype(np.float32).astype(jnp.bfloat16)


def turn(values, quarter, sign):
    half = values.shape[1] // 2
    lane = lax.broadcasted_iota(jnp.int32, (1, 2 * half), 1)
    second = lane >= half
    q = jnp.where(second, lane - half, lane)
    step = lax.rem(q * quarter, 4)
    one = jnp.where(step == 0, 1.0, jnp.where(step == 2, -1.0, 0.0))
    imag = jnp.where(step == 1, 1.0, jnp.where(step == 3, -1.0, 0.0)) * sign
    swap = jnp.concatenate([values[:, half:], values[:, :half]], axis=1)
    return values * one + swap * jnp.where(second, imag, -imag)


def column_weight(half):
    lane = lax.broadcasted_iota(jnp.int32, (1, 2 * half), 1)
    return jnp.where((lane == 0) | (lane == half), 1.0, 2.0)


def resident(value):
    return pltpu.with_memory_space_constraint(value, pltpu.VMEM)


def on_chip(kernel, outs, scratch, name, *values, place=pltpu.VMEM):
    spec = pl.BlockSpec(memory_space=pltpu.VMEM)
    many = isinstance(outs, list)
    return pl.pallas_call(
        kernel,
        in_specs=[spec] * len(values),
        out_specs=[spec] * len(outs) if many else spec,
        out_shape=[place(*out) for out in outs] if many else place(*outs),
        scratch_shapes=scratch,
        compiler_params=pltpu.CompilerParams(vmem_limit_bytes=48 << 20),
        name=name,
    )(*[resident(value) for value in values])


def forward_kernel(weighted, factor, block_ref, x_ref, y_ref, out_ref, rows_ref):
    owners, rows, _ = out_ref.shape
    _, channels, _, width = block_ref.shape
    slots = M1 // owners
    for channel in range(channels):
        block = block_ref[:, channel].reshape(-1, width)
        spec_x = dot(x_ref[...], block)
        if factor != 1.0:
            spec_x = spec_x * factor
        spec_x = spec_x.astype(BF)
        spec = dot(spec_x[:M1], y_ref[:width]) + dot(spec_x[M1:], y_ref[width:])
        spec = turn(spec, lax.axis_index("gy"), -1.0)
        if weighted:
            spec = spec * column_weight(M2)
        for slot in range(slots):
            for part in range(2):
                rows_ref[(channel * slots + slot) * 2 + part] = spec[
                    slot * owners : (slot + 1) * owners, part * M2 : (part + 1) * M2
                ]
    out_ref[...] = jnp.transpose(rows_ref[...], (1, 0, 2)).astype(BF)


def to_modes(block, weighted, factor, tables, owners):
    rows = block.shape[1] * (M1 // owners) * 2
    return on_chip(
        functools.partial(forward_kernel, weighted, factor),
        ((owners, rows, M2), BF),
        [pltpu.VMEM((rows, owners, M2), F32)],
        "to_modes",
        block,
        tables[0],
        tables[1],
        place=jax.ShapeDtypeStruct,
    )


def inverse_kernel(weighted, factor, spec_ref, x_ref, y_ref, out_ref, rows_ref):
    owners = spec_ref.shape[0]
    strips, channels, rows, width = out_ref.shape
    slots = M1 // owners
    rows_ref[...] = jnp.transpose(spec_ref[...].astype(F32), (1, 0, 2))
    for channel in range(channels):
        spec = jnp.concatenate(
            [
                jnp.concatenate(
                    [rows_ref[(channel * slots + slot) * 2 + part] for part in range(2)], axis=1
                )
                for slot in range(slots)
            ],
            axis=0,
        )
        spec = turn(spec, lax.axis_index("gy"), 1.0)
        if weighted:
            spec = spec * column_weight(M2)
        over_y = dot(spec.astype(BF), y_ref[...]).astype(BF)
        over_y = jnp.concatenate([over_y[:, :width], over_y[:, width:]], axis=0)
        total = dot(x_ref[...], over_y)
        if factor != 1.0:
            total = total * factor
        out_ref[:, channel] = total.astype(BF).reshape(strips, rows, width)


def to_field(spec, weighted, factor, tables, shape):
    owners, rows, _ = spec.shape
    return on_chip(
        functools.partial(inverse_kernel, weighted, factor),
        (shape, BF),
        [pltpu.VMEM((rows, owners, M2), F32)],
        "to_field",
        spec,
        tables[2],
        tables[3],
    )


def mix_kernel(sign, parts_ref, weight_ref, out_ref, spec_ref, sum_ref, mixed_ref, place_ref):
    strips, rows, kept = spec_ref.shape
    pieces = parts_ref.shape[0] // strips
    slots, _, ins, outs, _ = weight_ref.shape
    share = ins // strips
    total = jnp.sum(parts_ref[...].reshape(strips, pieces, rows, kept).astype(F32), axis=1).astype(BF)
    spec_ref[...] = total
    sum_ref[...] = total.astype(F32)
    for slot in range(slots):
        real = jnp.zeros((outs, kept), F32)
        imag = jnp.zeros((outs, kept), F32)
        for channel in range(ins):
            strip, row = channel // share, (channel % share * slots + slot) * 2
            real_s = sum_ref[strip, row : row + 1, :]
            imag_s = sum_ref[strip, row + 1 : row + 2, :]
            real_w = weight_ref[slot, 0, channel].astype(F32)
            imag_w = weight_ref[slot, 1, channel].astype(F32)
            if sign > 0:
                real = real + (real_s * real_w - imag_s * imag_w)
                imag = imag + (real_s * imag_w + imag_s * real_w)
            else:
                real = real + (real_s * real_w + imag_s * imag_w)
                imag = imag + (imag_s * real_w - real_s * imag_w)
        mixed_ref[slot * 2] = real
        mixed_ref[slot * 2 + 1] = imag
    share = outs // strips
    for channel in range(share):
        for row in range(2 * slots):
            place_ref[:, channel * 2 * slots + row, :] = mixed_ref[
                row, pl.ds(channel, strips, stride=share), :
            ]
    placed = place_ref[...].astype(BF)
    out_ref[...] = jnp.broadcast_to(placed[:, None], (strips, pieces, rows, kept)).reshape(
        strips * pieces, rows, kept
    )


def mix(parts, weight, sign, strips):
    owners, rows, kept = parts.shape
    slots, _, _, outs, _ = weight.shape
    return on_chip(
        functools.partial(mix_kernel, sign),
        [((owners, rows, kept), BF), ((strips, rows, kept), BF)],
        [
            pltpu.VMEM((strips, rows, kept), F32),
            pltpu.VMEM((2 * slots, outs, kept), F32),
            pltpu.VMEM((strips, rows, kept), F32),
        ],
        "mix",
        parts,
        weight,
    )


def by_mode(rows, slots):
    strips, count, kept = rows.shape
    split = rows.reshape(strips, count // slots // 2, slots, 2, kept)
    return jnp.transpose(split, (2, 3, 0, 1, 4)).reshape(slots, 2, -1, kept)


CONV_ROWS = 4


def conv_matrix(weight):
    outs, ins = weight.shape[1:]
    band = jnp.transpose(weight.reshape(3, 3, outs, ins), (1, 2, 0, 3)).reshape(3 * outs, 3 * ins)
    return jnp.concatenate(
        [
            jnp.pad(band, ((0, 0), (row * ins, (CONV_ROWS - 1 - row) * ins)))
            for row in range(CONV_ROWS)
        ],
        axis=0,
    )


def conv_kernel(matrix_ref, main_ref, side_ref, out_ref):
    ins = matrix_ref.shape[1] // (CONV_ROWS + 2)
    outs, rows, width = out_ref.shape
    window = (CONV_ROWS + 2) * ins
    tall = 2 * CONV_ROWS

    @pl.loop(0, rows // tall)
    def _(step):
        pieces = []
        for part in range(tall // CONV_ROWS):
            start = pl.multiple_of((step * tall + part * CONV_ROWS) * ins, ins)
            main = dot(matrix_ref[...], main_ref[pl.ds(start, window), :])
            side = dot(matrix_ref[...], side_ref[pl.ds(start, window), :])
            taps = jnp.concatenate([main, side], axis=1)
            full = taps.shape[1]
            for row in range(CONV_ROWS):
                base = row * 3 * outs
                low = pltpu.roll(taps[base : base + outs], 1, 1)[:, :width]
                mid = taps[base + outs : base + 2 * outs, :width]
                high = pltpu.roll(taps[base + 2 * outs : base + 3 * outs], full - 1, 1)[:, :width]
                pieces.append(low + mid + high)
        first = pl.multiple_of(step * tall, tall)
        out_ref[:, pl.ds(first, tall), :] = jnp.transpose(jnp.stack(pieces, axis=0), (1, 0, 2))


def conv(matrix, main, side, rows):
    outs = matrix.shape[0] // (3 * CONV_ROWS)
    return on_chip(
        conv_kernel, ((outs, rows, main.shape[1]), F32), [], "conv", matrix, main, side
    )


def swap(value, axis, back=False):
    count = lax.axis_size(axis)
    pairs = [(i, i + 1) for i in range(count - 1)]
    if back:
        pairs = [(b, a) for a, b in pairs]
    return lax.ppermute(value, axis, pairs)


def across_rows(field):
    return swap(field[:, -1], "gx"), swap(field[:, 0], "gx", back=True)


def stack_rows(field, above, below):
    channels, rows, width = field.shape
    main = jnp.concatenate([above[None], jnp.transpose(field, (1, 0, 2)), below[None]], axis=0)
    main = main.reshape((rows + 2) * channels, width)
    pick = np.zeros((2, width), np.float32)
    pick[0, 0] = pick[1, width - 1] = 1.0
    ends = jnp.einsum("ry,ny->rn", pick.astype(BF), main, preferred_element_type=F32).astype(BF)
    return main, ends


def across_columns(ends):
    return swap(ends[:1], "gy", back=True), swap(ends[1:], "gy")


def place_columns(right, left):
    place = np.zeros((2, 128), np.float32)
    place[0, 0] = place[1, 127] = 1.0
    return jnp.einsum(
        "rn,rk->nk", jnp.concatenate([right, left]), place.astype(BF), preferred_element_type=F32
    ).astype(BF)


def exchange(value, axes):
    return lax.all_to_all(value, axes, split_axis=0, concat_axis=0, tiled=True)


def pdot(form, left, right):
    return jnp.einsum(form, left, right, preferred_element_type=F32)


def weight_grads(spec, dmixed):
    real_s, imag_s = (spec[:, 0], spec[:, 1])
    real_d, imag_d = (dmixed[:, 0], dmixed[:, 1])
    form_w = "mcq,mdq->cdmq"
    grad_real = pdot(form_w, real_s, real_d) + pdot(form_w, imag_s, imag_d)
    grad_imag = pdot(form_w, real_s, imag_d) - pdot(form_w, imag_s, real_d)
    return jnp.stack([grad_real, grad_imag], axis=2)


def body(field_in, spectral_weight, conv_weight, conv_bias, upstream):
    strips, pieces = lax.axis_size("gx"), lax.axis_size("gy")
    owners = strips * pieces
    _, channels, width_x, width_y = field_in.shape
    length_x, length_y = width_x * strips, width_y * pieces
    scale = 1.0 / (length_x * length_y)
    both = ("gx", "gy")
    share = (strips, channels // strips, width_x, width_y)
    whole = (channels, width_x, width_y)

    table_x, table_y = x_table(length_x, owners), y_table(length_y, width_y)
    live = lax.axis_index("gx") < strips
    tables = [
        jnp.where(live, np.ascontiguousarray(table), jnp.zeros((), BF))
        for table in (table_x, table_y, table_x.T, table_y.T)
    ]
    hold = lax.optimization_barrier

    field = field_in[0]
    block = exchange(field.reshape(share), "gx")
    above, below = across_rows(field)
    main, ends = stack_rows(field, above, below)
    weight = jnp.transpose(spectral_weight, (3, 2, 0, 1, 4))
    block, main, ends, weight, tables = hold((block, main, ends, weight, tables))
    parts = exchange(to_modes(block, False, 1.0, tables, owners), both)
    parts, ends = hold((parts, ends))
    mixed, spec = mix(parts, weight, 1, strips)
    arrived = exchange(mixed, both)
    right, left = across_columns(ends)
    back = to_field(arrived, True, scale, tables, share)
    back, right, left, raw, dweight = hold((back, right, left, conv_weight, spectral_weight))
    spectral = exchange(back, "gx").reshape(whole)
    local = conv(conv_matrix(raw), main, place_columns(right, left), width_x)
    dmatrix = conv_matrix(jnp.transpose(raw[::-1], (0, 2, 1)))
    dweight = jnp.transpose(dweight, (3, 2, 1, 0, 4))
    spectral, local, dmatrix, dweight = hold((spectral, local, dmatrix, dweight))

    pre = spectral.astype(F32) + local + conv_bias[:, None, None]
    gate = jax.nn.sigmoid(pre)
    activation = pre * gate
    dpre = (upstream[0].astype(F32) * gate * (1.0 + pre * (1.0 - gate))).astype(BF)

    dblock = exchange(dpre.reshape(share), "gx")
    dabove, dbelow = across_rows(dpre)
    dparts = to_modes(dblock, True, scale, tables, owners)
    dparts, dhere, dabove, dbelow = hold((dparts, dpre, dabove, dbelow))
    dparts = exchange(dparts, both)
    dmain, dends = stack_rows(dhere, dabove, dbelow)
    dparts, dends, dmain = hold((dparts, dends, dmain))
    dmixed, dspec = mix(dparts, dweight, -1, strips)
    darrived = exchange(dmixed, both)
    dright, dleft = across_columns(dends)
    dback = to_field(darrived, False, 1.0, tables, share)
    dback, dright, dleft, spec, dspec = hold((dback, dright, dleft, spec, dspec))
    dfield = exchange(dback, "gx").reshape(whole)
    back_local = conv(dmatrix, dmain, place_columns(dright, dleft), width_x)
    slots = M1 // owners
    weight_grad = weight_grads(by_mode(spec, slots), by_mode(dspec, slots))
    dfield, back_local, weight_grad = hold((dfield, back_local, weight_grad))
    field_grad = dfield.astype(F32) + back_local
    return (activation[None], field_grad[None], weight_grad)


def solution(mesh):
    return jax.shard_map(
        body,
        mesh=mesh,
        in_specs=(
            P("dp", None, "gx", "gy"),
            P(None, None, None, ("gx", "gy"), None),
            P(),
            P(),
            P("dp", None, "gx", "gy"),
        ),
        out_specs=(
            P("dp", None, "gx", "gy"),
            P("dp", None, "gx", "gy"),
            P("dp", None, None, ("gx", "gy"), None),
        ),
        check_vma=False,
    )
```

```python
import functools
import math

import jax
import jax.numpy as jnp
import numpy as np
from jax import lax
from jax.experimental import pallas as pl
from jax.experimental.pallas import tpu as pltpu
from jax.sharding import PartitionSpec as P

M1 = 128
M2 = 128
BF = jnp.bfloat16
F32 = jnp.float32


def dot(left, right):
    return jnp.dot(left, right, preferred_element_type=F32)


@functools.lru_cache(maxsize=None)
def x_table(length, owners):
    slots = M1 // owners
    order = np.arange(M1).reshape(owners, slots).T.reshape(-1)
    modes = np.where(order < M1 // 2, order, order + length - M1)
    angle = (modes[:, None] * np.arange(length)[None, :] % length) * (2.0 * math.pi / length)
    table = np.concatenate([np.cos(angle), -np.sin(angle)], axis=0)
    return table.astype(np.float32).astype(jnp.bfloat16)


@functools.lru_cache(maxsize=None)
def y_table(length, width):
    angle = (np.arange(width)[:, None] * np.arange(M2)[None, :] % length) * (2.0 * math.pi / length)
    cosine, sine = np.cos(angle), np.sin(angle)
    table = np.concatenate(
        [np.concatenate([cosine, -sine], axis=1), np.concatenate([sine, cosine], axis=1)], axis=0
    )
    return table.astype(np.float32).astype(jnp.bfloat16)


def turn(values, quarter, sign):
    half = values.shape[1] // 2
    lane = lax.broadcasted_iota(jnp.int32, (1, 2 * half), 1)
    second = lane >= half
    q = jnp.where(second, lane - half, lane)
    step = lax.rem(q * quarter, 4)
    one = jnp.where(step == 0, 1.0, jnp.where(step == 2, -1.0, 0.0))
    imag = jnp.where(step == 1, 1.0, jnp.where(step == 3, -1.0, 0.0)) * sign
    swap = jnp.concatenate([values[:, half:], values[:, :half]], axis=1)
    return values * one + swap * jnp.where(second, imag, -imag)


def column_weight(half):
    lane = lax.broadcasted_iota(jnp.int32, (1, 2 * half), 1)
    return jnp.where((lane == 0) | (lane == half), 1.0, 2.0)


def resident(value):
    return pltpu.with_memory_space_constraint(value, pltpu.VMEM)


def on_chip(kernel, outs, scratch, name, *values, place=pltpu.VMEM):
    spec = pl.BlockSpec(memory_space=pltpu.VMEM)
    many = isinstance(outs, list)
    return pl.pallas_call(
        kernel,
        in_specs=[spec] * len(values),
        out_specs=[spec] * len(outs) if many else spec,
        out_shape=[place(*out) for out in outs] if many else place(*outs),
        scratch_shapes=scratch,
        compiler_params=pltpu.CompilerParams(vmem_limit_bytes=24 << 20),
        name=name,
    )(*[resident(value) for value in values])


def forward_kernel(weighted, factor, block_hbm, x_ref, y_ref, out_ref, rows_ref, block_ref, sems):
    owners, rows, _ = out_ref.shape
    channels, _, _, width = block_ref.shape
    slots = M1 // owners
    copies = [
        pltpu.make_async_copy(block_hbm.at[:, channel], block_ref.at[channel], sems.at[channel])
        for channel in range(channels)
    ]
    for copy in copies:
        copy.start()
    for channel in range(channels):
        copies[channel].wait()
        block = block_ref[channel].reshape(-1, width)
        spec_x = dot(x_ref[...], block)
        if factor != 1.0:
            spec_x = spec_x * factor
        spec_x = spec_x.astype(BF)
        spec = dot(spec_x[:M1], y_ref[:width]) + dot(spec_x[M1:], y_ref[width:])
        spec = turn(spec, lax.axis_index("gy"), -1.0)
        if weighted:
            spec = spec * column_weight(M2)
        for slot in range(slots):
            for part in range(2):
                rows_ref[(channel * slots + slot) * 2 + part] = spec[
                    slot * owners : (slot + 1) * owners, part * M2 : (part + 1) * M2
                ]
    out_ref[...] = jnp.transpose(rows_ref[...], (1, 0, 2)).astype(BF)


def to_modes(block, weighted, factor, tables, owners):
    strips, channels, width_x, width_y = block.shape
    rows = channels * (M1 // owners) * 2
    vmem = pl.BlockSpec(memory_space=pltpu.VMEM)
    return pl.pallas_call(
        functools.partial(forward_kernel, weighted, factor),
        in_specs=[pl.BlockSpec(memory_space=pltpu.HBM), vmem, vmem],
        out_specs=vmem,
        out_shape=jax.ShapeDtypeStruct((owners, rows, M2), BF),
        scratch_shapes=[
            pltpu.VMEM((rows, owners, M2), F32),
            pltpu.VMEM((channels, strips, width_x, width_y), BF),
            pltpu.SemaphoreType.DMA((channels,)),
        ],
        compiler_params=pltpu.CompilerParams(vmem_limit_bytes=24 << 20),
        name="to_modes",
    )(block, resident(tables[0]), resident(tables[1]))


CHUNK = 4


def stream_kernel(step, count, *refs):
    ins, held, out = refs[:count], refs[count], refs[count + 1]
    bufs, out_buf, in_sems, out_sems = refs[count + 2 : -3], refs[-3], refs[-2], refs[-1]
    pieces = [pl.ds(first, CHUNK) for first in range(0, out_buf.shape[0], CHUNK)]
    loads = [
        [
            pltpu.make_async_copy(ref.at[piece], buf.at[piece], in_sems.at[index, place])
            for index, (ref, buf) in enumerate(zip(ins, bufs))
        ]
        for place, piece in enumerate(pieces)
    ]
    stores = [
        pltpu.make_async_copy(out_buf.at[piece], out.at[piece], out_sems.at[place])
        for place, piece in enumerate(pieces)
    ]
    for load in loads:
        for copy in load:
            copy.start()
    for piece, load, store in zip(pieces, loads, stores):
        for copy in load:
            copy.wait()
        out_buf[piece] = step(held[piece], *[buf[piece] for buf in bufs])
        store.start()
    for store in stores:
        store.wait()


def stream(step, held, values, dtype, name):
    shape = held.shape
    pieces = shape[0] // CHUNK
    hbm = pl.BlockSpec(memory_space=pltpu.HBM)
    return pl.pallas_call(
        functools.partial(stream_kernel, step, len(values)),
        in_specs=[hbm] * len(values) + [pl.BlockSpec(memory_space=pltpu.VMEM)],
        out_specs=hbm,
        out_shape=jax.ShapeDtypeStruct(shape, dtype),
        scratch_shapes=[pltpu.VMEM(shape, value.dtype) for value in values]
        + [
            pltpu.VMEM(shape, dtype),
            pltpu.SemaphoreType.DMA((len(values), pieces)),
            pltpu.SemaphoreType.DMA((pieces,)),
        ],
        compiler_params=pltpu.CompilerParams(vmem_limit_bytes=24 << 20),
        name=name,
    )(*[pltpu.with_memory_space_constraint(value, pltpu.HBM) for value in values], resident(held))


def gate_grad(local, spectral, upstream):
    pre = spectral.astype(F32) + local
    gate = 0.5 + 0.5 * jnp.tanh(0.5 * pre)
    return (upstream.astype(F32) * gate * (1.0 + pre * (1.0 - gate))).astype(BF)


def add_field(local, field):
    return field.astype(F32) + local


def inverse_kernel(weighted, factor, spec_ref, x_ref, y_ref, out_ref, rows_ref):
    owners = spec_ref.shape[0]
    strips, channels, rows, width = out_ref.shape
    slots = M1 // owners
    rows_ref[...] = jnp.transpose(spec_ref[...].astype(F32), (1, 0, 2))
    for channel in range(channels):
        spec = jnp.concatenate(
            [
                jnp.concatenate(
                    [rows_ref[(channel * slots + slot) * 2 + part] for part in range(2)], axis=1
                )
                for slot in range(slots)
            ],
            axis=0,
        )
        spec = turn(spec, lax.axis_index("gy"), 1.0)
        if weighted:
            spec = spec * column_weight(M2)
        over_y = dot(spec.astype(BF), y_ref[...]).astype(BF)
        over_y = jnp.concatenate([over_y[:, :width], over_y[:, width:]], axis=0)
        total = dot(x_ref[...], over_y)
        if factor != 1.0:
            total = total * factor
        out_ref[:, channel] = total.astype(BF).reshape(strips, rows, width)


def to_field(spec, weighted, factor, tables, shape):
    owners, rows, _ = spec.shape
    return on_chip(
        functools.partial(inverse_kernel, weighted, factor),
        (shape, BF),
        [pltpu.VMEM((rows, owners, M2), F32)],
        "to_field",
        spec,
        tables[2],
        tables[3],
    )


def mix_kernel(sign, parts_ref, weight_ref, out_ref, spec_ref, sum_ref, mixed_ref, place_ref):
    strips, rows, kept = spec_ref.shape
    pieces = parts_ref.shape[0] // strips
    slots, _, ins, outs, _ = weight_ref.shape
    share = ins // strips
    total = jnp.sum(parts_ref[...].reshape(strips, pieces, rows, kept).astype(F32), axis=1).astype(BF)
    spec_ref[...] = total
    sum_ref[...] = total.astype(F32)
    for slot in range(slots):
        real = jnp.zeros((outs, kept), F32)
        imag = jnp.zeros((outs, kept), F32)
        for channel in range(ins):
            strip, row = channel // share, (channel % share * slots + slot) * 2
            real_s = sum_ref[strip, row : row + 1, :]
            imag_s = sum_ref[strip, row + 1 : row + 2, :]
            real_w = weight_ref[slot, 0, channel].astype(F32)
            imag_w = weight_ref[slot, 1, channel].astype(F32)
            if sign > 0:
                real = real + (real_s * real_w - imag_s * imag_w)
                imag = imag + (real_s * imag_w + imag_s * real_w)
            else:
                real = real + (real_s * real_w + imag_s * imag_w)
                imag = imag + (imag_s * real_w - real_s * imag_w)
        mixed_ref[slot * 2] = real
        mixed_ref[slot * 2 + 1] = imag
    share = outs // strips
    for channel in range(share):
        for row in range(2 * slots):
            place_ref[:, channel * 2 * slots + row, :] = mixed_ref[
                row, pl.ds(channel, strips, stride=share), :
            ]
    placed = place_ref[...].astype(BF)
    out_ref[...] = jnp.broadcast_to(placed[:, None], (strips, pieces, rows, kept)).reshape(
        strips * pieces, rows, kept
    )


def mix(parts, weight, sign, strips):
    owners, rows, kept = parts.shape
    slots, _, _, outs, _ = weight.shape
    return on_chip(
        functools.partial(mix_kernel, sign),
        [((owners, rows, kept), BF), ((strips, rows, kept), BF)],
        [
            pltpu.VMEM((strips, rows, kept), F32),
            pltpu.VMEM((2 * slots, outs, kept), F32),
            pltpu.VMEM((strips, rows, kept), F32),
        ],
        "mix",
        parts,
        weight,
    )


def by_mode(rows, slots):
    strips, count, kept = rows.shape
    split = rows.reshape(strips, count // slots // 2, slots, 2, kept)
    return jnp.transpose(split, (2, 3, 0, 1, 4)).reshape(slots, 2, -1, kept)


CONV_ROWS = 4


def conv_matrix(weight):
    outs, ins = weight.shape[1:]
    band = jnp.transpose(weight.reshape(3, 3, outs, ins), (1, 2, 0, 3)).reshape(3 * outs, 3 * ins)
    return jnp.concatenate(
        [
            jnp.pad(band, ((0, 0), (row * ins, (CONV_ROWS - 1 - row) * ins)))
            for row in range(CONV_ROWS)
        ],
        axis=0,
    )


def conv_kernel(matrix_ref, main_ref, side_ref, bias_ref, out_ref):
    ins = matrix_ref.shape[1] // (CONV_ROWS + 2)
    outs, rows, width = out_ref.shape
    window = (CONV_ROWS + 2) * ins
    tall = 2 * CONV_ROWS

    @pl.loop(0, rows // tall)
    def _(step):
        pieces = []
        for part in range(tall // CONV_ROWS):
            start = pl.multiple_of((step * tall + part * CONV_ROWS) * ins, ins)
            main = dot(matrix_ref[...], main_ref[pl.ds(start, window), :])
            side = dot(matrix_ref[...], side_ref[pl.ds(start, window), :])
            taps = jnp.concatenate([main, side], axis=1)
            full = taps.shape[1]
            for row in range(CONV_ROWS):
                base = row * 3 * outs
                low = pltpu.roll(taps[base : base + outs], 1, 1)[:, :width]
                mid = taps[base + outs : base + 2 * outs, :width]
                high = pltpu.roll(taps[base + 2 * outs : base + 3 * outs], full - 1, 1)[:, :width]
                pieces.append(low + mid + high + bias_ref[:, :1])
        first = pl.multiple_of(step * tall, tall)
        out_ref[:, pl.ds(first, tall), :] = jnp.transpose(jnp.stack(pieces, axis=0), (1, 0, 2))


def conv(matrix, main, side, bias, rows):
    outs = matrix.shape[0] // (3 * CONV_ROWS)
    return on_chip(
        conv_kernel, ((outs, rows, main.shape[1]), F32), [], "conv", matrix, main, side, bias
    )


def swap(value, axis, back=False):
    count = lax.axis_size(axis)
    pairs = [(i, i + 1) for i in range(count - 1)]
    if back:
        pairs = [(b, a) for a, b in pairs]
    return lax.ppermute(value, axis, pairs)


def across_rows(field):
    return swap(field[:, -1], "gx"), swap(field[:, 0], "gx", back=True)


def stack_rows(field, above, below):
    channels, rows, width = field.shape
    main = jnp.concatenate([above[None], jnp.transpose(field, (1, 0, 2)), below[None]], axis=0)
    main = main.reshape((rows + 2) * channels, width)
    pick = np.zeros((2, width), np.float32)
    pick[0, 0] = pick[1, width - 1] = 1.0
    ends = jnp.einsum("ry,ny->rn", pick.astype(BF), main, preferred_element_type=F32).astype(BF)
    return main, ends


def across_columns(ends):
    return swap(ends[:1], "gy", back=True), swap(ends[1:], "gy")


def side_slots():
    place = np.zeros((2, 128), np.float32)
    place[0, 0] = place[1, 127] = 1.0
    return place.astype(BF)


def place_columns(right, left, slots):
    return jnp.einsum(
        "rn,rk->nk", jnp.concatenate([right, left]), slots, preferred_element_type=F32
    ).astype(BF)


def exchange(value, axes):
    return lax.all_to_all(value, axes, split_axis=0, concat_axis=0, tiled=True)


def pdot(form, left, right):
    return jnp.einsum(form, left, right, preferred_element_type=F32)


def weight_grads(spec, dmixed):
    real_s, imag_s = (spec[:, 0], spec[:, 1])
    real_d, imag_d = (dmixed[:, 0], dmixed[:, 1])
    form_w = "mcq,mdq->cdmq"
    grad_real = pdot(form_w, real_s, real_d) + pdot(form_w, imag_s, imag_d)
    grad_imag = pdot(form_w, real_s, imag_d) - pdot(form_w, imag_s, real_d)
    return jnp.stack([grad_real, grad_imag], axis=2)


def body(field_in, spectral_weight, conv_weight, conv_bias, upstream):
    strips, pieces = lax.axis_size("gx"), lax.axis_size("gy")
    owners = strips * pieces
    _, channels, width_x, width_y = field_in.shape
    length_x, length_y = width_x * strips, width_y * pieces
    scale = 1.0 / (length_x * length_y)
    both = ("gx", "gy")
    share = (strips, channels // strips, width_x, width_y)
    whole = (channels, width_x, width_y)

    table_x, table_y = x_table(length_x, owners), y_table(length_y, width_y)
    live = lax.axis_index("gx") < strips
    tables = [
        jnp.where(live, np.ascontiguousarray(table), jnp.zeros((), BF))
        for table in (table_x, table_y, table_x.T, table_y.T)
    ]
    bias = jnp.broadcast_to(conv_bias[:, None], (channels, 128))
    hold = lax.optimization_barrier

    field = field_in[0]
    block = exchange(field.reshape(share), "gx")
    above, below = across_rows(field)
    main, ends = stack_rows(field, above, below)
    weight = jnp.transpose(spectral_weight, (3, 2, 0, 1, 4))
    block, ends, weight = hold((block, ends, weight))
    parts = exchange(to_modes(block, False, 1.0, tables, owners), both)
    parts, ends = hold((parts, ends))
    mixed, spec = mix(parts, weight, 1, strips)
    arrived = exchange(mixed, both)
    right, left = across_columns(ends)
    back = to_field(arrived, True, scale, tables, share)
    back, right, places, taps = hold((back, right, side_slots(), conv_weight))
    spectral = exchange(back, "gx").reshape(whole)
    local = conv(conv_matrix(taps), main, place_columns(right, left, places), bias, width_x)
    spectral, local = hold((spectral, local))

    dpre = stream(gate_grad, local, [spectral, upstream[0]], BF, "gate_grad")
    dpre, spectral, local, taps, dweight = hold((dpre, spectral, local, conv_weight, spectral_weight))

    dblock = exchange(dpre.reshape(share), "gx")
    dabove, dbelow = across_rows(dpre)
    pre = spectral.astype(F32) + local
    activation = pre * jax.nn.sigmoid(pre)
    dblock, activation, dweight, taps = hold((dblock, activation, dweight, taps))
    dparts = to_modes(dblock, True, scale, tables, owners)
    dparts, dhere, dabove, dbelow = hold((dparts, dpre, dabove, dbelow))
    dparts = exchange(dparts, both)
    dmatrix = conv_matrix(jnp.transpose(taps[::-1], (0, 2, 1)))
    dweight = jnp.transpose(dweight, (3, 2, 1, 0, 4))
    dmain, dends = stack_rows(dhere, dabove, dbelow)
    dparts, dends, dmain, dmatrix, dweight = hold((dparts, dends, dmain, dmatrix, dweight))
    dmixed, dspec = mix(dparts, dweight, -1, strips)
    darrived = exchange(dmixed, both)
    dright, dleft = across_columns(dends)
    dback = to_field(darrived, False, 1.0, tables, share)
    dback, dright, places, spec, dspec = hold((dback, dright, places, spec, dspec))
    dfield = exchange(dback, "gx").reshape(whole)
    dside = place_columns(dright, dleft, places)
    back_local = conv(dmatrix, dmain, dside, jnp.zeros_like(bias), width_x)
    slots = M1 // owners
    weight_grad = weight_grads(by_mode(spec, slots), by_mode(dspec, slots))
    dfield, back_local, weight_grad = hold((dfield, back_local, weight_grad))
    field_grad = stream(add_field, back_local, [dfield], F32, "add_field")
    return (activation[None], field_grad[None], weight_grad)


def solution(mesh):
    return jax.shard_map(
        body,
        mesh=mesh,
        in_specs=(
            P("dp", None, "gx", "gy"),
            P(None, None, None, ("gx", "gy"), None),
            P(),
            P(),
            P("dp", None, "gx", "gy"),
        ),
        out_specs=(
            P("dp", None, "gx", "gy"),
            P("dp", None, "gx", "gy"),
            P("dp", None, None, ("gx", "gy"), None),
        ),
        check_vma=False,
    )
```

```python
import functools
import math

import jax
import jax.numpy as jnp
import numpy as np
from jax import lax
from jax.experimental import pallas as pl
from jax.experimental.pallas import tpu as pltpu
from jax.sharding import PartitionSpec as P

M1 = 128
M2 = 128
BF = jnp.bfloat16
F32 = jnp.float32


def dot(left, right):
    return jnp.dot(left, right, preferred_element_type=F32)


@functools.lru_cache(maxsize=None)
def x_table(length, owners):
    slots = M1 // owners
    order = np.arange(M1).reshape(owners, slots).T.reshape(-1)
    modes = np.where(order < M1 // 2, order, order + length - M1)
    angle = (modes[:, None] * np.arange(length)[None, :] % length) * (2.0 * math.pi / length)
    table = np.concatenate([np.cos(angle), -np.sin(angle)], axis=0)
    return table.astype(np.float32).astype(jnp.bfloat16)


@functools.lru_cache(maxsize=None)
def y_table(length, width):
    angle = (np.arange(width)[:, None] * np.arange(M2)[None, :] % length) * (2.0 * math.pi / length)
    cosine, sine = np.cos(angle), np.sin(angle)
    table = np.concatenate(
        [np.concatenate([cosine, -sine], axis=1), np.concatenate([sine, cosine], axis=1)], axis=0
    )
    return table.astype(np.float32).astype(jnp.bfloat16)


def turn(values, quarter, sign):
    half = values.shape[1] // 2
    lane = lax.broadcasted_iota(jnp.int32, (1, 2 * half), 1)
    second = lane >= half
    q = jnp.where(second, lane - half, lane)
    step = lax.rem(q * quarter, 4)
    one = jnp.where(step == 0, 1.0, jnp.where(step == 2, -1.0, 0.0))
    imag = jnp.where(step == 1, 1.0, jnp.where(step == 3, -1.0, 0.0)) * sign
    swap = jnp.concatenate([values[:, half:], values[:, :half]], axis=1)
    return values * one + swap * jnp.where(second, imag, -imag)


def column_weight(half):
    lane = lax.broadcasted_iota(jnp.int32, (1, 2 * half), 1)
    return jnp.where((lane == 0) | (lane == half), 1.0, 2.0)


def resident(value):
    return pltpu.with_memory_space_constraint(value, pltpu.VMEM)


def on_chip(kernel, outs, scratch, name, *values, place=pltpu.VMEM):
    spec = pl.BlockSpec(memory_space=pltpu.VMEM)
    many = isinstance(outs, list)
    return pl.pallas_call(
        kernel,
        in_specs=[spec] * len(values),
        out_specs=[spec] * len(outs) if many else spec,
        out_shape=[place(*out) for out in outs] if many else place(*outs),
        scratch_shapes=scratch,
        compiler_params=pltpu.CompilerParams(vmem_limit_bytes=24 << 20),
        name=name,
    )(*[resident(value) for value in values])


def forward_kernel(weighted, factor, block_ref, table_ref, out_ref, rows_ref):
    length = block_ref.shape[0] * block_ref.shape[2]
    owners, rows, _ = out_ref.shape
    _, channels, _, width = block_ref.shape
    slots = M1 // owners
    for channel in range(channels):
        block = block_ref[:, channel].reshape(-1, width)
        spec_x = dot(table_ref[:, :length], block)
        if factor != 1.0:
            spec_x = spec_x * factor
        spec_x = spec_x.astype(BF)
        spec = dot(spec_x[:M1], table_ref[:, length : length + 2 * M2])
        spec = spec + dot(spec_x[M1:], table_ref[:, length + 2 * M2 :])
        spec = turn(spec, lax.axis_index("gy"), -1.0)
        if weighted:
            spec = spec * column_weight(M2)
        for slot in range(slots):
            for part in range(2):
                rows_ref[(channel * slots + slot) * 2 + part] = spec[
                    slot * owners : (slot + 1) * owners, part * M2 : (part + 1) * M2
                ]
    out_ref[...] = jnp.transpose(rows_ref[...], (1, 0, 2)).astype(BF)


def to_modes(block, weighted, factor, tables, owners):
    rows = block.shape[1] * (M1 // owners) * 2
    return on_chip(
        functools.partial(forward_kernel, weighted, factor),
        ((owners, rows, M2), BF),
        [pltpu.VMEM((rows, owners, M2), F32)],
        "to_modes",
        block,
        tables[0],
        place=jax.ShapeDtypeStruct,
    )


def inverse_kernel(weighted, factor, spec_ref, table_ref, out_ref, rows_ref):
    owners = spec_ref.shape[0]
    strips, channels, rows, width = out_ref.shape
    length = strips * rows
    slots = M1 // owners
    rows_ref[...] = jnp.transpose(spec_ref[...].astype(F32), (1, 0, 2))
    for channel in range(channels):
        spec = jnp.concatenate(
            [
                jnp.concatenate(
                    [rows_ref[(channel * slots + slot) * 2 + part] for part in range(2)], axis=1
                )
                for slot in range(slots)
            ],
            axis=0,
        )
        spec = turn(spec, lax.axis_index("gy"), 1.0)
        if weighted:
            spec = spec * column_weight(M2)
        spec = spec.astype(BF)
        over_y = [
            lax.dot_general(
                spec, table_ref[first : first + width], (((1,), (1,)), ((), ())), preferred_element_type=F32
            ).astype(BF)
            for first in (length, length + width)
        ]
        total = dot(table_ref[:length], jnp.concatenate(over_y, axis=0))
        if factor != 1.0:
            total = total * factor
        out_ref[:, channel] = total.astype(BF).reshape(strips, rows, width)


def to_field(spec, weighted, factor, tables, shape):
    owners, rows, _ = spec.shape
    return on_chip(
        functools.partial(inverse_kernel, weighted, factor),
        (shape, BF),
        [pltpu.VMEM((rows, owners, M2), F32)],
        "to_field",
        spec,
        tables[1],
    )


def mix_kernel(sign, parts_ref, weight_ref, out_ref, spec_ref, sum_ref, mixed_ref, place_ref):
    strips, rows, kept = spec_ref.shape
    pieces = parts_ref.shape[0] // strips
    slots, _, ins, outs, _ = weight_ref.shape
    share = ins // strips
    total = jnp.sum(parts_ref[...].reshape(strips, pieces, rows, kept).astype(F32), axis=1).astype(BF)
    spec_ref[...] = total
    sum_ref[...] = total.astype(F32)
    for slot in range(slots):
        real = jnp.zeros((outs, kept), F32)
        imag = jnp.zeros((outs, kept), F32)
        for channel in range(ins):
            strip, row = channel // share, (channel % share * slots + slot) * 2
            real_s = sum_ref[strip, row : row + 1, :]
            imag_s = sum_ref[strip, row + 1 : row + 2, :]
            real_w = weight_ref[slot, 0, channel].astype(F32)
            imag_w = weight_ref[slot, 1, channel].astype(F32)
            if sign > 0:
                real = real + (real_s * real_w - imag_s * imag_w)
                imag = imag + (real_s * imag_w + imag_s * real_w)
            else:
                real = real + (real_s * real_w + imag_s * imag_w)
                imag = imag + (imag_s * real_w - real_s * imag_w)
        mixed_ref[slot * 2] = real
        mixed_ref[slot * 2 + 1] = imag
    share = outs // strips
    for channel in range(share):
        for row in range(2 * slots):
            place_ref[:, channel * 2 * slots + row, :] = mixed_ref[
                row, pl.ds(channel, strips, stride=share), :
            ]
    placed = place_ref[...].astype(BF)
    out_ref[...] = jnp.broadcast_to(placed[:, None], (strips, pieces, rows, kept)).reshape(
        strips * pieces, rows, kept
    )


def mix(parts, weight, sign, strips):
    owners, rows, kept = parts.shape
    slots, _, _, outs, _ = weight.shape
    return on_chip(
        functools.partial(mix_kernel, sign),
        [((owners, rows, kept), BF), ((strips, rows, kept), BF)],
        [
            pltpu.VMEM((strips, rows, kept), F32),
            pltpu.VMEM((2 * slots, outs, kept), F32),
            pltpu.VMEM((strips, rows, kept), F32),
        ],
        "mix",
        parts,
        weight,
    )


def by_mode(rows, slots):
    strips, count, kept = rows.shape
    split = rows.reshape(strips, count // slots // 2, slots, 2, kept)
    return jnp.transpose(split, (2, 3, 0, 1, 4)).reshape(slots, 2, -1, kept)


CONV_ROWS = 4


def conv_matrix(weight):
    outs, ins = weight.shape[1:]
    band = jnp.transpose(weight.reshape(3, 3, outs, ins), (1, 2, 0, 3)).reshape(3 * outs, 3 * ins)
    return jnp.concatenate(
        [
            jnp.pad(band, ((0, 0), (row * ins, (CONV_ROWS - 1 - row) * ins)))
            for row in range(CONV_ROWS)
        ],
        axis=0,
    )


def conv_kernel(matrix_ref, main_ref, side_ref, out_ref):
    ins = matrix_ref.shape[1] // (CONV_ROWS + 2)
    outs, rows, width = out_ref.shape
    window = (CONV_ROWS + 2) * ins
    tall = 2 * CONV_ROWS

    @pl.loop(0, rows // tall)
    def _(step):
        pieces = []
        for part in range(tall // CONV_ROWS):
            start = pl.multiple_of((step * tall + part * CONV_ROWS) * ins, ins)
            main = dot(matrix_ref[...], main_ref[pl.ds(start, window), :])
            side = dot(matrix_ref[...], side_ref[pl.ds(start, window), :])
            taps = jnp.concatenate([main, side], axis=1)
            full = taps.shape[1]
            for row in range(CONV_ROWS):
                base = row * 3 * outs
                low = pltpu.roll(taps[base : base + outs], 1, 1)[:, :width]
                mid = taps[base + outs : base + 2 * outs, :width]
                high = pltpu.roll(taps[base + 2 * outs : base + 3 * outs], full - 1, 1)[:, :width]
                pieces.append(low + mid + high)
        first = pl.multiple_of(step * tall, tall)
        out_ref[:, pl.ds(first, tall), :] = jnp.transpose(jnp.stack(pieces, axis=0), (1, 0, 2))


def conv(matrix, main, side, rows):
    outs = matrix.shape[0] // (3 * CONV_ROWS)
    return on_chip(
        conv_kernel, ((outs, rows, main.shape[1]), F32), [], "conv", matrix, main, side
    )


def swap(value, axis, back=False):
    count = lax.axis_size(axis)
    pairs = [(i, i + 1) for i in range(count - 1)]
    if back:
        pairs = [(b, a) for a, b in pairs]
    return lax.ppermute(value, axis, pairs)


def across_rows(field):
    return swap(field[:, -1], "gx"), swap(field[:, 0], "gx", back=True)


def stack_rows(field, above, below):
    channels, rows, width = field.shape
    main = jnp.concatenate([above[None], jnp.transpose(field, (1, 0, 2)), below[None]], axis=0)
    main = main.reshape((rows + 2) * channels, width)
    pick = np.zeros((2, width), np.float32)
    pick[0, 0] = pick[1, width - 1] = 1.0
    ends = jnp.einsum("ry,ny->rn", pick.astype(BF), main, preferred_element_type=F32).astype(BF)
    return main, ends


def across_columns(ends):
    return swap(ends[:1], "gy", back=True), swap(ends[1:], "gy")


def side_slots():
    place = np.zeros((2, 128), np.float32)
    place[0, 0] = place[1, 127] = 1.0
    return place.astype(BF)


def place_columns(right, left, slots):
    return jnp.einsum(
        "rn,rk->nk", jnp.concatenate([right, left]), slots, preferred_element_type=F32
    ).astype(BF)


def exchange(value, axes):
    return lax.all_to_all(value, axes, split_axis=0, concat_axis=0, tiled=True)


def pdot(form, left, right):
    return jnp.einsum(form, left, right, preferred_element_type=F32)


def weight_grads(spec, dmixed):
    real_s, imag_s = (spec[:, 0], spec[:, 1])
    real_d, imag_d = (dmixed[:, 0], dmixed[:, 1])
    form_w = "mcq,mdq->cdmq"
    grad_real = pdot(form_w, real_s, real_d) + pdot(form_w, imag_s, imag_d)
    grad_imag = pdot(form_w, real_s, imag_d) - pdot(form_w, imag_s, real_d)
    return jnp.stack([grad_real, grad_imag], axis=2)


def body(field_in, spectral_weight, conv_weight, conv_bias, upstream):
    strips, pieces = lax.axis_size("gx"), lax.axis_size("gy")
    owners = strips * pieces
    _, channels, width_x, width_y = field_in.shape
    length_x, length_y = width_x * strips, width_y * pieces
    scale = 1.0 / (length_x * length_y)
    both = ("gx", "gy")
    share = (strips, channels // strips, width_x, width_y)
    whole = (channels, width_x, width_y)

    table_x, table_y = x_table(length_x, owners), y_table(length_y, width_y)
    hold = lax.optimization_barrier
    tables = [
        jnp.asarray(np.concatenate([table_x, table_y[:width_y], table_y[width_y:]], axis=1)),
        jnp.asarray(np.concatenate([table_x.T, table_y], axis=0)),
    ]

    field = field_in[0]
    block = exchange(field.reshape(share), "gx")
    above, below = across_rows(field)
    main, ends = stack_rows(field, above, below)
    weight = jnp.transpose(spectral_weight, (3, 2, 0, 1, 4))
    block, ends, weight = hold((block, ends, weight))
    parts = to_modes(block, False, 1.0, tables, owners)
    parts, ends, taps = hold((parts, ends, conv_weight))
    parts = exchange(parts, both)
    right, left = across_columns(ends)
    matrix = conv_matrix(taps)
    parts, right, left, matrix, places = hold((parts, right, left, matrix, side_slots()))
    mixed, spec = mix(parts, weight, 1, strips)
    arrived = exchange(mixed, both)
    local = conv(matrix, main, place_columns(right, left, places), width_x)
    arrived, local = hold((arrived, local))
    back = to_field(arrived, True, scale, tables, share)
    spectral = exchange(back, "gx").reshape(whole)

    pre = spectral.astype(F32) + local + conv_bias[:, None, None]
    gate = jax.nn.sigmoid(pre)
    activation = pre * gate
    dpre = (upstream[0].astype(F32) * gate * (1.0 + pre * (1.0 - gate))).astype(BF)

    dblock = exchange(dpre.reshape(share), "gx")
    dabove, dbelow = across_rows(dpre)
    dparts = to_modes(dblock, True, scale, tables, owners)
    dparts, dhere, dabove, dbelow, taps, dweight = hold(
        (dparts, dpre, dabove, dbelow, taps, spectral_weight)
    )
    dparts = exchange(dparts, both)
    dmatrix = conv_matrix(jnp.transpose(taps[::-1], (0, 2, 1)))
    dweight = jnp.transpose(dweight, (3, 2, 1, 0, 4))
    dmain, dends = stack_rows(dhere, dabove, dbelow)
    dparts, dends, dmain, dmatrix, dweight = hold((dparts, dends, dmain, dmatrix, dweight))
    dmixed, dspec = mix(dparts, dweight, -1, strips)
    darrived = exchange(dmixed, both)
    dright, dleft = across_columns(dends)
    dback = to_field(darrived, False, 1.0, tables, share)
    dback, dright, dleft, places, spec, dspec = hold((dback, dright, dleft, places, spec, dspec))
    dfield = exchange(dback, "gx").reshape(whole)
    back_local = conv(dmatrix, dmain, place_columns(dright, dleft, places), width_x)
    slots = M1 // owners
    weight_grad = weight_grads(by_mode(spec, slots), by_mode(dspec, slots))
    dfield, back_local, weight_grad = hold((dfield, back_local, weight_grad))
    field_grad = dfield.astype(F32) + back_local
    return (activation[None], field_grad[None], weight_grad)


def solution(mesh):
    return jax.shard_map(
        body,
        mesh=mesh,
        in_specs=(
            P("dp", None, "gx", "gy"),
            P(None, None, None, ("gx", "gy"), None),
            P(),
            P(),
            P("dp", None, "gx", "gy"),
        ),
        out_specs=(
            P("dp", None, "gx", "gy"),
            P("dp", None, "gx", "gy"),
            P("dp", None, None, ("gx", "gy"), None),
        ),
        check_vma=False,
    )
```

```python
import functools
import math

import jax
import jax.numpy as jnp
import numpy as np
from jax import lax
from jax.experimental import pallas as pl
from jax.experimental.pallas import tpu as pltpu
from jax.sharding import PartitionSpec as P

M1 = 128
M2 = 128
BF = jnp.bfloat16
F32 = jnp.float32


def dot(left, right):
    return jnp.dot(left, right, preferred_element_type=F32)


@functools.lru_cache(maxsize=None)
def x_table(length, owners):
    slots = M1 // owners
    order = np.arange(M1).reshape(owners, slots).T.reshape(-1)
    modes = np.where(order < M1 // 2, order, order + length - M1)
    angle = (modes[:, None] * np.arange(length)[None, :] % length) * (2.0 * math.pi / length)
    table = np.concatenate([np.cos(angle), -np.sin(angle)], axis=0)
    return table.astype(np.float32).astype(jnp.bfloat16)


@functools.lru_cache(maxsize=None)
def y_table(length, width):
    angle = (np.arange(width)[:, None] * np.arange(M2)[None, :] % length) * (2.0 * math.pi / length)
    cosine, sine = np.cos(angle), np.sin(angle)
    table = np.concatenate(
        [np.concatenate([cosine, -sine], axis=1), np.concatenate([sine, cosine], axis=1)], axis=0
    )
    return table.astype(np.float32).astype(jnp.bfloat16)


def turn(values, quarter, sign):
    half = values.shape[1] // 2
    lane = lax.broadcasted_iota(jnp.int32, (1, 2 * half), 1)
    second = lane >= half
    q = jnp.where(second, lane - half, lane)
    step = lax.rem(q * quarter, 4)
    one = jnp.where(step == 0, 1.0, jnp.where(step == 2, -1.0, 0.0))
    imag = jnp.where(step == 1, 1.0, jnp.where(step == 3, -1.0, 0.0)) * sign
    swap = jnp.concatenate([values[:, half:], values[:, :half]], axis=1)
    return values * one + swap * jnp.where(second, imag, -imag)


def column_weight(half):
    lane = lax.broadcasted_iota(jnp.int32, (1, 2 * half), 1)
    return jnp.where((lane == 0) | (lane == half), 1.0, 2.0)


def resident(value):
    return pltpu.with_memory_space_constraint(value, pltpu.VMEM)


def on_chip(kernel, outs, scratch, name, *values, place=pltpu.VMEM, apart=()):
    spec = pl.BlockSpec(memory_space=pltpu.VMEM)
    many = isinstance(outs, list)
    return pl.pallas_call(
        kernel,
        in_specs=[spec] * len(values),
        out_specs=[spec] * len(outs) if many else spec,
        out_shape=[place(*out) for out in outs] if many else place(*outs),
        scratch_shapes=scratch,
        compiler_params=pltpu.CompilerParams(vmem_limit_bytes=24 << 20),
        name=name,
    )(*[value if index in apart else resident(value) for index, value in enumerate(values)])


def forward_kernel(weighted, factor, block_ref, table_ref, out_ref, rows_ref):
    length = block_ref.shape[0] * block_ref.shape[2]
    owners, rows, _ = out_ref.shape
    _, channels, _, width = block_ref.shape
    slots = M1 // owners
    for channel in range(channels):
        block = block_ref[:, channel].reshape(-1, width)
        spec_x = dot(table_ref[:, :length], block)
        if factor != 1.0:
            spec_x = spec_x * factor
        spec_x = spec_x.astype(BF)
        spec = dot(spec_x[:M1], table_ref[:, length : length + 2 * M2])
        spec = spec + dot(spec_x[M1:], table_ref[:, length + 2 * M2 :])
        spec = turn(spec, lax.axis_index("gy"), -1.0)
        if weighted:
            spec = spec * column_weight(M2)
        for slot in range(slots):
            for part in range(2):
                rows_ref[(channel * slots + slot) * 2 + part] = spec[
                    slot * owners : (slot + 1) * owners, part * M2 : (part + 1) * M2
                ]
    out_ref[...] = jnp.transpose(rows_ref[...], (1, 0, 2)).astype(BF)


def to_modes(block, weighted, factor, tables, owners):
    rows = block.shape[1] * (M1 // owners) * 2
    return on_chip(
        functools.partial(forward_kernel, weighted, factor),
        ((owners, rows, M2), BF),
        [pltpu.VMEM((rows, owners, M2), F32)],
        "to_modes",
        block,
        tables[0],
        place=jax.ShapeDtypeStruct,
    )


def inverse_kernel(weighted, factor, spec_ref, table_ref, out_ref, rows_ref):
    owners = spec_ref.shape[0]
    strips, channels, rows, width = out_ref.shape
    length = strips * rows
    slots = M1 // owners
    rows_ref[...] = jnp.transpose(spec_ref[...].astype(F32), (1, 0, 2))
    for channel in range(channels):
        spec = jnp.concatenate(
            [
                jnp.concatenate(
                    [rows_ref[(channel * slots + slot) * 2 + part] for part in range(2)], axis=1
                )
                for slot in range(slots)
            ],
            axis=0,
        )
        spec = turn(spec, lax.axis_index("gy"), 1.0)
        if weighted:
            spec = spec * column_weight(M2)
        spec = spec.astype(BF)
        over_y = [
            lax.dot_general(
                spec, table_ref[first : first + width], (((1,), (1,)), ((), ())), preferred_element_type=F32
            ).astype(BF)
            for first in (length, length + width)
        ]
        total = dot(table_ref[:length], jnp.concatenate(over_y, axis=0))
        if factor != 1.0:
            total = total * factor
        out_ref[:, channel] = total.astype(BF).reshape(strips, rows, width)


def to_field(spec, weighted, factor, tables, shape):
    owners, rows, _ = spec.shape
    return on_chip(
        functools.partial(inverse_kernel, weighted, factor),
        (shape, BF),
        [pltpu.VMEM((rows, owners, M2), F32)],
        "to_field",
        spec,
        tables[1],
    )


def mix_kernel(sign, parts_ref, weight_ref, out_ref, spec_ref, sum_ref, mixed_ref, place_ref):
    strips, rows, kept = spec_ref.shape
    pieces = parts_ref.shape[0] // strips
    slots, _, ins, outs, _ = weight_ref.shape
    share = ins // strips
    total = jnp.sum(parts_ref[...].reshape(strips, pieces, rows, kept).astype(F32), axis=1).astype(BF)
    spec_ref[...] = total
    sum_ref[...] = total.astype(F32)
    for slot in range(slots):
        real = jnp.zeros((outs, kept), F32)
        imag = jnp.zeros((outs, kept), F32)
        for channel in range(ins):
            strip, row = channel // share, (channel % share * slots + slot) * 2
            real_s = sum_ref[strip, row : row + 1, :]
            imag_s = sum_ref[strip, row + 1 : row + 2, :]
            real_w = weight_ref[slot, 0, channel].astype(F32)
            imag_w = weight_ref[slot, 1, channel].astype(F32)
            if sign > 0:
                real = real + (real_s * real_w - imag_s * imag_w)
                imag = imag + (real_s * imag_w + imag_s * real_w)
            else:
                real = real + (real_s * real_w + imag_s * imag_w)
                imag = imag + (imag_s * real_w - real_s * imag_w)
        mixed_ref[slot * 2] = real
        mixed_ref[slot * 2 + 1] = imag
    share = outs // strips
    for channel in range(share):
        for row in range(2 * slots):
            place_ref[:, channel * 2 * slots + row, :] = mixed_ref[
                row, pl.ds(channel, strips, stride=share), :
            ]
    placed = place_ref[...].astype(BF)
    out_ref[...] = jnp.broadcast_to(placed[:, None], (strips, pieces, rows, kept)).reshape(
        strips * pieces, rows, kept
    )


def mix(parts, weight, sign, strips):
    owners, rows, kept = parts.shape
    slots, _, _, outs, _ = weight.shape
    return on_chip(
        functools.partial(mix_kernel, sign),
        [((owners, rows, kept), BF), ((strips, rows, kept), BF)],
        [
            pltpu.VMEM((strips, rows, kept), F32),
            pltpu.VMEM((2 * slots, outs, kept), F32),
            pltpu.VMEM((strips, rows, kept), F32),
        ],
        "mix",
        parts,
        weight,
    )


def by_mode(rows, slots):
    strips, count, kept = rows.shape
    split = rows.reshape(strips, count // slots // 2, slots, 2, kept)
    return jnp.transpose(split, (2, 3, 0, 1, 4)).reshape(slots, 2, -1, kept)


CHUNK = 4


def gate_kernel(local_ref, field_ref, up_ref, grad_out, act_out, grad_ref, act_ref, sems):
    copies = []
    for place, first in enumerate(range(0, local_ref.shape[0], CHUNK)):
        piece = pl.ds(first, CHUNK)
        pre = field_ref[piece].astype(F32) + local_ref[piece]
        gate = 0.5 + 0.5 * jnp.tanh(0.5 * pre)
        grad_ref[piece] = (up_ref[piece].astype(F32) * gate * (1.0 + pre * (1.0 - gate))).astype(BF)
        act_ref[piece] = pre * gate
        for index, (ref, out) in enumerate(((grad_ref, grad_out), (act_ref, act_out))):
            copies.append(pltpu.make_async_copy(ref.at[piece], out.at[piece], sems.at[index, place]))
            copies[-1].start()
    for copy in copies:
        copy.wait()


def gate_both(local, field, upstream):
    shape = local.shape
    vmem, hbm = pl.BlockSpec(memory_space=pltpu.VMEM), pl.BlockSpec(memory_space=pltpu.HBM)
    return pl.pallas_call(
        gate_kernel,
        in_specs=[vmem] * 3,
        out_specs=[hbm] * 2,
        out_shape=[jax.ShapeDtypeStruct(shape, BF), jax.ShapeDtypeStruct(shape, F32)],
        scratch_shapes=[
            pltpu.VMEM(shape, BF),
            pltpu.VMEM(shape, F32),
            pltpu.SemaphoreType.DMA((2, shape[0] // CHUNK)),
        ],
        compiler_params=pltpu.CompilerParams(vmem_limit_bytes=24 << 20),
        name="gate_both",
    )(resident(local), resident(field), resident(upstream))


def add_kernel(local_ref, field_hbm, out, field_ref, out_ref, in_sems, out_sems):
    pieces = [pl.ds(first, CHUNK) for first in range(0, local_ref.shape[0], CHUNK)]
    loads = [
        pltpu.make_async_copy(field_hbm.at[piece], field_ref.at[piece], in_sems.at[place])
        for place, piece in enumerate(pieces)
    ]
    stores = [
        pltpu.make_async_copy(out_ref.at[piece], out.at[piece], out_sems.at[place])
        for place, piece in enumerate(pieces)
    ]
    for load in loads:
        load.start()
    for piece, load, store in zip(pieces, loads, stores):
        load.wait()
        out_ref[piece] = field_ref[piece].astype(F32) + local_ref[piece]
        store.start()
    for store in stores:
        store.wait()


def add_field(local, field):
    shape = local.shape
    vmem, hbm = pl.BlockSpec(memory_space=pltpu.VMEM), pl.BlockSpec(memory_space=pltpu.HBM)
    return pl.pallas_call(
        add_kernel,
        in_specs=[vmem, hbm],
        out_specs=hbm,
        out_shape=jax.ShapeDtypeStruct(shape, F32),
        scratch_shapes=[
            pltpu.VMEM(shape, BF),
            pltpu.VMEM(shape, F32),
            pltpu.SemaphoreType.DMA((shape[0] // CHUNK,)),
            pltpu.SemaphoreType.DMA((shape[0] // CHUNK,)),
        ],
        compiler_params=pltpu.CompilerParams(vmem_limit_bytes=24 << 20),
        name="add_field",
    )(resident(local), pltpu.with_memory_space_constraint(field, pltpu.HBM))


CONV_ROWS = 4


def conv_matrix(weight):
    outs, ins = weight.shape[1:]
    band = jnp.transpose(weight.reshape(3, 3, outs, ins), (1, 2, 0, 3)).reshape(3 * outs, 3 * ins)
    return jnp.concatenate(
        [
            jnp.pad(band, ((0, 0), (row * ins, (CONV_ROWS - 1 - row) * ins)))
            for row in range(CONV_ROWS)
        ],
        axis=0,
    )


def conv_kernel(matrix_ref, main_ref, side_ref, bias_ref, out_ref):
    ins = matrix_ref.shape[1] // (CONV_ROWS + 2)
    outs, rows, width = out_ref.shape
    window = (CONV_ROWS + 2) * ins
    tall = 2 * CONV_ROWS

    @pl.loop(0, rows // tall)
    def _(step):
        pieces = []
        for part in range(tall // CONV_ROWS):
            start = pl.multiple_of((step * tall + part * CONV_ROWS) * ins, ins)
            main = dot(matrix_ref[...], main_ref[pl.ds(start, window), :])
            side = dot(matrix_ref[...], side_ref[pl.ds(start, window), :])
            taps = jnp.concatenate([main, side], axis=1)
            full = taps.shape[1]
            for row in range(CONV_ROWS):
                base = row * 3 * outs
                low = pltpu.roll(taps[base : base + outs], 1, 1)[:, :width]
                mid = taps[base + outs : base + 2 * outs, :width]
                high = pltpu.roll(taps[base + 2 * outs : base + 3 * outs], full - 1, 1)[:, :width]
                pieces.append(low + mid + high + bias_ref[:, :1])
        first = pl.multiple_of(step * tall, tall)
        out_ref[:, pl.ds(first, tall), :] = jnp.transpose(jnp.stack(pieces, axis=0), (1, 0, 2))


def conv(matrix, main, side, bias, rows):
    outs = matrix.shape[0] // (3 * CONV_ROWS)
    return on_chip(
        conv_kernel,
        ((outs, rows, main.shape[1]), F32),
        [],
        "conv",
        matrix,
        pltpu.with_memory_space_constraint(main, pltpu.HBM),
        side,
        bias,
        apart=(1,),
    )


def swap(value, axis, back=False):
    count = lax.axis_size(axis)
    pairs = [(i, i + 1) for i in range(count - 1)]
    if back:
        pairs = [(b, a) for a, b in pairs]
    return lax.ppermute(value, axis, pairs)


def across_rows(field):
    return swap(field[:, -1], "gx"), swap(field[:, 0], "gx", back=True)


def stack_rows(field, above, below):
    channels, rows, width = field.shape
    main = jnp.concatenate([above[None], jnp.transpose(field, (1, 0, 2)), below[None]], axis=0)
    main = main.reshape((rows + 2) * channels, width)
    pick = np.zeros((2, width), np.float32)
    pick[0, 0] = pick[1, width - 1] = 1.0
    ends = jnp.einsum("ry,ny->rn", pick.astype(BF), main, preferred_element_type=F32).astype(BF)
    return main, ends


def across_columns(ends):
    return swap(ends[:1], "gy", back=True), swap(ends[1:], "gy")


def side_slots():
    place = np.zeros((2, 128), np.float32)
    place[0, 0] = place[1, 127] = 1.0
    return place.astype(BF)


def place_columns(right, left, slots):
    return jnp.einsum(
        "rn,rk->nk", jnp.concatenate([right, left]), slots, preferred_element_type=F32
    ).astype(BF)


def exchange(value, axes):
    return lax.all_to_all(value, axes, split_axis=0, concat_axis=0, tiled=True)


def pdot(form, left, right):
    return jnp.einsum(form, left, right, preferred_element_type=F32)


def weight_grads(spec, dmixed):
    real_s, imag_s = (spec[:, 0], spec[:, 1])
    real_d, imag_d = (dmixed[:, 0], dmixed[:, 1])
    form_w = "mcq,mdq->cdmq"
    grad_real = pdot(form_w, real_s, real_d) + pdot(form_w, imag_s, imag_d)
    grad_imag = pdot(form_w, real_s, imag_d) - pdot(form_w, imag_s, real_d)
    return jnp.stack([grad_real, grad_imag], axis=2)


def body(field_in, spectral_weight, conv_weight, conv_bias, upstream):
    strips, pieces = lax.axis_size("gx"), lax.axis_size("gy")
    owners = strips * pieces
    _, channels, width_x, width_y = field_in.shape
    length_x, length_y = width_x * strips, width_y * pieces
    scale = 1.0 / (length_x * length_y)
    both = ("gx", "gy")
    share = (strips, channels // strips, width_x, width_y)
    whole = (channels, width_x, width_y)

    table_x, table_y = x_table(length_x, owners), y_table(length_y, width_y)
    hold = lax.optimization_barrier
    tables = [
        jnp.asarray(np.concatenate([table_x, table_y[:width_y], table_y[width_y:]], axis=1)),
        jnp.asarray(np.concatenate([table_x.T, table_y], axis=0)),
    ]

    field = field_in[0]
    bias = jnp.broadcast_to(conv_bias[:, None], (channels, 128))
    block = exchange(field.reshape(share), "gx")
    above, below = across_rows(field)
    main, ends = stack_rows(field, above, below)
    weight = jnp.transpose(spectral_weight, (3, 2, 0, 1, 4))
    block, ends, weight = hold((block, ends, weight))
    parts = to_modes(block, False, 1.0, tables, owners)
    parts, ends, taps = hold((parts, ends, conv_weight))
    parts = exchange(parts, both)
    right, left = across_columns(ends)
    matrix = conv_matrix(taps)
    parts, matrix, places = hold((parts, matrix, side_slots()))
    mixed, spec = mix(parts, weight, 1, strips)
    mixed, right, left = hold((mixed, right, left))
    arrived = exchange(mixed, both)
    local = conv(matrix, main, place_columns(right, left, places), bias, width_x)
    arrived, local = hold((arrived, local))
    back = to_field(arrived, True, scale, tables, share)
    spectral = exchange(back, "gx").reshape(whole)

    dpre, activation = gate_both(local, spectral, upstream[0])

    dblock = exchange(dpre.reshape(share), "gx")
    dabove, dbelow = across_rows(dpre)
    dparts = to_modes(dblock, True, scale, tables, owners)
    dparts, dhere, dabove, dbelow, taps, dweight = hold(
        (dparts, dpre, dabove, dbelow, taps, spectral_weight)
    )
    dparts = exchange(dparts, both)
    dmatrix = conv_matrix(jnp.transpose(taps[::-1], (0, 2, 1)))
    dweight = jnp.transpose(dweight, (3, 2, 1, 0, 4))
    dmain, dends = stack_rows(dhere, dabove, dbelow)
    dparts, dends, dmain, dmatrix, dweight = hold((dparts, dends, dmain, dmatrix, dweight))
    dmixed, dspec = mix(dparts, dweight, -1, strips)
    darrived = exchange(dmixed, both)
    dright, dleft = across_columns(dends)
    dback = to_field(darrived, False, 1.0, tables, share)
    dback, dright, dleft, places, spec, dspec = hold((dback, dright, dleft, places, spec, dspec))
    dfield = exchange(dback, "gx").reshape(whole)
    back_local = conv(dmatrix, dmain, place_columns(dright, dleft, places), jnp.zeros_like(bias), width_x)
    slots = M1 // owners
    weight_grad = weight_grads(by_mode(spec, slots), by_mode(dspec, slots))
    dfield, back_local, weight_grad = hold((dfield, back_local, weight_grad))
    field_grad = add_field(back_local, dfield)
    return (activation[None], field_grad[None], weight_grad)


def solution(mesh):
    return jax.shard_map(
        body,
        mesh=mesh,
        in_specs=(
            P("dp", None, "gx", "gy"),
            P(None, None, None, ("gx", "gy"), None),
            P(),
            P(),
            P("dp", None, "gx", "gy"),
        ),
        out_specs=(
            P("dp", None, "gx", "gy"),
            P("dp", None, "gx", "gy"),
            P("dp", None, None, ("gx", "gy"), None),
        ),
        check_vma=False,
    )
```

```python
import functools
import math

import jax
import jax.numpy as jnp
import numpy as np
from jax import lax
from jax.experimental import pallas as pl
from jax.experimental.pallas import tpu as pltpu
from jax.sharding import PartitionSpec as P

M1 = 128
M2 = 128
BF = jnp.bfloat16
F32 = jnp.float32


def dot(left, right):
    return jnp.dot(left, right, preferred_element_type=F32)


@functools.lru_cache(maxsize=None)
def x_table(length, owners):
    slots = M1 // owners
    order = np.arange(M1).reshape(owners, slots).T.reshape(-1)
    modes = np.where(order < M1 // 2, order, order + length - M1)
    angle = (modes[:, None] * np.arange(length)[None, :] % length) * (2.0 * math.pi / length)
    table = np.concatenate([np.cos(angle), -np.sin(angle)], axis=0)
    return table.astype(np.float32).astype(jnp.bfloat16)


@functools.lru_cache(maxsize=None)
def y_table(length, width):
    angle = (np.arange(width)[:, None] * np.arange(M2)[None, :] % length) * (2.0 * math.pi / length)
    cosine, sine = np.cos(angle), np.sin(angle)
    table = np.concatenate(
        [np.concatenate([cosine, -sine], axis=1), np.concatenate([sine, cosine], axis=1)], axis=0
    )
    return table.astype(np.float32).astype(jnp.bfloat16)


def turn(values, quarter, sign):
    half = values.shape[1] // 2
    lane = lax.broadcasted_iota(jnp.int32, (1, 2 * half), 1)
    second = lane >= half
    q = jnp.where(second, lane - half, lane)
    step = lax.rem(q * quarter, 4)
    one = jnp.where(step == 0, 1.0, jnp.where(step == 2, -1.0, 0.0))
    imag = jnp.where(step == 1, 1.0, jnp.where(step == 3, -1.0, 0.0)) * sign
    swap = jnp.concatenate([values[:, half:], values[:, :half]], axis=1)
    return values * one + swap * jnp.where(second, imag, -imag)


def column_weight(half):
    lane = lax.broadcasted_iota(jnp.int32, (1, 2 * half), 1)
    return jnp.where((lane == 0) | (lane == half), 1.0, 2.0)


def resident(value):
    return pltpu.with_memory_space_constraint(value, pltpu.VMEM)


def on_chip(kernel, outs, scratch, name, *values, place=pltpu.VMEM, apart=()):
    spec = pl.BlockSpec(memory_space=pltpu.VMEM)
    many = isinstance(outs, list)
    return pl.pallas_call(
        kernel,
        in_specs=[spec] * len(values),
        out_specs=[spec] * len(outs) if many else spec,
        out_shape=[place(*out) for out in outs] if many else place(*outs),
        scratch_shapes=scratch,
        compiler_params=pltpu.CompilerParams(vmem_limit_bytes=24 << 20),
        name=name,
    )(*[value if index in apart else resident(value) for index, value in enumerate(values)])


def forward_kernel(weighted, factor, block_ref, table_ref, out_ref, rows_ref):
    length = block_ref.shape[0] * block_ref.shape[2]
    owners, rows, _ = out_ref.shape
    _, channels, _, width = block_ref.shape
    slots = M1 // owners
    for channel in range(channels):
        block = block_ref[:, channel].reshape(-1, width)
        spec_x = dot(table_ref[:, :length], block)
        if factor != 1.0:
            spec_x = spec_x * factor
        spec_x = spec_x.astype(BF)
        spec = dot(spec_x[:M1], table_ref[:, length : length + 2 * M2])
        spec = spec + dot(spec_x[M1:], table_ref[:, length + 2 * M2 :])
        spec = turn(spec, lax.axis_index("gy"), -1.0)
        if weighted:
            spec = spec * column_weight(M2)
        for slot in range(slots):
            for part in range(2):
                rows_ref[(channel * slots + slot) * 2 + part] = spec[
                    slot * owners : (slot + 1) * owners, part * M2 : (part + 1) * M2
                ]
    out_ref[...] = jnp.transpose(rows_ref[...], (1, 0, 2)).astype(BF)


def to_modes(block, weighted, factor, tables, owners):
    rows = block.shape[1] * (M1 // owners) * 2
    return on_chip(
        functools.partial(forward_kernel, weighted, factor),
        ((owners, rows, M2), BF),
        [pltpu.VMEM((rows, owners, M2), F32)],
        "to_modes",
        block,
        tables[0],
        place=jax.ShapeDtypeStruct,
    )


def inverse_kernel(weighted, factor, spec_ref, table_ref, out_ref, rows_ref):
    owners = spec_ref.shape[0]
    strips, channels, rows, width = out_ref.shape
    length = strips * rows
    slots = M1 // owners
    rows_ref[...] = jnp.transpose(spec_ref[...].astype(F32), (1, 0, 2))
    for channel in range(channels):
        spec = jnp.concatenate(
            [
                jnp.concatenate(
                    [rows_ref[(channel * slots + slot) * 2 + part] for part in range(2)], axis=1
                )
                for slot in range(slots)
            ],
            axis=0,
        )
        spec = turn(spec, lax.axis_index("gy"), 1.0)
        if weighted:
            spec = spec * column_weight(M2)
        spec = spec.astype(BF)
        over_y = [
            lax.dot_general(
                spec, table_ref[first : first + width], (((1,), (1,)), ((), ())), preferred_element_type=F32
            ).astype(BF)
            for first in (length, length + width)
        ]
        total = dot(table_ref[:length], jnp.concatenate(over_y, axis=0))
        if factor != 1.0:
            total = total * factor
        out_ref[:, channel] = total.astype(BF).reshape(strips, rows, width)


def to_field(spec, weighted, factor, tables, shape):
    owners, rows, _ = spec.shape
    return on_chip(
        functools.partial(inverse_kernel, weighted, factor),
        (shape, BF),
        [pltpu.VMEM((rows, owners, M2), F32)],
        "to_field",
        spec,
        tables[1],
    )


def mix_kernel(sign, parts_ref, weight_ref, out_ref, spec_ref, sum_ref, mixed_ref, place_ref):
    strips, rows, kept = spec_ref.shape
    pieces = parts_ref.shape[0] // strips
    slots, _, ins, outs, _ = weight_ref.shape
    share = ins // strips
    total = jnp.sum(parts_ref[...].reshape(strips, pieces, rows, kept).astype(F32), axis=1).astype(BF)
    spec_ref[...] = total
    sum_ref[...] = total.astype(F32)
    for slot in range(slots):
        real = jnp.zeros((outs, kept), F32)
        imag = jnp.zeros((outs, kept), F32)
        for channel in range(ins):
            strip, row = channel // share, (channel % share * slots + slot) * 2
            real_s = sum_ref[strip, row : row + 1, :]
            imag_s = sum_ref[strip, row + 1 : row + 2, :]
            real_w = weight_ref[slot, 0, channel].astype(F32)
            imag_w = weight_ref[slot, 1, channel].astype(F32)
            if sign > 0:
                real = real + (real_s * real_w - imag_s * imag_w)
                imag = imag + (real_s * imag_w + imag_s * real_w)
            else:
                real = real + (real_s * real_w + imag_s * imag_w)
                imag = imag + (imag_s * real_w - real_s * imag_w)
        mixed_ref[slot * 2] = real
        mixed_ref[slot * 2 + 1] = imag
    share = outs // strips
    for channel in range(share):
        for row in range(2 * slots):
            place_ref[:, channel * 2 * slots + row, :] = mixed_ref[
                row, pl.ds(channel, strips, stride=share), :
            ]
    placed = place_ref[...].astype(BF)
    out_ref[...] = jnp.broadcast_to(placed[:, None], (strips, pieces, rows, kept)).reshape(
        strips * pieces, rows, kept
    )


def mix(parts, weight, sign, strips):
    owners, rows, kept = parts.shape
    slots, _, _, outs, _ = weight.shape
    return on_chip(
        functools.partial(mix_kernel, sign),
        [((owners, rows, kept), BF), ((strips, rows, kept), BF)],
        [
            pltpu.VMEM((strips, rows, kept), F32),
            pltpu.VMEM((2 * slots, outs, kept), F32),
            pltpu.VMEM((strips, rows, kept), F32),
        ],
        "mix",
        parts,
        weight,
    )


def by_mode(rows, slots):
    strips, count, kept = rows.shape
    split = rows.reshape(strips, count // slots // 2, slots, 2, kept)
    return jnp.transpose(split, (2, 3, 0, 1, 4)).reshape(slots, 2, -1, kept)


CHUNK = 4


def gate_kernel(local_ref, field_ref, up_ref, grad_out, act_out, grad_ref, act_ref, sems):
    copies = []
    for place, first in enumerate(range(0, local_ref.shape[0], CHUNK)):
        piece = pl.ds(first, CHUNK)
        pre = field_ref[piece].astype(F32) + local_ref[piece]
        gate = 0.5 + 0.5 * jnp.tanh(0.5 * pre)
        grad_ref[piece] = (up_ref[piece].astype(F32) * gate * (1.0 + pre * (1.0 - gate))).astype(BF)
        act_ref[piece] = pre * gate
        for index, (ref, out) in enumerate(((grad_ref, grad_out), (act_ref, act_out))):
            copies.append(pltpu.make_async_copy(ref.at[piece], out.at[piece], sems.at[index, place]))
            copies[-1].start()
    for copy in copies:
        copy.wait()


def gate_both(local, field, upstream):
    shape = local.shape
    vmem, hbm = pl.BlockSpec(memory_space=pltpu.VMEM), pl.BlockSpec(memory_space=pltpu.HBM)
    return pl.pallas_call(
        gate_kernel,
        in_specs=[vmem] * 3,
        out_specs=[hbm] * 2,
        out_shape=[jax.ShapeDtypeStruct(shape, BF), jax.ShapeDtypeStruct(shape, F32)],
        scratch_shapes=[
            pltpu.VMEM(shape, BF),
            pltpu.VMEM(shape, F32),
            pltpu.SemaphoreType.DMA((2, shape[0] // CHUNK)),
        ],
        compiler_params=pltpu.CompilerParams(vmem_limit_bytes=24 << 20),
        name="gate_both",
    )(resident(local), resident(field), resident(upstream))


def add_kernel(local_ref, field_ref, out, out_ref, sems):
    copies = []
    for place, first in enumerate(range(0, local_ref.shape[0], CHUNK)):
        piece = pl.ds(first, CHUNK)
        out_ref[piece] = field_ref[piece].astype(F32) + local_ref[piece]
        copies.append(pltpu.make_async_copy(out_ref.at[piece], out.at[piece], sems.at[place]))
        copies[-1].start()
    for copy in copies:
        copy.wait()


def add_field(local, field):
    shape = local.shape
    vmem, hbm = pl.BlockSpec(memory_space=pltpu.VMEM), pl.BlockSpec(memory_space=pltpu.HBM)
    return pl.pallas_call(
        add_kernel,
        in_specs=[vmem, vmem],
        out_specs=hbm,
        out_shape=jax.ShapeDtypeStruct(shape, F32),
        scratch_shapes=[
            pltpu.VMEM(shape, F32),
            pltpu.SemaphoreType.DMA((shape[0] // CHUNK,)),
        ],
        compiler_params=pltpu.CompilerParams(vmem_limit_bytes=24 << 20),
        name="add_field",
    )(resident(local), resident(field))


CONV_ROWS = 4


def conv_matrix(weight):
    outs, ins = weight.shape[1:]
    band = jnp.transpose(weight.reshape(3, 3, outs, ins), (1, 2, 0, 3)).reshape(3 * outs, 3 * ins)
    return jnp.concatenate(
        [
            jnp.pad(band, ((0, 0), (row * ins, (CONV_ROWS - 1 - row) * ins)))
            for row in range(CONV_ROWS)
        ],
        axis=0,
    )


def conv_kernel(matrix_ref, main_ref, side_ref, bias_ref, out_ref):
    ins = matrix_ref.shape[1] // (CONV_ROWS + 2)
    outs, rows, width = out_ref.shape
    window = (CONV_ROWS + 2) * ins
    tall = 2 * CONV_ROWS

    @pl.loop(0, rows // tall)
    def _(step):
        pieces = []
        for part in range(tall // CONV_ROWS):
            start = pl.multiple_of((step * tall + part * CONV_ROWS) * ins, ins)
            main = dot(matrix_ref[...], main_ref[pl.ds(start, window), :])
            side = dot(matrix_ref[...], side_ref[pl.ds(start, window), :])
            taps = jnp.concatenate([main, side], axis=1)
            full = taps.shape[1]
            for row in range(CONV_ROWS):
                base = row * 3 * outs
                low = pltpu.roll(taps[base : base + outs], 1, 1)[:, :width]
                mid = taps[base + outs : base + 2 * outs, :width]
                high = pltpu.roll(taps[base + 2 * outs : base + 3 * outs], full - 1, 1)[:, :width]
                pieces.append(low + mid + high + bias_ref[:, :1])
        first = pl.multiple_of(step * tall, tall)
        out_ref[:, pl.ds(first, tall), :] = jnp.transpose(jnp.stack(pieces, axis=0), (1, 0, 2))


def conv(matrix, main, side, bias, rows):
    outs = matrix.shape[0] // (3 * CONV_ROWS)
    return on_chip(
        conv_kernel,
        ((outs, rows, main.shape[1]), F32),
        [],
        "conv",
        matrix,
        pltpu.with_memory_space_constraint(main, pltpu.HBM),
        side,
        bias,
        apart=(1,),
    )


def swap(value, axis, back=False):
    count = lax.axis_size(axis)
    pairs = [(i, i + 1) for i in range(count - 1)]
    if back:
        pairs = [(b, a) for a, b in pairs]
    return lax.ppermute(value, axis, pairs)


def across_rows(field):
    return swap(field[:, -1], "gx"), swap(field[:, 0], "gx", back=True)


def stack_rows(field, above, below):
    channels, rows, width = field.shape
    main = jnp.concatenate([above[None], jnp.transpose(field, (1, 0, 2)), below[None]], axis=0)
    main = main.reshape((rows + 2) * channels, width)
    pick = np.zeros((2, width), np.float32)
    pick[0, 0] = pick[1, width - 1] = 1.0
    ends = jnp.einsum("ry,ny->rn", pick.astype(BF), main, preferred_element_type=F32).astype(BF)
    return main, ends


def across_columns(ends):
    return swap(ends[:1], "gy", back=True), swap(ends[1:], "gy")


def side_slots():
    place = np.zeros((2, 128), np.float32)
    place[0, 0] = place[1, 127] = 1.0
    return place.astype(BF)


def place_columns(right, left, slots):
    return jnp.einsum(
        "rn,rk->nk", jnp.concatenate([right, left]), slots, preferred_element_type=F32
    ).astype(BF)


def exchange(value, axes):
    return lax.all_to_all(value, axes, split_axis=0, concat_axis=0, tiled=True)


def pdot(form, left, right):
    return jnp.einsum(form, left, right, preferred_element_type=F32)


def weight_grads(spec, dmixed):
    real_s, imag_s = (spec[:, 0], spec[:, 1])
    real_d, imag_d = (dmixed[:, 0], dmixed[:, 1])
    form_w = "mcq,mdq->cdmq"
    grad_real = pdot(form_w, real_s, real_d) + pdot(form_w, imag_s, imag_d)
    grad_imag = pdot(form_w, real_s, imag_d) - pdot(form_w, imag_s, real_d)
    return jnp.stack([grad_real, grad_imag], axis=2)


def body(field_in, spectral_weight, conv_weight, conv_bias, upstream):
    strips, pieces = lax.axis_size("gx"), lax.axis_size("gy")
    owners = strips * pieces
    _, channels, width_x, width_y = field_in.shape
    length_x, length_y = width_x * strips, width_y * pieces
    scale = 1.0 / (length_x * length_y)
    both = ("gx", "gy")
    share = (strips, channels // strips, width_x, width_y)
    whole = (channels, width_x, width_y)

    table_x, table_y = x_table(length_x, owners), y_table(length_y, width_y)
    hold = lax.optimization_barrier
    tables = [
        jnp.asarray(np.concatenate([table_x, table_y[:width_y], table_y[width_y:]], axis=1)),
        jnp.asarray(np.concatenate([table_x.T, table_y], axis=0)),
    ]

    field = field_in[0]
    bias = jnp.broadcast_to(conv_bias[:, None], (channels, 128))
    block = exchange(field.reshape(share), "gx")
    above, below = across_rows(field)
    main, ends = stack_rows(field, above, below)
    weight = jnp.transpose(spectral_weight, (3, 2, 0, 1, 4))
    matrix = conv_matrix(conv_weight)
    block, ends, weight, matrix = hold((block, ends, weight, matrix))
    parts = to_modes(block, False, 1.0, tables, owners)
    parts, ends, taps = hold((parts, ends, conv_weight))
    parts = exchange(parts, both)
    right, left = across_columns(ends)
    parts, places = hold((parts, side_slots()))
    mixed, spec = mix(parts, weight, 1, strips)
    mixed, right, left = hold((mixed, right, left))
    arrived = exchange(mixed, both)
    local = conv(matrix, main, place_columns(right, left, places), bias, width_x)
    arrived, local = hold((arrived, local))
    back = to_field(arrived, True, scale, tables, share)
    spectral = exchange(back, "gx").reshape(whole)

    dpre, activation = gate_both(local, spectral, upstream[0])

    dblock = exchange(dpre.reshape(share), "gx")
    dabove, dbelow = across_rows(dpre)
    dparts = to_modes(dblock, True, scale, tables, owners)
    dparts, dhere, dabove, dbelow, taps, dweight = hold(
        (dparts, dpre, dabove, dbelow, taps, spectral_weight)
    )
    dparts = exchange(dparts, both)
    dmatrix = conv_matrix(jnp.transpose(taps[::-1], (0, 2, 1)))
    dweight = jnp.transpose(dweight, (3, 2, 1, 0, 4))
    dmain, dends = stack_rows(dhere, dabove, dbelow)
    dparts, dends, dmain, dmatrix, dweight = hold((dparts, dends, dmain, dmatrix, dweight))
    dmixed, dspec = mix(dparts, dweight, -1, strips)
    darrived = exchange(dmixed, both)
    dright, dleft = across_columns(dends)
    dback = to_field(darrived, False, 1.0, tables, share)
    dback, dright, dleft, places, spec, dspec = hold((dback, dright, dleft, places, spec, dspec))
    dfield = exchange(dback, "gx").reshape(whole)
    back_local = conv(dmatrix, dmain, place_columns(dright, dleft, places), jnp.zeros_like(bias), width_x)
    slots = M1 // owners
    weight_grad = weight_grads(by_mode(spec, slots), by_mode(dspec, slots))
    dfield, back_local, weight_grad = hold((dfield, back_local, weight_grad))
    field_grad = add_field(back_local, dfield)
    return (activation[None], field_grad[None], weight_grad)


def solution(mesh):
    return jax.shard_map(
        body,
        mesh=mesh,
        in_specs=(
            P("dp", None, "gx", "gy"),
            P(None, None, None, ("gx", "gy"), None),
            P(),
            P(),
            P("dp", None, "gx", "gy"),
        ),
        out_specs=(
            P("dp", None, "gx", "gy"),
            P("dp", None, "gx", "gy"),
            P("dp", None, None, ("gx", "gy"), None),
        ),
        check_vma=False,
    )
```

```python
import functools
import math

import jax
import jax.numpy as jnp
import numpy as np
from jax import lax
from jax.experimental import pallas as pl
from jax.experimental.pallas import tpu as pltpu
from jax.sharding import PartitionSpec as P

M1 = 128
M2 = 128
BF = jnp.bfloat16
F32 = jnp.float32


def dot(left, right):
    return jnp.dot(left, right, preferred_element_type=F32)


@functools.lru_cache(maxsize=None)
def x_table(length, owners):
    slots = M1 // owners
    order = np.arange(M1).reshape(owners, slots).T.reshape(-1)
    modes = np.where(order < M1 // 2, order, order + length - M1)
    angle = (modes[:, None] * np.arange(length)[None, :] % length) * (2.0 * math.pi / length)
    table = np.concatenate([np.cos(angle), -np.sin(angle)], axis=0)
    return table.astype(np.float32).astype(jnp.bfloat16)


@functools.lru_cache(maxsize=None)
def y_table(length, width):
    angle = (np.arange(width)[:, None] * np.arange(M2)[None, :] % length) * (2.0 * math.pi / length)
    cosine, sine = np.cos(angle), np.sin(angle)
    table = np.concatenate(
        [np.concatenate([cosine, -sine], axis=1), np.concatenate([sine, cosine], axis=1)], axis=0
    )
    return table.astype(np.float32).astype(jnp.bfloat16)


def turn(values, quarter, sign):
    half = values.shape[1] // 2
    lane = lax.broadcasted_iota(jnp.int32, (1, 2 * half), 1)
    second = lane >= half
    q = jnp.where(second, lane - half, lane)
    step = lax.rem(q * quarter, 4)
    one = jnp.where(step == 0, 1.0, jnp.where(step == 2, -1.0, 0.0))
    imag = jnp.where(step == 1, 1.0, jnp.where(step == 3, -1.0, 0.0)) * sign
    swap = jnp.concatenate([values[:, half:], values[:, :half]], axis=1)
    return values * one + swap * jnp.where(second, imag, -imag)


def column_weight(half):
    lane = lax.broadcasted_iota(jnp.int32, (1, 2 * half), 1)
    return jnp.where((lane == 0) | (lane == half), 1.0, 2.0)


def resident(value):
    return pltpu.with_memory_space_constraint(value, pltpu.VMEM)


def on_chip(kernel, outs, scratch, name, *values, place=pltpu.VMEM, apart=()):
    spec = pl.BlockSpec(memory_space=pltpu.VMEM)
    many = isinstance(outs, list)
    return pl.pallas_call(
        kernel,
        in_specs=[spec] * len(values),
        out_specs=[spec] * len(outs) if many else spec,
        out_shape=[place(*out) for out in outs] if many else place(*outs),
        scratch_shapes=scratch,
        compiler_params=pltpu.CompilerParams(vmem_limit_bytes=24 << 20),
        name=name,
    )(*[value if index in apart else resident(value) for index, value in enumerate(values)])


def forward_kernel(weighted, factor, block_ref, table_ref, out_ref, rows_ref):
    length = block_ref.shape[0] * block_ref.shape[2]
    owners, rows, _ = out_ref.shape
    _, channels, _, width = block_ref.shape
    slots = M1 // owners
    for channel in range(channels):
        block = block_ref[:, channel].reshape(-1, width)
        spec_x = dot(table_ref[:, :length], block)
        if factor != 1.0:
            spec_x = spec_x * factor
        spec_x = spec_x.astype(BF)
        spec = dot(spec_x[:M1], table_ref[:, length : length + 2 * M2])
        spec = spec + dot(spec_x[M1:], table_ref[:, length + 2 * M2 :])
        spec = turn(spec, lax.axis_index("gy"), -1.0)
        if weighted:
            spec = spec * column_weight(M2)
        for slot in range(slots):
            for part in range(2):
                rows_ref[(channel * slots + slot) * 2 + part] = spec[
                    slot * owners : (slot + 1) * owners, part * M2 : (part + 1) * M2
                ]
    out_ref[...] = jnp.transpose(rows_ref[...], (1, 0, 2)).astype(BF)


def to_modes(block, weighted, factor, tables, owners):
    rows = block.shape[1] * (M1 // owners) * 2
    return on_chip(
        functools.partial(forward_kernel, weighted, factor),
        ((owners, rows, M2), BF),
        [pltpu.VMEM((rows, owners, M2), F32)],
        "to_modes",
        block,
        tables[0],
        place=jax.ShapeDtypeStruct,
    )


def inverse_kernel(weighted, factor, spec_ref, table_ref, out_ref, rows_ref):
    owners = spec_ref.shape[0]
    strips, channels, rows, width = out_ref.shape
    length = strips * rows
    slots = M1 // owners
    rows_ref[...] = jnp.transpose(spec_ref[...].astype(F32), (1, 0, 2))
    for channel in range(channels):
        spec = jnp.concatenate(
            [
                jnp.concatenate(
                    [rows_ref[(channel * slots + slot) * 2 + part] for part in range(2)], axis=1
                )
                for slot in range(slots)
            ],
            axis=0,
        )
        spec = turn(spec, lax.axis_index("gy"), 1.0)
        if weighted:
            spec = spec * column_weight(M2)
        spec = spec.astype(BF)
        over_y = [
            lax.dot_general(
                spec, table_ref[first : first + width], (((1,), (1,)), ((), ())), preferred_element_type=F32
            ).astype(BF)
            for first in (length, length + width)
        ]
        total = dot(table_ref[:length], jnp.concatenate(over_y, axis=0))
        if factor != 1.0:
            total = total * factor
        out_ref[:, channel] = total.astype(BF).reshape(strips, rows, width)


def to_field(spec, weighted, factor, tables, shape):
    owners, rows, _ = spec.shape
    return on_chip(
        functools.partial(inverse_kernel, weighted, factor),
        (shape, BF),
        [pltpu.VMEM((rows, owners, M2), F32)],
        "to_field",
        spec,
        tables[1],
    )


def mix_kernel(sign, parts_ref, weight_ref, out_ref, spec_ref, sum_ref, mixed_ref, place_ref):
    strips, rows, kept = spec_ref.shape
    pieces = parts_ref.shape[0] // strips
    slots, _, ins, outs, _ = weight_ref.shape
    share = ins // strips
    total = jnp.sum(parts_ref[...].reshape(strips, pieces, rows, kept).astype(F32), axis=1).astype(BF)
    spec_ref[...] = total
    sum_ref[...] = total.astype(F32)
    for slot in range(slots):
        real = jnp.zeros((outs, kept), F32)
        imag = jnp.zeros((outs, kept), F32)
        for channel in range(ins):
            strip, row = channel // share, (channel % share * slots + slot) * 2
            real_s = sum_ref[strip, row : row + 1, :]
            imag_s = sum_ref[strip, row + 1 : row + 2, :]
            real_w = weight_ref[slot, 0, channel].astype(F32)
            imag_w = weight_ref[slot, 1, channel].astype(F32)
            if sign > 0:
                real = real + (real_s * real_w - imag_s * imag_w)
                imag = imag + (real_s * imag_w + imag_s * real_w)
            else:
                real = real + (real_s * real_w + imag_s * imag_w)
                imag = imag + (imag_s * real_w - real_s * imag_w)
        mixed_ref[slot * 2] = real
        mixed_ref[slot * 2 + 1] = imag
    share = outs // strips
    for channel in range(share):
        for row in range(2 * slots):
            place_ref[:, channel * 2 * slots + row, :] = mixed_ref[
                row, pl.ds(channel, strips, stride=share), :
            ]
    placed = place_ref[...].astype(BF)
    out_ref[...] = jnp.broadcast_to(placed[:, None], (strips, pieces, rows, kept)).reshape(
        strips * pieces, rows, kept
    )


def mix(parts, weight, sign, strips):
    owners, rows, kept = parts.shape
    slots, _, _, outs, _ = weight.shape
    return on_chip(
        functools.partial(mix_kernel, sign),
        [((owners, rows, kept), BF), ((strips, rows, kept), BF)],
        [
            pltpu.VMEM((strips, rows, kept), F32),
            pltpu.VMEM((2 * slots, outs, kept), F32),
            pltpu.VMEM((strips, rows, kept), F32),
        ],
        "mix",
        parts,
        weight,
    )


def by_mode(rows, slots):
    strips, count, kept = rows.shape
    split = rows.reshape(strips, count // slots // 2, slots, 2, kept)
    return jnp.transpose(split, (2, 3, 0, 1, 4)).reshape(slots, 2, -1, kept)


CHUNK = 4


def gate_kernel(local_ref, field_ref, up_ref, grad_out, act_out, grad_ref, act_ref, sems):
    copies = []
    for place, first in enumerate(range(0, local_ref.shape[0], CHUNK)):
        piece = pl.ds(first, CHUNK)
        pre = field_ref[piece].astype(F32) + local_ref[piece]
        gate = 0.5 + 0.5 * jnp.tanh(0.5 * pre)
        grad_ref[piece] = (up_ref[piece].astype(F32) * gate * (1.0 + pre * (1.0 - gate))).astype(BF)
        act_ref[piece] = pre * gate
        for index, (ref, out) in enumerate(((grad_ref, grad_out), (act_ref, act_out))):
            copies.append(pltpu.make_async_copy(ref.at[piece], out.at[piece], sems.at[index, place]))
            copies[-1].start()
    for copy in copies:
        copy.wait()


def gate_both(local, field, upstream):
    shape = local.shape
    vmem, hbm = pl.BlockSpec(memory_space=pltpu.VMEM), pl.BlockSpec(memory_space=pltpu.HBM)
    return pl.pallas_call(
        gate_kernel,
        in_specs=[vmem] * 3,
        out_specs=[hbm] * 2,
        out_shape=[jax.ShapeDtypeStruct(shape, BF), jax.ShapeDtypeStruct(shape, F32)],
        scratch_shapes=[
            pltpu.VMEM(shape, BF),
            pltpu.VMEM(shape, F32),
            pltpu.SemaphoreType.DMA((2, shape[0] // CHUNK)),
        ],
        compiler_params=pltpu.CompilerParams(vmem_limit_bytes=24 << 20),
        name="gate_both",
    )(resident(local), resident(field), resident(upstream))


def add_kernel(local_ref, field_ref, out, out_ref, sems):
    copies = []
    for place, first in enumerate(range(0, local_ref.shape[0], CHUNK)):
        piece = pl.ds(first, CHUNK)
        out_ref[piece] = field_ref[piece].astype(F32) + local_ref[piece]
        copies.append(pltpu.make_async_copy(out_ref.at[piece], out.at[piece], sems.at[place]))
        copies[-1].start()
    for copy in copies:
        copy.wait()


def add_field(local, field):
    shape = local.shape
    vmem, hbm = pl.BlockSpec(memory_space=pltpu.VMEM), pl.BlockSpec(memory_space=pltpu.HBM)
    return pl.pallas_call(
        add_kernel,
        in_specs=[vmem, vmem],
        out_specs=hbm,
        out_shape=jax.ShapeDtypeStruct(shape, F32),
        scratch_shapes=[
            pltpu.VMEM(shape, F32),
            pltpu.SemaphoreType.DMA((shape[0] // CHUNK,)),
        ],
        compiler_params=pltpu.CompilerParams(vmem_limit_bytes=24 << 20),
        name="add_field",
    )(resident(local), resident(field))


CONV_ROWS = 4


def conv_matrix(weight):
    outs, ins = weight.shape[1:]
    band = jnp.transpose(weight.reshape(3, 3, outs, ins), (1, 2, 0, 3)).reshape(3 * outs, 3 * ins)
    return jnp.concatenate(
        [
            jnp.pad(band, ((0, 0), (row * ins, (CONV_ROWS - 1 - row) * ins)))
            for row in range(CONV_ROWS)
        ],
        axis=0,
    )


def conv_kernel(
    matrix_ref, main_hbm, side_hbm, above_ref, below_ref, bias_ref, out_ref, all_ref, sems
):
    ins = matrix_ref.shape[1] // (CONV_ROWS + 2)
    outs, rows, width = out_ref.shape
    full = all_ref.shape[1]
    window = (CONV_ROWS + 2) * ins
    tall = 2 * CONV_ROWS
    inner = pl.ds(ins, rows * ins)
    copies = [
        pltpu.make_async_copy(main_hbm, all_ref.at[inner, pl.ds(0, width)], sems.at[0]),
        pltpu.make_async_copy(side_hbm, all_ref.at[inner, pl.ds(width, full - width)], sems.at[1]),
    ]
    for copy in copies:
        copy.start()
    all_ref[:ins, :] = above_ref[...]
    all_ref[(rows + 1) * ins :, :] = below_ref[...]
    for copy in copies:
        copy.wait()

    @pl.loop(0, rows // tall)
    def _(step):
        pieces = []
        for part in range(tall // CONV_ROWS):
            start = pl.multiple_of((step * tall + part * CONV_ROWS) * ins, ins)
            taps = dot(matrix_ref[...], all_ref[pl.ds(start, window), :])
            for row in range(CONV_ROWS):
                base = row * 3 * outs
                low = pltpu.roll(taps[base : base + outs], 1, 1)[:, :width]
                mid = taps[base + outs : base + 2 * outs, :width]
                high = pltpu.roll(taps[base + 2 * outs : base + 3 * outs], full - 1, 1)[:, :width]
                pieces.append(low + mid + high + bias_ref[:, :1])
        first = pl.multiple_of(step * tall, tall)
        out_ref[:, pl.ds(first, tall), :] = jnp.transpose(jnp.stack(pieces, axis=0), (1, 0, 2))


def conv(matrix, main, side, above, below, bias):
    outs = matrix.shape[0] // (3 * CONV_ROWS)
    ins = above.shape[0]
    rows, width = main.shape[0] // ins, main.shape[1]
    vmem, hbm = pl.BlockSpec(memory_space=pltpu.VMEM), pl.BlockSpec(memory_space=pltpu.HBM)
    return pl.pallas_call(
        conv_kernel,
        in_specs=[vmem, hbm, hbm, vmem, vmem, vmem],
        out_specs=vmem,
        out_shape=pltpu.VMEM((outs, rows, width), F32),
        scratch_shapes=[
            pltpu.VMEM(((rows + 2) * ins, above.shape[1]), BF),
            pltpu.SemaphoreType.DMA((2,)),
        ],
        compiler_params=pltpu.CompilerParams(vmem_limit_bytes=24 << 20),
        name="conv",
    )(
        resident(matrix),
        pltpu.with_memory_space_constraint(main, pltpu.HBM),
        pltpu.with_memory_space_constraint(side, pltpu.HBM),
        resident(above),
        resident(below),
        resident(bias),
    )


def swap(value, axis, back=False):
    count = lax.axis_size(axis)
    pairs = [(i, i + 1) for i in range(count - 1)]
    if back:
        pairs = [(b, a) for a, b in pairs]
    return lax.ppermute(value, axis, pairs)


def by_rows(field):
    channels, rows, width = field.shape
    main = jnp.transpose(field, (1, 0, 2)).reshape(rows * channels, width)
    pick = np.zeros((2, width), np.float32)
    pick[0, 0] = pick[1, width - 1] = 1.0
    ends = jnp.einsum("ry,ny->rn", pick.astype(BF), main, preferred_element_type=F32).astype(BF)
    return main, ends


def edge_rows(main, side, channels):
    return (
        jnp.concatenate([main[:channels], side[:channels]], axis=1),
        jnp.concatenate([main[-channels:], side[-channels:]], axis=1),
    )


def across_rows(first, last):
    return swap(last, "gx"), swap(first, "gx", back=True)


def across_columns(ends):
    return swap(ends[:1], "gy", back=True), swap(ends[1:], "gy")


def side_slots():
    place = np.zeros((2, 128), np.float32)
    place[0, 0] = place[1, 127] = 1.0
    return place.astype(BF)


def place_columns(right, left, slots):
    return jnp.einsum(
        "rn,rk->nk", jnp.concatenate([right, left]), slots, preferred_element_type=F32
    ).astype(BF)


def exchange(value, axes):
    return lax.all_to_all(value, axes, split_axis=0, concat_axis=0, tiled=True)


def pdot(form, left, right):
    return jnp.einsum(form, left, right, preferred_element_type=F32)


def weight_grads(spec, dmixed):
    real_s, imag_s = (spec[:, 0], spec[:, 1])
    real_d, imag_d = (dmixed[:, 0], dmixed[:, 1])
    form_w = "mcq,mdq->cdmq"
    grad_real = pdot(form_w, real_s, real_d) + pdot(form_w, imag_s, imag_d)
    grad_imag = pdot(form_w, real_s, imag_d) - pdot(form_w, imag_s, real_d)
    return jnp.stack([grad_real, grad_imag], axis=2)


def body(field_in, spectral_weight, conv_weight, conv_bias, upstream):
    strips, pieces = lax.axis_size("gx"), lax.axis_size("gy")
    owners = strips * pieces
    _, channels, width_x, width_y = field_in.shape
    length_x, length_y = width_x * strips, width_y * pieces
    scale = 1.0 / (length_x * length_y)
    both = ("gx", "gy")
    share = (strips, channels // strips, width_x, width_y)
    whole = (channels, width_x, width_y)

    table_x, table_y = x_table(length_x, owners), y_table(length_y, width_y)
    hold = lax.optimization_barrier
    tables = [
        jnp.asarray(np.concatenate([table_x, table_y[:width_y], table_y[width_y:]], axis=1)),
        jnp.asarray(np.concatenate([table_x.T, table_y], axis=0)),
    ]

    field = field_in[0]
    bias = jnp.broadcast_to(conv_bias[:, None], (channels, 128))
    block = exchange(field.reshape(share), "gx")
    main, ends = by_rows(field)
    right, left = across_columns(ends)
    weight = jnp.transpose(spectral_weight, (3, 2, 0, 1, 4))
    matrix = conv_matrix(conv_weight)
    side = place_columns(right, left, side_slots())
    first, last = edge_rows(main, side, channels)
    block, first, last, weight, matrix = hold((block, first, last, weight, matrix))
    parts = to_modes(block, False, 1.0, tables, owners)
    parts, first, last = hold((parts, first, last))
    parts = exchange(parts, both)
    above, below = across_rows(first, last)
    mixed, spec = mix(parts, weight, 1, strips)
    mixed, above, below = hold((mixed, above, below))
    arrived = exchange(mixed, both)
    local = conv(matrix, main, side, above, below, bias)
    arrived, local = hold((arrived, local))
    back = to_field(arrived, True, scale, tables, share)
    spectral = exchange(back, "gx").reshape(whole)

    dpre, activation = gate_both(local, spectral, upstream[0])
    dpre, taps, dweight = hold((dpre, conv_weight, spectral_weight))

    dblock = exchange(dpre.reshape(share), "gx")
    dmain, dends = by_rows(dpre)
    dright, dleft = across_columns(dends)
    dmatrix = conv_matrix(jnp.transpose(taps[::-1], (0, 2, 1)))
    dblock, dmatrix, dmain = hold((dblock, dmatrix, dmain))
    dparts = to_modes(dblock, True, scale, tables, owners)
    dparts, dright, dleft, dweight, places = hold((dparts, dright, dleft, dweight, side_slots()))
    dparts = exchange(dparts, both)
    dweight = jnp.transpose(dweight, (3, 2, 1, 0, 4))
    dside = place_columns(dright, dleft, places)
    dabove, dbelow = across_rows(*edge_rows(dmain, dside, channels))
    dparts, dweight = hold((dparts, dweight))
    dmixed, dspec = mix(dparts, dweight, -1, strips)
    dmixed, dabove, dbelow = hold((dmixed, dabove, dbelow))
    darrived = exchange(dmixed, both)
    back_local = conv(dmatrix, dmain, dside, dabove, dbelow, jnp.zeros_like(bias))
    slots = M1 // owners
    weight_grad = weight_grads(by_mode(spec, slots), by_mode(dspec, slots))
    darrived, back_local, weight_grad = hold((darrived, back_local, weight_grad))
    dback = to_field(darrived, False, 1.0, tables, share)
    dfield = exchange(dback, "gx").reshape(whole)
    field_grad = add_field(back_local, dfield)
    return (activation[None], field_grad[None], weight_grad)


def solution(mesh):
    return jax.shard_map(
        body,
        mesh=mesh,
        in_specs=(
            P("dp", None, "gx", "gy"),
            P(None, None, None, ("gx", "gy"), None),
            P(),
            P(),
            P("dp", None, "gx", "gy"),
        ),
        out_specs=(
            P("dp", None, "gx", "gy"),
            P("dp", None, "gx", "gy"),
            P("dp", None, None, ("gx", "gy"), None),
        ),
        check_vma=False,
    )
```

```python
import functools
import math

import jax
import jax.numpy as jnp
import numpy as np
from jax import lax
from jax.experimental import pallas as pl
from jax.experimental.pallas import tpu as pltpu
from jax.sharding import PartitionSpec as P

M1 = 128
M2 = 128
BF = jnp.bfloat16
F32 = jnp.float32


def dot(left, right):
    return jnp.dot(left, right, preferred_element_type=F32)


@functools.lru_cache(maxsize=None)
def x_table(length, owners):
    slots = M1 // owners
    order = np.arange(M1).reshape(owners, slots).T.reshape(-1)
    modes = np.where(order < M1 // 2, order, order + length - M1)
    angle = (modes[:, None] * np.arange(length)[None, :] % length) * (2.0 * math.pi / length)
    table = np.concatenate([np.cos(angle), -np.sin(angle)], axis=0)
    return table.astype(np.float32).astype(jnp.bfloat16)


@functools.lru_cache(maxsize=None)
def y_table(length, width):
    angle = (np.arange(width)[:, None] * np.arange(M2)[None, :] % length) * (2.0 * math.pi / length)
    cosine, sine = np.cos(angle), np.sin(angle)
    table = np.concatenate(
        [np.concatenate([cosine, -sine], axis=1), np.concatenate([sine, cosine], axis=1)], axis=0
    )
    return table.astype(np.float32).astype(jnp.bfloat16)


def turn(values, quarter, sign):
    half = values.shape[1] // 2
    lane = lax.broadcasted_iota(jnp.int32, (1, 2 * half), 1)
    second = lane >= half
    q = jnp.where(second, lane - half, lane)
    step = lax.rem(q * quarter, 4)
    one = jnp.where(step == 0, 1.0, jnp.where(step == 2, -1.0, 0.0))
    imag = jnp.where(step == 1, 1.0, jnp.where(step == 3, -1.0, 0.0)) * sign
    swap = jnp.concatenate([values[:, half:], values[:, :half]], axis=1)
    return values * one + swap * jnp.where(second, imag, -imag)


def column_weight(half):
    lane = lax.broadcasted_iota(jnp.int32, (1, 2 * half), 1)
    return jnp.where((lane == 0) | (lane == half), 1.0, 2.0)


def resident(value):
    return pltpu.with_memory_space_constraint(value, pltpu.VMEM)


def on_chip(kernel, outs, scratch, name, *values, place=pltpu.VMEM, apart=()):
    spec = pl.BlockSpec(memory_space=pltpu.VMEM)
    many = isinstance(outs, list)
    return pl.pallas_call(
        kernel,
        in_specs=[spec] * len(values),
        out_specs=[spec] * len(outs) if many else spec,
        out_shape=[place(*out) for out in outs] if many else place(*outs),
        scratch_shapes=scratch,
        compiler_params=pltpu.CompilerParams(vmem_limit_bytes=24 << 20),
        name=name,
    )(*[value if index in apart else resident(value) for index, value in enumerate(values)])


def forward_kernel(weighted, factor, block_ref, table_ref, out_ref, rows_ref):
    length = block_ref.shape[0] * block_ref.shape[2]
    owners, rows, _ = out_ref.shape
    _, channels, _, width = block_ref.shape
    slots = M1 // owners
    for channel in range(channels):
        block = block_ref[:, channel].reshape(-1, width)
        spec_x = dot(table_ref[:, :length], block)
        if factor != 1.0:
            spec_x = spec_x * factor
        spec_x = spec_x.astype(BF)
        spec = dot(spec_x[:M1], table_ref[:, length : length + 2 * M2])
        spec = spec + dot(spec_x[M1:], table_ref[:, length + 2 * M2 :])
        spec = turn(spec, lax.axis_index("gy"), -1.0)
        if weighted:
            spec = spec * column_weight(M2)
        for slot in range(slots):
            for part in range(2):
                rows_ref[(channel * slots + slot) * 2 + part] = spec[
                    slot * owners : (slot + 1) * owners, part * M2 : (part + 1) * M2
                ]
    out_ref[...] = jnp.transpose(rows_ref[...], (1, 0, 2)).astype(BF)


def to_modes(block, weighted, factor, tables, owners):
    rows = block.shape[1] * (M1 // owners) * 2
    return on_chip(
        functools.partial(forward_kernel, weighted, factor),
        ((owners, rows, M2), BF),
        [pltpu.VMEM((rows, owners, M2), F32)],
        "to_modes",
        block,
        tables[0],
        place=jax.ShapeDtypeStruct,
    )


def inverse_kernel(weighted, factor, spec_ref, table_ref, out_ref, rows_ref):
    owners = spec_ref.shape[0]
    strips, channels, rows, width = out_ref.shape
    length = strips * rows
    slots = M1 // owners
    rows_ref[...] = jnp.transpose(spec_ref[...].astype(F32), (1, 0, 2))
    for channel in range(channels):
        spec = jnp.concatenate(
            [
                jnp.concatenate(
                    [rows_ref[(channel * slots + slot) * 2 + part] for part in range(2)], axis=1
                )
                for slot in range(slots)
            ],
            axis=0,
        )
        spec = turn(spec, lax.axis_index("gy"), 1.0)
        if weighted:
            spec = spec * column_weight(M2)
        spec = spec.astype(BF)
        over_y = [
            lax.dot_general(
                spec, table_ref[first : first + width], (((1,), (1,)), ((), ())), preferred_element_type=F32
            ).astype(BF)
            for first in (length, length + width)
        ]
        total = dot(table_ref[:length], jnp.concatenate(over_y, axis=0))
        if factor != 1.0:
            total = total * factor
        out_ref[:, channel] = total.astype(BF).reshape(strips, rows, width)


def to_field(spec, weighted, factor, tables, shape):
    owners, rows, _ = spec.shape
    return on_chip(
        functools.partial(inverse_kernel, weighted, factor),
        (shape, BF),
        [pltpu.VMEM((rows, owners, M2), F32)],
        "to_field",
        spec,
        tables[1],
    )


def mix_kernel(sign, parts_ref, weight_ref, out_ref, spec_ref, sum_ref, mixed_ref, place_ref):
    strips, rows, kept = spec_ref.shape
    pieces = parts_ref.shape[0] // strips
    slots, _, ins, outs, _ = weight_ref.shape
    share = ins // strips
    total = jnp.sum(parts_ref[...].reshape(strips, pieces, rows, kept).astype(F32), axis=1).astype(BF)
    spec_ref[...] = total
    sum_ref[...] = total.astype(F32)
    for slot in range(slots):
        real = jnp.zeros((outs, kept), F32)
        imag = jnp.zeros((outs, kept), F32)
        for channel in range(ins):
            strip, row = channel // share, (channel % share * slots + slot) * 2
            real_s = sum_ref[strip, row : row + 1, :]
            imag_s = sum_ref[strip, row + 1 : row + 2, :]
            real_w = weight_ref[slot, 0, channel].astype(F32)
            imag_w = weight_ref[slot, 1, channel].astype(F32)
            if sign > 0:
                real = real + (real_s * real_w - imag_s * imag_w)
                imag = imag + (real_s * imag_w + imag_s * real_w)
            else:
                real = real + (real_s * real_w + imag_s * imag_w)
                imag = imag + (imag_s * real_w - real_s * imag_w)
        mixed_ref[slot * 2] = real
        mixed_ref[slot * 2 + 1] = imag
    share = outs // strips
    for channel in range(share):
        for row in range(2 * slots):
            place_ref[:, channel * 2 * slots + row, :] = mixed_ref[
                row, pl.ds(channel, strips, stride=share), :
            ]
    placed = place_ref[...].astype(BF)
    out_ref[...] = jnp.broadcast_to(placed[:, None], (strips, pieces, rows, kept)).reshape(
        strips * pieces, rows, kept
    )


def mix(parts, weight, sign, strips):
    owners, rows, kept = parts.shape
    slots, _, _, outs, _ = weight.shape
    return on_chip(
        functools.partial(mix_kernel, sign),
        [((owners, rows, kept), BF), ((strips, rows, kept), BF)],
        [
            pltpu.VMEM((strips, rows, kept), F32),
            pltpu.VMEM((2 * slots, outs, kept), F32),
            pltpu.VMEM((strips, rows, kept), F32),
        ],
        "mix",
        parts,
        weight,
    )


def by_mode(rows, slots):
    strips, count, kept = rows.shape
    split = rows.reshape(strips, count // slots // 2, slots, 2, kept)
    return jnp.transpose(split, (2, 3, 0, 1, 4)).reshape(slots, 2, -1, kept)


CHUNK = 4


def gate_kernel(local_ref, field_ref, up_ref, grad_out, act_out, grad_ref, act_ref, sems):
    copies = []
    for place, first in enumerate(range(0, local_ref.shape[0], CHUNK)):
        piece = pl.ds(first, CHUNK)
        pre = field_ref[piece].astype(F32) + local_ref[piece]
        gate = 0.5 + 0.5 * jnp.tanh(0.5 * pre)
        grad_ref[piece] = (up_ref[piece].astype(F32) * gate * (1.0 + pre * (1.0 - gate))).astype(BF)
        act_ref[piece] = pre * gate
        for index, (ref, out) in enumerate(((grad_ref, grad_out), (act_ref, act_out))):
            copies.append(pltpu.make_async_copy(ref.at[piece], out.at[piece], sems.at[index, place]))
            copies[-1].start()
    for copy in copies:
        copy.wait()


def gate_both(local, field, upstream):
    shape = local.shape
    vmem, hbm = pl.BlockSpec(memory_space=pltpu.VMEM), pl.BlockSpec(memory_space=pltpu.HBM)
    return pl.pallas_call(
        gate_kernel,
        in_specs=[vmem] * 3,
        out_specs=[hbm] * 2,
        out_shape=[jax.ShapeDtypeStruct(shape, BF), jax.ShapeDtypeStruct(shape, F32)],
        scratch_shapes=[
            pltpu.VMEM(shape, BF),
            pltpu.VMEM(shape, F32),
            pltpu.SemaphoreType.DMA((2, shape[0] // CHUNK)),
        ],
        compiler_params=pltpu.CompilerParams(vmem_limit_bytes=24 << 20),
        name="gate_both",
    )(resident(local), resident(field), resident(upstream))


def add_kernel(local_ref, field_ref, out, out_ref, sems):
    copies = []
    for place, first in enumerate(range(0, local_ref.shape[0], CHUNK)):
        piece = pl.ds(first, CHUNK)
        out_ref[piece] = field_ref[piece].astype(F32) + local_ref[piece]
        copies.append(pltpu.make_async_copy(out_ref.at[piece], out.at[piece], sems.at[place]))
        copies[-1].start()
    for copy in copies:
        copy.wait()


def add_field(local, field):
    shape = local.shape
    vmem, hbm = pl.BlockSpec(memory_space=pltpu.VMEM), pl.BlockSpec(memory_space=pltpu.HBM)
    return pl.pallas_call(
        add_kernel,
        in_specs=[vmem, vmem],
        out_specs=hbm,
        out_shape=jax.ShapeDtypeStruct(shape, F32),
        scratch_shapes=[
            pltpu.VMEM(shape, F32),
            pltpu.SemaphoreType.DMA((shape[0] // CHUNK,)),
        ],
        compiler_params=pltpu.CompilerParams(vmem_limit_bytes=24 << 20),
        name="add_field",
    )(resident(local), resident(field))


CONV_ROWS = 4


def conv_matrix(weight):
    outs, ins = weight.shape[1:]
    band = jnp.transpose(weight.reshape(3, 3, outs, ins), (1, 2, 0, 3)).reshape(3 * outs, 3 * ins)
    return jnp.concatenate(
        [
            jnp.pad(band, ((0, 0), (row * ins, (CONV_ROWS - 1 - row) * ins)))
            for row in range(CONV_ROWS)
        ],
        axis=0,
    )


def conv_kernel(
    matrix_ref, main_hbm, side_hbm, above_ref, below_ref, bias_ref, out_ref, all_ref, sems
):
    ins = matrix_ref.shape[1] // (CONV_ROWS + 2)
    outs, rows, width = out_ref.shape
    full = all_ref.shape[1]
    window = (CONV_ROWS + 2) * ins
    tall = 2 * CONV_ROWS
    inner = pl.ds(ins, rows * ins)
    copies = [
        pltpu.make_async_copy(main_hbm, all_ref.at[inner, pl.ds(0, width)], sems.at[0]),
        pltpu.make_async_copy(side_hbm, all_ref.at[inner, pl.ds(width, full - width)], sems.at[1]),
    ]
    for copy in copies:
        copy.start()
    all_ref[:ins, :] = above_ref[...]
    all_ref[(rows + 1) * ins :, :] = below_ref[...]
    for copy in copies:
        copy.wait()

    @pl.loop(0, rows // tall)
    def _(step):
        pieces = []
        for part in range(tall // CONV_ROWS):
            start = pl.multiple_of((step * tall + part * CONV_ROWS) * ins, ins)
            taps = dot(matrix_ref[...], all_ref[pl.ds(start, window), :])
            for row in range(CONV_ROWS):
                base = row * 3 * outs
                low = pltpu.roll(taps[base : base + outs], 1, 1)[:, :width]
                mid = taps[base + outs : base + 2 * outs, :width]
                high = pltpu.roll(taps[base + 2 * outs : base + 3 * outs], full - 1, 1)[:, :width]
                pieces.append(low + mid + high + bias_ref[:, :1])
        first = pl.multiple_of(step * tall, tall)
        out_ref[:, pl.ds(first, tall), :] = jnp.transpose(jnp.stack(pieces, axis=0), (1, 0, 2))


def conv(matrix, main, side, above, below, bias):
    outs = matrix.shape[0] // (3 * CONV_ROWS)
    ins = above.shape[0]
    rows, width = main.shape[0] // ins, main.shape[1]
    vmem, hbm = pl.BlockSpec(memory_space=pltpu.VMEM), pl.BlockSpec(memory_space=pltpu.HBM)
    return pl.pallas_call(
        conv_kernel,
        in_specs=[vmem, hbm, hbm, vmem, vmem, vmem],
        out_specs=vmem,
        out_shape=pltpu.VMEM((outs, rows, width), F32),
        scratch_shapes=[
            pltpu.VMEM(((rows + 2) * ins, above.shape[1]), BF),
            pltpu.SemaphoreType.DMA((2,)),
        ],
        compiler_params=pltpu.CompilerParams(vmem_limit_bytes=24 << 20),
        name="conv",
    )(
        resident(matrix),
        pltpu.with_memory_space_constraint(main, pltpu.HBM),
        pltpu.with_memory_space_constraint(side, pltpu.HBM),
        resident(above),
        resident(below),
        resident(bias),
    )


def swap(value, axis, back=False):
    count = lax.axis_size(axis)
    pairs = [(i, i + 1) for i in range(count - 1)]
    if back:
        pairs = [(b, a) for a, b in pairs]
    return lax.ppermute(value, axis, pairs)


def by_rows(field):
    channels, rows, width = field.shape
    main = jnp.transpose(field, (1, 0, 2)).reshape(rows * channels, width)
    pick = np.zeros((2, width), np.float32)
    pick[0, 0] = pick[1, width - 1] = 1.0
    ends = jnp.einsum("ry,ny->rn", pick.astype(BF), main, preferred_element_type=F32).astype(BF)
    return main, ends


def edge_rows(main, side, channels):
    return (
        jnp.concatenate([main[:channels], side[:channels]], axis=1),
        jnp.concatenate([main[-channels:], side[-channels:]], axis=1),
    )


def across_rows(first, last):
    return swap(last, "gx"), swap(first, "gx", back=True)


def across_columns(ends):
    return swap(ends[:1], "gy", back=True), swap(ends[1:], "gy")


def side_slots():
    place = np.zeros((2, 128), np.float32)
    place[0, 0] = place[1, 127] = 1.0
    return place.astype(BF)


def place_columns(right, left, slots):
    return jnp.einsum(
        "rn,rk->nk", jnp.concatenate([right, left]), slots, preferred_element_type=F32
    ).astype(BF)


def exchange(value, axes):
    return lax.all_to_all(value, axes, split_axis=0, concat_axis=0, tiled=True)


def pdot(form, left, right):
    return jnp.einsum(form, left, right, preferred_element_type=F32)


def weight_grads(spec, dmixed):
    real_s, imag_s = (spec[:, 0], spec[:, 1])
    real_d, imag_d = (dmixed[:, 0], dmixed[:, 1])
    form_w = "mcq,mdq->cdmq"
    grad_real = pdot(form_w, real_s, real_d) + pdot(form_w, imag_s, imag_d)
    grad_imag = pdot(form_w, real_s, imag_d) - pdot(form_w, imag_s, real_d)
    return jnp.stack([grad_real, grad_imag], axis=2)


def body(field_in, spectral_weight, conv_weight, conv_bias, upstream):
    strips, pieces = lax.axis_size("gx"), lax.axis_size("gy")
    owners = strips * pieces
    _, channels, width_x, width_y = field_in.shape
    length_x, length_y = width_x * strips, width_y * pieces
    scale = 1.0 / (length_x * length_y)
    both = ("gx", "gy")
    share = (strips, channels // strips, width_x, width_y)
    whole = (channels, width_x, width_y)

    table_x, table_y = x_table(length_x, owners), y_table(length_y, width_y)
    hold = lax.optimization_barrier
    tables = [
        jnp.asarray(np.concatenate([table_x, table_y[:width_y], table_y[width_y:]], axis=1)),
        jnp.asarray(np.concatenate([table_x.T, table_y], axis=0)),
    ]

    field = field_in[0]
    bias = jnp.broadcast_to(conv_bias[:, None], (channels, 128))
    block = exchange(field.reshape(share), "gx")
    main, ends = by_rows(field)
    right, left = across_columns(ends)
    weight = jnp.transpose(spectral_weight, (3, 2, 0, 1, 4))
    matrix = conv_matrix(conv_weight)
    side = place_columns(right, left, side_slots())
    first, last = edge_rows(main, side, channels)
    block, first, last, weight, matrix = hold((block, first, last, weight, matrix))
    parts = to_modes(block, False, 1.0, tables, owners)
    parts, first, last = hold((parts, first, last))
    parts = exchange(parts, both)
    above, below = across_rows(first, last)
    mixed, spec = mix(parts, weight, 1, strips)
    mixed, above, below = hold((mixed, above, below))
    arrived = exchange(mixed, both)
    local = conv(matrix, main, side, above, below, bias)
    arrived, local = hold((arrived, local))
    back = to_field(arrived, True, scale, tables, share)
    spectral = exchange(back, "gx").reshape(whole)

    dpre, activation = gate_both(local, spectral, upstream[0])
    dpre, taps, dweight = hold((dpre, conv_weight, spectral_weight))

    dblock = exchange(dpre.reshape(share), "gx")
    dmain, dends = by_rows(dpre)
    dright, dleft = across_columns(dends)
    dmatrix = conv_matrix(jnp.transpose(taps[::-1], (0, 2, 1)))
    dside = place_columns(dright, dleft, side_slots())
    dfirst, dlast = edge_rows(dmain, dside, channels)
    dblock, dmatrix, dfirst, dlast = hold((dblock, dmatrix, dfirst, dlast))
    dparts = to_modes(dblock, True, scale, tables, owners)
    dparts, dfirst, dlast, dweight = hold((dparts, dfirst, dlast, dweight))
    dparts = exchange(dparts, both)
    dweight = jnp.transpose(dweight, (3, 2, 1, 0, 4))
    dabove, dbelow = across_rows(dfirst, dlast)
    dparts, dweight = hold((dparts, dweight))
    dmixed, dspec = mix(dparts, dweight, -1, strips)
    dmixed, dabove, dbelow = hold((dmixed, dabove, dbelow))
    darrived = exchange(dmixed, both)
    dback = to_field(darrived, False, 1.0, tables, share)
    dback, dabove, dbelow, spec, dspec = hold((dback, dabove, dbelow, spec, dspec))
    dfield = exchange(dback, "gx").reshape(whole)
    back_local = conv(dmatrix, dmain, dside, dabove, dbelow, jnp.zeros_like(bias))
    slots = M1 // owners
    weight_grad = weight_grads(by_mode(spec, slots), by_mode(dspec, slots))
    dfield, back_local, weight_grad = hold((dfield, back_local, weight_grad))
    field_grad = add_field(back_local, dfield)
    return (activation[None], field_grad[None], weight_grad)


def solution(mesh):
    return jax.shard_map(
        body,
        mesh=mesh,
        in_specs=(
            P("dp", None, "gx", "gy"),
            P(None, None, None, ("gx", "gy"), None),
            P(),
            P(),
            P("dp", None, "gx", "gy"),
        ),
        out_specs=(
            P("dp", None, "gx", "gy"),
            P("dp", None, "gx", "gy"),
            P("dp", None, None, ("gx", "gy"), None),
        ),
        check_vma=False,
    )
```

```python
import functools
import math

import jax
import jax.numpy as jnp
import numpy as np
from jax import lax
from jax.experimental import pallas as pl
from jax.experimental.pallas import tpu as pltpu
from jax.sharding import PartitionSpec as P

M1 = 128
M2 = 128
BF = jnp.bfloat16
F32 = jnp.float32


def dot(left, right):
    return jnp.dot(left, right, preferred_element_type=F32)


@functools.lru_cache(maxsize=None)
def x_table(length, owners):
    slots = M1 // owners
    order = np.arange(M1).reshape(owners, slots).T.reshape(-1)
    modes = np.where(order < M1 // 2, order, order + length - M1)
    angle = (modes[:, None] * np.arange(length)[None, :] % length) * (2.0 * math.pi / length)
    table = np.concatenate([np.cos(angle), -np.sin(angle)], axis=0)
    return table.astype(np.float32).astype(jnp.bfloat16)


@functools.lru_cache(maxsize=None)
def y_table(length, width):
    angle = (np.arange(width)[:, None] * np.arange(M2)[None, :] % length) * (2.0 * math.pi / length)
    cosine, sine = np.cos(angle), np.sin(angle)
    table = np.concatenate(
        [np.concatenate([cosine, -sine], axis=1), np.concatenate([sine, cosine], axis=1)], axis=0
    )
    return table.astype(np.float32).astype(jnp.bfloat16)


def turn(values, quarter, sign):
    half = values.shape[1] // 2
    lane = lax.broadcasted_iota(jnp.int32, (1, 2 * half), 1)
    second = lane >= half
    q = jnp.where(second, lane - half, lane)
    step = lax.rem(q * quarter, 4)
    one = jnp.where(step == 0, 1.0, jnp.where(step == 2, -1.0, 0.0))
    imag = jnp.where(step == 1, 1.0, jnp.where(step == 3, -1.0, 0.0)) * sign
    swap = jnp.concatenate([values[:, half:], values[:, :half]], axis=1)
    return values * one + swap * jnp.where(second, imag, -imag)


def column_weight(half):
    lane = lax.broadcasted_iota(jnp.int32, (1, 2 * half), 1)
    return jnp.where((lane == 0) | (lane == half), 1.0, 2.0)


def resident(value):
    return pltpu.with_memory_space_constraint(value, pltpu.VMEM)


def on_chip(kernel, outs, scratch, name, *values, place=pltpu.VMEM, apart=()):
    spec = pl.BlockSpec(memory_space=pltpu.VMEM)
    many = isinstance(outs, list)
    return pl.pallas_call(
        kernel,
        in_specs=[spec] * len(values),
        out_specs=[spec] * len(outs) if many else spec,
        out_shape=[place(*out) for out in outs] if many else place(*outs),
        scratch_shapes=scratch,
        compiler_params=pltpu.CompilerParams(vmem_limit_bytes=24 << 20),
        name=name,
    )(*[value if index in apart else resident(value) for index, value in enumerate(values)])


def forward_kernel(weighted, factor, block_ref, table_ref, out_ref, rows_ref):
    length = block_ref.shape[0] * block_ref.shape[2]
    owners, rows, _ = out_ref.shape
    _, channels, _, width = block_ref.shape
    slots = M1 // owners
    for channel in range(channels):
        block = block_ref[:, channel].reshape(-1, width)
        spec_x = dot(table_ref[:, :length], block)
        if factor != 1.0:
            spec_x = spec_x * factor
        spec_x = spec_x.astype(BF)
        spec = dot(spec_x[:M1], table_ref[:, length : length + 2 * M2])
        spec = spec + dot(spec_x[M1:], table_ref[:, length + 2 * M2 :])
        spec = turn(spec, lax.axis_index("gy"), -1.0)
        if weighted:
            spec = spec * column_weight(M2)
        for slot in range(slots):
            for part in range(2):
                rows_ref[(channel * slots + slot) * 2 + part] = spec[
                    slot * owners : (slot + 1) * owners, part * M2 : (part + 1) * M2
                ]
    out_ref[...] = jnp.transpose(rows_ref[...], (1, 0, 2)).astype(BF)


def to_modes(block, weighted, factor, tables, owners):
    rows = block.shape[1] * (M1 // owners) * 2
    return on_chip(
        functools.partial(forward_kernel, weighted, factor),
        ((owners, rows, M2), BF),
        [pltpu.VMEM((rows, owners, M2), F32)],
        "to_modes",
        block,
        tables[0],
        place=jax.ShapeDtypeStruct,
    )


def inverse_kernel(weighted, factor, spec_ref, table_ref, out_ref, rows_ref):
    owners = spec_ref.shape[0]
    strips, channels, rows, width = out_ref.shape
    length = strips * rows
    slots = M1 // owners
    rows_ref[...] = jnp.transpose(spec_ref[...].astype(F32), (1, 0, 2))
    for channel in range(channels):
        spec = jnp.concatenate(
            [
                jnp.concatenate(
                    [rows_ref[(channel * slots + slot) * 2 + part] for part in range(2)], axis=1
                )
                for slot in range(slots)
            ],
            axis=0,
        )
        spec = turn(spec, lax.axis_index("gy"), 1.0)
        if weighted:
            spec = spec * column_weight(M2)
        spec = spec.astype(BF)
        over_y = [
            lax.dot_general(
                spec, table_ref[first : first + width], (((1,), (1,)), ((), ())), preferred_element_type=F32
            ).astype(BF)
            for first in (length, length + width)
        ]
        total = dot(table_ref[:length], jnp.concatenate(over_y, axis=0))
        if factor != 1.0:
            total = total * factor
        out_ref[:, channel] = total.astype(BF).reshape(strips, rows, width)


def to_field(spec, weighted, factor, tables, shape):
    owners, rows, _ = spec.shape
    return on_chip(
        functools.partial(inverse_kernel, weighted, factor),
        (shape, BF),
        [pltpu.VMEM((rows, owners, M2), F32)],
        "to_field",
        spec,
        tables[1],
    )


def mix_kernel(sign, parts_ref, weight_ref, out_ref, spec_ref, sum_ref, mixed_ref, place_ref):
    strips, rows, kept = spec_ref.shape
    pieces = parts_ref.shape[0] // strips
    slots, _, ins, outs, _ = weight_ref.shape
    share = ins // strips
    total = jnp.sum(parts_ref[...].reshape(strips, pieces, rows, kept).astype(F32), axis=1).astype(BF)
    spec_ref[...] = total
    sum_ref[...] = total.astype(F32)
    for slot in range(slots):
        real = jnp.zeros((outs, kept), F32)
        imag = jnp.zeros((outs, kept), F32)
        for channel in range(ins):
            strip, row = channel // share, (channel % share * slots + slot) * 2
            real_s = sum_ref[strip, row : row + 1, :]
            imag_s = sum_ref[strip, row + 1 : row + 2, :]
            real_w = weight_ref[slot, 0, channel].astype(F32)
            imag_w = weight_ref[slot, 1, channel].astype(F32)
            if sign > 0:
                real = real + (real_s * real_w - imag_s * imag_w)
                imag = imag + (real_s * imag_w + imag_s * real_w)
            else:
                real = real + (real_s * real_w + imag_s * imag_w)
                imag = imag + (imag_s * real_w - real_s * imag_w)
        mixed_ref[slot * 2] = real
        mixed_ref[slot * 2 + 1] = imag
    share = outs // strips
    for channel in range(share):
        for row in range(2 * slots):
            place_ref[:, channel * 2 * slots + row, :] = mixed_ref[
                row, pl.ds(channel, strips, stride=share), :
            ]
    placed = place_ref[...].astype(BF)
    out_ref[...] = jnp.broadcast_to(placed[:, None], (strips, pieces, rows, kept)).reshape(
        strips * pieces, rows, kept
    )


def mix(parts, weight, sign, strips):
    owners, rows, kept = parts.shape
    slots, _, _, outs, _ = weight.shape
    return on_chip(
        functools.partial(mix_kernel, sign),
        [((owners, rows, kept), BF), ((strips, rows, kept), BF)],
        [
            pltpu.VMEM((strips, rows, kept), F32),
            pltpu.VMEM((2 * slots, outs, kept), F32),
            pltpu.VMEM((strips, rows, kept), F32),
        ],
        "mix",
        parts,
        weight,
    )


def by_mode(rows, slots):
    strips, count, kept = rows.shape
    split = rows.reshape(strips, count // slots // 2, slots, 2, kept)
    return jnp.transpose(split, (2, 3, 0, 1, 4)).reshape(slots, 2, -1, kept)


CHUNK = 4


def gate_kernel(local_ref, field_ref, up_ref, grad_out, act_out, grad_ref, act_ref, sems):
    copies = []
    for place, first in enumerate(range(0, local_ref.shape[0], CHUNK)):
        piece = pl.ds(first, CHUNK)
        pre = field_ref[piece].astype(F32) + local_ref[piece]
        gate = 0.5 + 0.5 * jnp.tanh(0.5 * pre)
        grad_ref[piece] = (up_ref[piece].astype(F32) * gate * (1.0 + pre * (1.0 - gate))).astype(BF)
        act_ref[piece] = pre * gate
        for index, (ref, out) in enumerate(((grad_ref, grad_out), (act_ref, act_out))):
            copies.append(pltpu.make_async_copy(ref.at[piece], out.at[piece], sems.at[index, place]))
            copies[-1].start()
    for copy in copies:
        copy.wait()


def gate_both(local, field, upstream):
    shape = local.shape
    vmem, hbm = pl.BlockSpec(memory_space=pltpu.VMEM), pl.BlockSpec(memory_space=pltpu.HBM)
    return pl.pallas_call(
        gate_kernel,
        in_specs=[vmem] * 3,
        out_specs=[hbm] * 2,
        out_shape=[jax.ShapeDtypeStruct(shape, BF), jax.ShapeDtypeStruct(shape, F32)],
        scratch_shapes=[
            pltpu.VMEM(shape, BF),
            pltpu.VMEM(shape, F32),
            pltpu.SemaphoreType.DMA((2, shape[0] // CHUNK)),
        ],
        compiler_params=pltpu.CompilerParams(vmem_limit_bytes=24 << 20),
        name="gate_both",
    )(resident(local), resident(field), resident(upstream))


def add_kernel(local_ref, field_ref, out, out_ref, sems):
    copies = []
    for place, first in enumerate(range(0, local_ref.shape[0], CHUNK)):
        piece = pl.ds(first, CHUNK)
        out_ref[piece] = field_ref[piece].astype(F32) + local_ref[piece]
        copies.append(pltpu.make_async_copy(out_ref.at[piece], out.at[piece], sems.at[place]))
        copies[-1].start()
    for copy in copies:
        copy.wait()


def add_field(local, field):
    shape = local.shape
    vmem, hbm = pl.BlockSpec(memory_space=pltpu.VMEM), pl.BlockSpec(memory_space=pltpu.HBM)
    return pl.pallas_call(
        add_kernel,
        in_specs=[vmem, vmem],
        out_specs=hbm,
        out_shape=jax.ShapeDtypeStruct(shape, F32),
        scratch_shapes=[
            pltpu.VMEM(shape, F32),
            pltpu.SemaphoreType.DMA((shape[0] // CHUNK,)),
        ],
        compiler_params=pltpu.CompilerParams(vmem_limit_bytes=24 << 20),
        name="add_field",
    )(resident(local), resident(field))


CONV_ROWS = 4


def conv_matrix(weight):
    outs, ins = weight.shape[1:]
    band = jnp.transpose(weight.reshape(3, 3, outs, ins), (1, 2, 0, 3)).reshape(3 * outs, 3 * ins)
    return jnp.concatenate(
        [
            jnp.pad(band, ((0, 0), (row * ins, (CONV_ROWS - 1 - row) * ins)))
            for row in range(CONV_ROWS)
        ],
        axis=0,
    )


def conv_kernel(
    matrix_ref, main_hbm, side_hbm, above_ref, below_ref, bias_ref, out_ref, all_ref, sems
):
    ins = matrix_ref.shape[1] // (CONV_ROWS + 2)
    outs, rows, width = out_ref.shape
    full = all_ref.shape[1]
    window = (CONV_ROWS + 2) * ins
    tall = 2 * CONV_ROWS
    inner = pl.ds(ins, rows * ins)
    copies = [
        pltpu.make_async_copy(main_hbm, all_ref.at[inner, pl.ds(0, width)], sems.at[0]),
        pltpu.make_async_copy(side_hbm, all_ref.at[inner, pl.ds(width, full - width)], sems.at[1]),
    ]
    for copy in copies:
        copy.start()
    all_ref[:ins, :] = above_ref[...]
    all_ref[(rows + 1) * ins :, :] = below_ref[...]
    for copy in copies:
        copy.wait()

    @pl.loop(0, rows // tall)
    def _(step):
        pieces = []
        for part in range(tall // CONV_ROWS):
            start = pl.multiple_of((step * tall + part * CONV_ROWS) * ins, ins)
            taps = dot(matrix_ref[...], all_ref[pl.ds(start, window), :])
            for row in range(CONV_ROWS):
                base = row * 3 * outs
                low = pltpu.roll(taps[base : base + outs], 1, 1)[:, :width]
                mid = taps[base + outs : base + 2 * outs, :width]
                high = pltpu.roll(taps[base + 2 * outs : base + 3 * outs], full - 1, 1)[:, :width]
                pieces.append(low + mid + high + bias_ref[:, :1])
        first = pl.multiple_of(step * tall, tall)
        out_ref[:, pl.ds(first, tall), :] = jnp.transpose(jnp.stack(pieces, axis=0), (1, 0, 2))


def conv(matrix, main, side, above, below, bias):
    outs = matrix.shape[0] // (3 * CONV_ROWS)
    ins = above.shape[0]
    rows, width = main.shape[0] // ins, main.shape[1]
    vmem, hbm = pl.BlockSpec(memory_space=pltpu.VMEM), pl.BlockSpec(memory_space=pltpu.HBM)
    return pl.pallas_call(
        conv_kernel,
        in_specs=[vmem, hbm, hbm, vmem, vmem, vmem],
        out_specs=vmem,
        out_shape=pltpu.VMEM((outs, rows, width), F32),
        scratch_shapes=[
            pltpu.VMEM(((rows + 2) * ins, above.shape[1]), BF),
            pltpu.SemaphoreType.DMA((2,)),
        ],
        compiler_params=pltpu.CompilerParams(vmem_limit_bytes=24 << 20),
        name="conv",
    )(
        resident(matrix),
        pltpu.with_memory_space_constraint(main, pltpu.HBM),
        pltpu.with_memory_space_constraint(side, pltpu.HBM),
        resident(above),
        resident(below),
        resident(bias),
    )


def conv_stacked_kernel(matrix_ref, main_ref, side_ref, bias_ref, out_ref):
    ins = matrix_ref.shape[1] // (CONV_ROWS + 2)
    outs, rows, width = out_ref.shape
    window = (CONV_ROWS + 2) * ins
    tall = 2 * CONV_ROWS

    @pl.loop(0, rows // tall)
    def _(step):
        pieces = []
        for part in range(tall // CONV_ROWS):
            start = pl.multiple_of((step * tall + part * CONV_ROWS) * ins, ins)
            main = dot(matrix_ref[...], main_ref[pl.ds(start, window), :])
            side = dot(matrix_ref[...], side_ref[pl.ds(start, window), :])
            taps = jnp.concatenate([main, side], axis=1)
            full = taps.shape[1]
            for row in range(CONV_ROWS):
                base = row * 3 * outs
                low = pltpu.roll(taps[base : base + outs], 1, 1)[:, :width]
                mid = taps[base + outs : base + 2 * outs, :width]
                high = pltpu.roll(taps[base + 2 * outs : base + 3 * outs], full - 1, 1)[:, :width]
                pieces.append(low + mid + high + bias_ref[:, :1])
        first = pl.multiple_of(step * tall, tall)
        out_ref[:, pl.ds(first, tall), :] = jnp.transpose(jnp.stack(pieces, axis=0), (1, 0, 2))


def conv_stacked(matrix, main, side, bias, rows):
    outs = matrix.shape[0] // (3 * CONV_ROWS)
    return on_chip(
        conv_stacked_kernel,
        ((outs, rows, main.shape[1]), F32),
        [],
        "conv_stacked",
        matrix,
        pltpu.with_memory_space_constraint(main, pltpu.HBM),
        side,
        bias,
        apart=(1,),
    )


def swap(value, axis, back=False):
    count = lax.axis_size(axis)
    pairs = [(i, i + 1) for i in range(count - 1)]
    if back:
        pairs = [(b, a) for a, b in pairs]
    return lax.ppermute(value, axis, pairs)


def across_edges(field):
    return swap(field[:, -1], "gx"), swap(field[:, 0], "gx", back=True)


def stack_rows(field, above, below):
    channels, rows, width = field.shape
    main = jnp.concatenate([above[None], jnp.transpose(field, (1, 0, 2)), below[None]], axis=0)
    main = main.reshape((rows + 2) * channels, width)
    pick = np.zeros((2, width), np.float32)
    pick[0, 0] = pick[1, width - 1] = 1.0
    ends = jnp.einsum("ry,ny->rn", pick.astype(BF), main, preferred_element_type=F32).astype(BF)
    return main, ends


def by_rows(field):
    channels, rows, width = field.shape
    main = jnp.transpose(field, (1, 0, 2)).reshape(rows * channels, width)
    pick = np.zeros((2, width), np.float32)
    pick[0, 0] = pick[1, width - 1] = 1.0
    ends = jnp.einsum("ry,ny->rn", pick.astype(BF), main, preferred_element_type=F32).astype(BF)
    return main, ends


def edge_rows(main, side, channels):
    return (
        jnp.concatenate([main[:channels], side[:channels]], axis=1),
        jnp.concatenate([main[-channels:], side[-channels:]], axis=1),
    )


def across_rows(first, last):
    return swap(last, "gx"), swap(first, "gx", back=True)


def across_columns(ends):
    return swap(ends[:1], "gy", back=True), swap(ends[1:], "gy")


def side_slots():
    place = np.zeros((2, 128), np.float32)
    place[0, 0] = place[1, 127] = 1.0
    return place.astype(BF)


def place_columns(right, left, slots):
    return jnp.einsum(
        "rn,rk->nk", jnp.concatenate([right, left]), slots, preferred_element_type=F32
    ).astype(BF)


def exchange(value, axes):
    return lax.all_to_all(value, axes, split_axis=0, concat_axis=0, tiled=True)


def pdot(form, left, right):
    return jnp.einsum(form, left, right, preferred_element_type=F32)


def weight_grads(spec, dmixed):
    real_s, imag_s = (spec[:, 0], spec[:, 1])
    real_d, imag_d = (dmixed[:, 0], dmixed[:, 1])
    form_w = "mcq,mdq->cdmq"
    grad_real = pdot(form_w, real_s, real_d) + pdot(form_w, imag_s, imag_d)
    grad_imag = pdot(form_w, real_s, imag_d) - pdot(form_w, imag_s, real_d)
    return jnp.stack([grad_real, grad_imag], axis=2)


def body(field_in, spectral_weight, conv_weight, conv_bias, upstream):
    strips, pieces = lax.axis_size("gx"), lax.axis_size("gy")
    owners = strips * pieces
    _, channels, width_x, width_y = field_in.shape
    length_x, length_y = width_x * strips, width_y * pieces
    scale = 1.0 / (length_x * length_y)
    both = ("gx", "gy")
    share = (strips, channels // strips, width_x, width_y)
    whole = (channels, width_x, width_y)

    table_x, table_y = x_table(length_x, owners), y_table(length_y, width_y)
    hold = lax.optimization_barrier
    tables = [
        jnp.asarray(np.concatenate([table_x, table_y[:width_y], table_y[width_y:]], axis=1)),
        jnp.asarray(np.concatenate([table_x.T, table_y], axis=0)),
    ]

    field = field_in[0]
    bias = jnp.broadcast_to(conv_bias[:, None], (channels, 128))
    block = exchange(field.reshape(share), "gx")
    main, ends = by_rows(field)
    right, left = across_columns(ends)
    weight = jnp.transpose(spectral_weight, (3, 2, 0, 1, 4))
    matrix = conv_matrix(conv_weight)
    block, weight, matrix = hold((block, weight, matrix))
    parts = to_modes(block, False, 1.0, tables, owners)
    parts, right, left, places = hold((parts, right, left, side_slots()))
    parts = exchange(parts, both)
    side = place_columns(right, left, places)
    above, below = across_rows(*edge_rows(main, side, channels))
    mixed, spec = mix(parts, weight, 1, strips)
    mixed, above, below = hold((mixed, above, below))
    arrived = exchange(mixed, both)
    local = conv(matrix, main, side, above, below, bias)
    arrived, local = hold((arrived, local))
    back = to_field(arrived, True, scale, tables, share)
    spectral = exchange(back, "gx").reshape(whole)

    dpre, activation = gate_both(local, spectral, upstream[0])

    dblock = exchange(dpre.reshape(share), "gx")
    dabove, dbelow = across_edges(dpre)
    dparts = to_modes(dblock, True, scale, tables, owners)
    dparts, dhere, dabove, dbelow, taps, dweight = hold(
        (dparts, dpre, dabove, dbelow, conv_weight, spectral_weight)
    )
    dparts = exchange(dparts, both)
    dmatrix = conv_matrix(jnp.transpose(taps[::-1], (0, 2, 1)))
    dweight = jnp.transpose(dweight, (3, 2, 1, 0, 4))
    dmain, dends = stack_rows(dhere, dabove, dbelow)
    dparts, dends, dmain, dmatrix, dweight = hold((dparts, dends, dmain, dmatrix, dweight))
    dmixed, dspec = mix(dparts, dweight, -1, strips)
    darrived = exchange(dmixed, both)
    dright, dleft = across_columns(dends)
    dback = to_field(darrived, False, 1.0, tables, share)
    dback, dright, dleft, places, spec, dspec = hold((dback, dright, dleft, places, spec, dspec))
    dfield = exchange(dback, "gx").reshape(whole)
    back_local = conv_stacked(dmatrix, dmain, place_columns(dright, dleft, places), jnp.zeros_like(bias), width_x)
    slots = M1 // owners
    weight_grad = weight_grads(by_mode(spec, slots), by_mode(dspec, slots))
    dfield, back_local, weight_grad = hold((dfield, back_local, weight_grad))
    field_grad = add_field(back_local, dfield)
    return (activation[None], field_grad[None], weight_grad)


def solution(mesh):
    return jax.shard_map(
        body,
        mesh=mesh,
        in_specs=(
            P("dp", None, "gx", "gy"),
            P(None, None, None, ("gx", "gy"), None),
            P(),
            P(),
            P("dp", None, "gx", "gy"),
        ),
        out_specs=(
            P("dp", None, "gx", "gy"),
            P("dp", None, "gx", "gy"),
            P("dp", None, None, ("gx", "gy"), None),
        ),
        check_vma=False,
    )
```

```python
import functools
import math

import jax
import jax.numpy as jnp
import numpy as np
from jax import lax
from jax.experimental import pallas as pl
from jax.experimental.pallas import tpu as pltpu
from jax.sharding import PartitionSpec as P

M1 = 128
M2 = 128
BF = jnp.bfloat16
F32 = jnp.float32


def dot(left, right):
    return jnp.dot(left, right, preferred_element_type=F32)


@functools.lru_cache(maxsize=None)
def x_table(length, owners):
    slots = M1 // owners
    order = np.arange(M1).reshape(owners, slots).T.reshape(-1)
    modes = np.where(order < M1 // 2, order, order + length - M1)
    angle = (modes[:, None] * np.arange(length)[None, :] % length) * (2.0 * math.pi / length)
    table = np.concatenate([np.cos(angle), -np.sin(angle)], axis=0)
    return table.astype(np.float32).astype(jnp.bfloat16)


@functools.lru_cache(maxsize=None)
def y_table(length, width):
    angle = (np.arange(width)[:, None] * np.arange(M2)[None, :] % length) * (2.0 * math.pi / length)
    cosine, sine = np.cos(angle), np.sin(angle)
    table = np.concatenate(
        [np.concatenate([cosine, -sine], axis=1), np.concatenate([sine, cosine], axis=1)], axis=0
    )
    return table.astype(np.float32).astype(jnp.bfloat16)


def turn(values, quarter, sign):
    half = values.shape[1] // 2
    lane = lax.broadcasted_iota(jnp.int32, (1, 2 * half), 1)
    second = lane >= half
    q = jnp.where(second, lane - half, lane)
    step = lax.rem(q * quarter, 4)
    one = jnp.where(step == 0, 1.0, jnp.where(step == 2, -1.0, 0.0))
    imag = jnp.where(step == 1, 1.0, jnp.where(step == 3, -1.0, 0.0)) * sign
    swap = jnp.concatenate([values[:, half:], values[:, :half]], axis=1)
    return values * one + swap * jnp.where(second, imag, -imag)


def column_weight(half):
    lane = lax.broadcasted_iota(jnp.int32, (1, 2 * half), 1)
    return jnp.where((lane == 0) | (lane == half), 1.0, 2.0)


def resident(value):
    return pltpu.with_memory_space_constraint(value, pltpu.VMEM)


def on_chip(kernel, outs, scratch, name, *values, place=pltpu.VMEM, apart=()):
    spec = pl.BlockSpec(memory_space=pltpu.VMEM)
    many = isinstance(outs, list)
    return pl.pallas_call(
        kernel,
        in_specs=[spec] * len(values),
        out_specs=[spec] * len(outs) if many else spec,
        out_shape=[place(*out) for out in outs] if many else place(*outs),
        scratch_shapes=scratch,
        compiler_params=pltpu.CompilerParams(vmem_limit_bytes=24 << 20),
        name=name,
    )(*[value if index in apart else resident(value) for index, value in enumerate(values)])


def forward_kernel(weighted, factor, block_ref, table_ref, out_ref, rows_ref):
    length = block_ref.shape[0] * block_ref.shape[2]
    owners, rows, _ = out_ref.shape
    _, channels, _, width = block_ref.shape
    slots = M1 // owners
    for channel in range(channels):
        block = block_ref[:, channel].reshape(-1, width)
        spec_x = dot(table_ref[:, :length], block)
        if factor != 1.0:
            spec_x = spec_x * factor
        spec_x = spec_x.astype(BF)
        spec = dot(spec_x[:M1], table_ref[:, length : length + 2 * M2])
        spec = spec + dot(spec_x[M1:], table_ref[:, length + 2 * M2 :])
        spec = turn(spec, lax.axis_index("gy"), -1.0)
        if weighted:
            spec = spec * column_weight(M2)
        for slot in range(slots):
            for part in range(2):
                rows_ref[(channel * slots + slot) * 2 + part] = spec[
                    slot * owners : (slot + 1) * owners, part * M2 : (part + 1) * M2
                ]
    out_ref[...] = jnp.transpose(rows_ref[...], (1, 0, 2)).astype(BF)


def to_modes(block, weighted, factor, tables, owners):
    rows = block.shape[1] * (M1 // owners) * 2
    return on_chip(
        functools.partial(forward_kernel, weighted, factor),
        ((owners, rows, M2), BF),
        [pltpu.VMEM((rows, owners, M2), F32)],
        "to_modes",
        block,
        tables[0],
        place=jax.ShapeDtypeStruct,
    )


def inverse_kernel(weighted, factor, spec_ref, table_ref, out_ref, rows_ref):
    owners = spec_ref.shape[0]
    strips, channels, rows, width = out_ref.shape
    length = strips * rows
    slots = M1 // owners
    rows_ref[...] = jnp.transpose(spec_ref[...].astype(F32), (1, 0, 2))
    for channel in range(channels):
        spec = jnp.concatenate(
            [
                jnp.concatenate(
                    [rows_ref[(channel * slots + slot) * 2 + part] for part in range(2)], axis=1
                )
                for slot in range(slots)
            ],
            axis=0,
        )
        spec = turn(spec, lax.axis_index("gy"), 1.0)
        if weighted:
            spec = spec * column_weight(M2)
        spec = spec.astype(BF)
        over_y = [
            lax.dot_general(
                spec, table_ref[first : first + width], (((1,), (1,)), ((), ())), preferred_element_type=F32
            ).astype(BF)
            for first in (length, length + width)
        ]
        total = dot(table_ref[:length], jnp.concatenate(over_y, axis=0))
        if factor != 1.0:
            total = total * factor
        out_ref[:, channel] = total.astype(BF).reshape(strips, rows, width)


def to_field(spec, weighted, factor, tables, shape):
    owners, rows, _ = spec.shape
    return on_chip(
        functools.partial(inverse_kernel, weighted, factor),
        (shape, BF),
        [pltpu.VMEM((rows, owners, M2), F32)],
        "to_field",
        spec,
        tables[1],
    )


def mix_kernel(sign, parts_ref, weight_ref, out_ref, spec_ref, sum_ref, mixed_ref, place_ref):
    strips, rows, kept = spec_ref.shape
    pieces = parts_ref.shape[0] // strips
    slots, _, ins, outs, _ = weight_ref.shape
    share = ins // strips
    total = jnp.sum(parts_ref[...].reshape(strips, pieces, rows, kept).astype(F32), axis=1).astype(BF)
    spec_ref[...] = total
    sum_ref[...] = total.astype(F32)
    for slot in range(slots):
        real = jnp.zeros((outs, kept), F32)
        imag = jnp.zeros((outs, kept), F32)
        for channel in range(ins):
            strip, row = channel // share, (channel % share * slots + slot) * 2
            real_s = sum_ref[strip, row : row + 1, :]
            imag_s = sum_ref[strip, row + 1 : row + 2, :]
            real_w = weight_ref[slot, 0, channel].astype(F32)
            imag_w = weight_ref[slot, 1, channel].astype(F32)
            if sign > 0:
                real = real + (real_s * real_w - imag_s * imag_w)
                imag = imag + (real_s * imag_w + imag_s * real_w)
            else:
                real = real + (real_s * real_w + imag_s * imag_w)
                imag = imag + (imag_s * real_w - real_s * imag_w)
        mixed_ref[slot * 2] = real
        mixed_ref[slot * 2 + 1] = imag
    share = outs // strips
    for channel in range(share):
        for row in range(2 * slots):
            place_ref[:, channel * 2 * slots + row, :] = mixed_ref[
                row, pl.ds(channel, strips, stride=share), :
            ]
    placed = place_ref[...].astype(BF)
    out_ref[...] = jnp.broadcast_to(placed[:, None], (strips, pieces, rows, kept)).reshape(
        strips * pieces, rows, kept
    )


def mix(parts, weight, sign, strips):
    owners, rows, kept = parts.shape
    slots, _, _, outs, _ = weight.shape
    return on_chip(
        functools.partial(mix_kernel, sign),
        [((owners, rows, kept), BF), ((strips, rows, kept), BF)],
        [
            pltpu.VMEM((strips, rows, kept), F32),
            pltpu.VMEM((2 * slots, outs, kept), F32),
            pltpu.VMEM((strips, rows, kept), F32),
        ],
        "mix",
        parts,
        weight,
    )


def by_mode(rows, slots):
    strips, count, kept = rows.shape
    split = rows.reshape(strips, count // slots // 2, slots, 2, kept)
    return jnp.transpose(split, (2, 3, 0, 1, 4)).reshape(slots, 2, -1, kept)


CHUNK = 4


def gate_kernel(local_ref, field_ref, up_ref, grad_out, act_out, grad_ref, act_ref, sems):
    copies = []
    for place, first in enumerate(range(0, local_ref.shape[0], CHUNK)):
        piece = pl.ds(first, CHUNK)
        pre = field_ref[piece].astype(F32) + local_ref[piece]
        gate = 0.5 + 0.5 * jnp.tanh(0.5 * pre)
        grad_ref[piece] = (up_ref[piece].astype(F32) * gate * (1.0 + pre * (1.0 - gate))).astype(BF)
        act_ref[piece] = pre * gate
        for index, (ref, out) in enumerate(((grad_ref, grad_out), (act_ref, act_out))):
            copies.append(pltpu.make_async_copy(ref.at[piece], out.at[piece], sems.at[index, place]))
            copies[-1].start()
    for copy in copies:
        copy.wait()


def gate_both(local, field, upstream):
    shape = local.shape
    vmem, hbm = pl.BlockSpec(memory_space=pltpu.VMEM), pl.BlockSpec(memory_space=pltpu.HBM)
    return pl.pallas_call(
        gate_kernel,
        in_specs=[vmem] * 3,
        out_specs=[hbm] * 2,
        out_shape=[jax.ShapeDtypeStruct(shape, BF), jax.ShapeDtypeStruct(shape, F32)],
        scratch_shapes=[
            pltpu.VMEM(shape, BF),
            pltpu.VMEM(shape, F32),
            pltpu.SemaphoreType.DMA((2, shape[0] // CHUNK)),
        ],
        compiler_params=pltpu.CompilerParams(vmem_limit_bytes=24 << 20),
        name="gate_both",
    )(resident(local), resident(field), resident(upstream))


def add_kernel(local_ref, field_ref, out, out_ref, sems):
    copies = []
    for place, first in enumerate(range(0, local_ref.shape[0], CHUNK)):
        piece = pl.ds(first, CHUNK)
        out_ref[piece] = field_ref[piece].astype(F32) + local_ref[piece]
        copies.append(pltpu.make_async_copy(out_ref.at[piece], out.at[piece], sems.at[place]))
        copies[-1].start()
    for copy in copies:
        copy.wait()


def add_field(local, field):
    shape = local.shape
    vmem, hbm = pl.BlockSpec(memory_space=pltpu.VMEM), pl.BlockSpec(memory_space=pltpu.HBM)
    return pl.pallas_call(
        add_kernel,
        in_specs=[vmem, vmem],
        out_specs=hbm,
        out_shape=jax.ShapeDtypeStruct(shape, F32),
        scratch_shapes=[
            pltpu.VMEM(shape, F32),
            pltpu.SemaphoreType.DMA((shape[0] // CHUNK,)),
        ],
        compiler_params=pltpu.CompilerParams(vmem_limit_bytes=24 << 20),
        name="add_field",
    )(resident(local), resident(field))


CONV_ROWS = 4


def conv_matrix(weight):
    outs, ins = weight.shape[1:]
    band = jnp.transpose(weight.reshape(3, 3, outs, ins), (1, 2, 0, 3)).reshape(3 * outs, 3 * ins)
    return jnp.concatenate(
        [
            jnp.pad(band, ((0, 0), (row * ins, (CONV_ROWS - 1 - row) * ins)))
            for row in range(CONV_ROWS)
        ],
        axis=0,
    )


def conv_kernel(
    matrix_ref, main_hbm, side_hbm, above_ref, below_ref, bias_ref, out_ref, all_ref, sems
):
    ins = matrix_ref.shape[1] // (CONV_ROWS + 2)
    outs, rows, width = out_ref.shape
    full = all_ref.shape[1]
    window = (CONV_ROWS + 2) * ins
    tall = 2 * CONV_ROWS
    inner = pl.ds(ins, rows * ins)
    copies = [
        pltpu.make_async_copy(main_hbm, all_ref.at[inner, pl.ds(0, width)], sems.at[0]),
        pltpu.make_async_copy(side_hbm, all_ref.at[inner, pl.ds(width, full - width)], sems.at[1]),
    ]
    for copy in copies:
        copy.start()
    all_ref[:ins, :] = above_ref[...]
    all_ref[(rows + 1) * ins :, :] = below_ref[...]
    for copy in copies:
        copy.wait()

    @pl.loop(0, rows // tall)
    def _(step):
        pieces = []
        for part in range(tall // CONV_ROWS):
            start = pl.multiple_of((step * tall + part * CONV_ROWS) * ins, ins)
            taps = dot(matrix_ref[...], all_ref[pl.ds(start, window), :])
            for row in range(CONV_ROWS):
                base = row * 3 * outs
                low = pltpu.roll(taps[base : base + outs], 1, 1)[:, :width]
                mid = taps[base + outs : base + 2 * outs, :width]
                high = pltpu.roll(taps[base + 2 * outs : base + 3 * outs], full - 1, 1)[:, :width]
                pieces.append(low + mid + high + bias_ref[:, :1])
        first = pl.multiple_of(step * tall, tall)
        out_ref[:, pl.ds(first, tall), :] = jnp.transpose(jnp.stack(pieces, axis=0), (1, 0, 2))


def conv(matrix, main, side, above, below, bias):
    outs = matrix.shape[0] // (3 * CONV_ROWS)
    ins = above.shape[0]
    rows, width = main.shape[0] // ins, main.shape[1]
    vmem, hbm = pl.BlockSpec(memory_space=pltpu.VMEM), pl.BlockSpec(memory_space=pltpu.HBM)
    return pl.pallas_call(
        conv_kernel,
        in_specs=[vmem, hbm, hbm, vmem, vmem, vmem],
        out_specs=vmem,
        out_shape=pltpu.VMEM((outs, rows, width), F32),
        scratch_shapes=[
            pltpu.VMEM(((rows + 2) * ins, above.shape[1]), BF),
            pltpu.SemaphoreType.DMA((2,)),
        ],
        compiler_params=pltpu.CompilerParams(vmem_limit_bytes=24 << 20),
        name="conv",
    )(
        resident(matrix),
        pltpu.with_memory_space_constraint(main, pltpu.HBM),
        pltpu.with_memory_space_constraint(side, pltpu.HBM),
        resident(above),
        resident(below),
        resident(bias),
    )


def conv_stacked_kernel(matrix_ref, main_ref, side_ref, bias_ref, out_ref):
    ins = matrix_ref.shape[1] // (CONV_ROWS + 2)
    outs, rows, width = out_ref.shape
    window = (CONV_ROWS + 2) * ins
    tall = 2 * CONV_ROWS

    @pl.loop(0, rows // tall)
    def _(step):
        pieces = []
        for part in range(tall // CONV_ROWS):
            start = pl.multiple_of((step * tall + part * CONV_ROWS) * ins, ins)
            main = dot(matrix_ref[...], main_ref[pl.ds(start, window), :])
            side = dot(matrix_ref[...], side_ref[pl.ds(start, window), :])
            taps = jnp.concatenate([main, side], axis=1)
            full = taps.shape[1]
            for row in range(CONV_ROWS):
                base = row * 3 * outs
                low = pltpu.roll(taps[base : base + outs], 1, 1)[:, :width]
                mid = taps[base + outs : base + 2 * outs, :width]
                high = pltpu.roll(taps[base + 2 * outs : base + 3 * outs], full - 1, 1)[:, :width]
                pieces.append(low + mid + high + bias_ref[:, :1])
        first = pl.multiple_of(step * tall, tall)
        out_ref[:, pl.ds(first, tall), :] = jnp.transpose(jnp.stack(pieces, axis=0), (1, 0, 2))


def conv_stacked(matrix, main, side, bias, rows):
    outs = matrix.shape[0] // (3 * CONV_ROWS)
    return on_chip(
        conv_stacked_kernel,
        ((outs, rows, main.shape[1]), F32),
        [],
        "conv_stacked",
        matrix,
        pltpu.with_memory_space_constraint(main, pltpu.HBM),
        side,
        bias,
        apart=(1,),
    )


def swap(value, axis, back=False):
    count = lax.axis_size(axis)
    pairs = [(i, i + 1) for i in range(count - 1)]
    if back:
        pairs = [(b, a) for a, b in pairs]
    return lax.ppermute(value, axis, pairs)


def across_edges(field):
    return swap(field[:, -1], "gx"), swap(field[:, 0], "gx", back=True)


def stack_rows(field, above, below):
    channels, rows, width = field.shape
    main = jnp.concatenate([above[None], jnp.transpose(field, (1, 0, 2)), below[None]], axis=0)
    main = main.reshape((rows + 2) * channels, width)
    pick = np.zeros((2, width), np.float32)
    pick[0, 0] = pick[1, width - 1] = 1.0
    ends = jnp.einsum("ry,ny->rn", pick.astype(BF), main, preferred_element_type=F32).astype(BF)
    return main, ends


def by_rows(field):
    channels, rows, width = field.shape
    main = jnp.transpose(field, (1, 0, 2)).reshape(rows * channels, width)
    pick = np.zeros((2, width), np.float32)
    pick[0, 0] = pick[1, width - 1] = 1.0
    ends = jnp.einsum("ry,ny->rn", pick.astype(BF), main, preferred_element_type=F32).astype(BF)
    return main, ends


def edge_rows(main, side, channels):
    return (
        jnp.concatenate([main[:channels], side[:channels]], axis=1),
        jnp.concatenate([main[-channels:], side[-channels:]], axis=1),
    )


def across_rows(first, last):
    return swap(last, "gx"), swap(first, "gx", back=True)


def across_columns(ends):
    return swap(ends[:1], "gy", back=True), swap(ends[1:], "gy")


def side_slots():
    place = np.zeros((2, 128), np.float32)
    place[0, 0] = place[1, 127] = 1.0
    return place.astype(BF)


def place_columns(right, left, slots):
    return jnp.einsum(
        "rn,rk->nk", jnp.concatenate([right, left]), slots, preferred_element_type=F32
    ).astype(BF)


def exchange(value, axes):
    return lax.all_to_all(value, axes, split_axis=0, concat_axis=0, tiled=True)


def pdot(form, left, right):
    return jnp.einsum(form, left, right, preferred_element_type=F32)


def weight_grads(spec, dmixed):
    real_s, imag_s = (spec[:, 0], spec[:, 1])
    real_d, imag_d = (dmixed[:, 0], dmixed[:, 1])
    form_w = "mcq,mdq->cdmq"
    grad_real = pdot(form_w, real_s, real_d) + pdot(form_w, imag_s, imag_d)
    grad_imag = pdot(form_w, real_s, imag_d) - pdot(form_w, imag_s, real_d)
    return jnp.stack([grad_real, grad_imag], axis=2)


def body(field_in, spectral_weight, conv_weight, conv_bias, upstream):
    strips, pieces = lax.axis_size("gx"), lax.axis_size("gy")
    owners = strips * pieces
    _, channels, width_x, width_y = field_in.shape
    length_x, length_y = width_x * strips, width_y * pieces
    scale = 1.0 / (length_x * length_y)
    both = ("gx", "gy")
    share = (strips, channels // strips, width_x, width_y)
    whole = (channels, width_x, width_y)

    table_x, table_y = x_table(length_x, owners), y_table(length_y, width_y)
    hold = lax.optimization_barrier
    tables = [
        jnp.asarray(np.concatenate([table_x, table_y[:width_y], table_y[width_y:]], axis=1)),
        jnp.asarray(np.concatenate([table_x.T, table_y], axis=0)),
    ]

    field = field_in[0]
    bias = jnp.broadcast_to(conv_bias[:, None], (channels, 128))
    block = exchange(field.reshape(share), "gx")
    main, ends = by_rows(field)
    right, left = across_columns(ends)
    weight = jnp.transpose(spectral_weight, (3, 2, 0, 1, 4))
    matrix = conv_matrix(conv_weight)
    block, weight, matrix = hold((block, weight, matrix))
    parts = to_modes(block, False, 1.0, tables, owners)
    parts, right, left, places = hold((parts, right, left, side_slots()))
    parts = exchange(parts, both)
    side = place_columns(right, left, places)
    first, last = edge_rows(main, side, channels)
    parts, first, last = hold((parts, first, last))
    mixed, spec = mix(parts, weight, 1, strips)
    arrived = exchange(mixed, both)
    above, below = across_rows(first, last)
    local = conv(matrix, main, side, above, below, bias)
    arrived, local = hold((arrived, local))
    back = to_field(arrived, True, scale, tables, share)
    spectral = exchange(back, "gx").reshape(whole)

    dpre, activation = gate_both(local, spectral, upstream[0])

    dblock = exchange(dpre.reshape(share), "gx")
    dabove, dbelow = across_edges(dpre)
    dparts = to_modes(dblock, True, scale, tables, owners)
    dparts, dhere, dabove, dbelow, taps, dweight = hold(
        (dparts, dpre, dabove, dbelow, conv_weight, spectral_weight)
    )
    dparts = exchange(dparts, both)
    dmatrix = conv_matrix(jnp.transpose(taps[::-1], (0, 2, 1)))
    dweight = jnp.transpose(dweight, (3, 2, 1, 0, 4))
    dmain, dends = stack_rows(dhere, dabove, dbelow)
    dparts, dends, dmain, dmatrix, dweight = hold((dparts, dends, dmain, dmatrix, dweight))
    dmixed, dspec = mix(dparts, dweight, -1, strips)
    darrived = exchange(dmixed, both)
    dright, dleft = across_columns(dends)
    dback = to_field(darrived, False, 1.0, tables, share)
    dback, dright, dleft, places, spec, dspec = hold((dback, dright, dleft, places, spec, dspec))
    dfield = exchange(dback, "gx").reshape(whole)
    back_local = conv_stacked(dmatrix, dmain, place_columns(dright, dleft, places), jnp.zeros_like(bias), width_x)
    slots = M1 // owners
    weight_grad = weight_grads(by_mode(spec, slots), by_mode(dspec, slots))
    dfield, back_local, weight_grad = hold((dfield, back_local, weight_grad))
    field_grad = add_field(back_local, dfield)
    return (activation[None], field_grad[None], weight_grad)


def solution(mesh):
    return jax.shard_map(
        body,
        mesh=mesh,
        in_specs=(
            P("dp", None, "gx", "gy"),
            P(None, None, None, ("gx", "gy"), None),
            P(),
            P(),
            P("dp", None, "gx", "gy"),
        ),
        out_specs=(
            P("dp", None, "gx", "gy"),
            P("dp", None, "gx", "gy"),
            P("dp", None, None, ("gx", "gy"), None),
        ),
        check_vma=False,
    )
```

```python
import functools
import math

import jax
import jax.numpy as jnp
import numpy as np
from jax import lax
from jax.experimental import pallas as pl
from jax.experimental.pallas import tpu as pltpu
from jax.sharding import PartitionSpec as P

M1 = 128
M2 = 128
BF = jnp.bfloat16
F32 = jnp.float32


def dot(left, right):
    return jnp.dot(left, right, preferred_element_type=F32)


@functools.lru_cache(maxsize=None)
def x_table(length, owners):
    slots = M1 // owners
    order = np.arange(M1).reshape(owners, slots).T.reshape(-1)
    modes = np.where(order < M1 // 2, order, order + length - M1)
    angle = (modes[:, None] * np.arange(length)[None, :] % length) * (2.0 * math.pi / length)
    table = np.concatenate([np.cos(angle), -np.sin(angle)], axis=0)
    return table.astype(np.float32).astype(jnp.bfloat16)


@functools.lru_cache(maxsize=None)
def y_table(length, width):
    angle = (np.arange(width)[:, None] * np.arange(M2)[None, :] % length) * (2.0 * math.pi / length)
    cosine, sine = np.cos(angle), np.sin(angle)
    table = np.concatenate(
        [np.concatenate([cosine, -sine], axis=1), np.concatenate([sine, cosine], axis=1)], axis=0
    )
    return table.astype(np.float32).astype(jnp.bfloat16)


def turn(values, quarter, sign):
    half = values.shape[1] // 2
    lane = lax.broadcasted_iota(jnp.int32, (1, 2 * half), 1)
    second = lane >= half
    q = jnp.where(second, lane - half, lane)
    step = lax.rem(q * quarter, 4)
    one = jnp.where(step == 0, 1.0, jnp.where(step == 2, -1.0, 0.0))
    imag = jnp.where(step == 1, 1.0, jnp.where(step == 3, -1.0, 0.0)) * sign
    swap = jnp.concatenate([values[:, half:], values[:, :half]], axis=1)
    return values * one + swap * jnp.where(second, imag, -imag)


def column_weight(half):
    lane = lax.broadcasted_iota(jnp.int32, (1, 2 * half), 1)
    return jnp.where((lane == 0) | (lane == half), 1.0, 2.0)


def resident(value):
    return pltpu.with_memory_space_constraint(value, pltpu.VMEM)


def on_chip(kernel, outs, scratch, name, *values, place=pltpu.VMEM, apart=()):
    spec = pl.BlockSpec(memory_space=pltpu.VMEM)
    many = isinstance(outs, list)
    return pl.pallas_call(
        kernel,
        in_specs=[spec] * len(values),
        out_specs=[spec] * len(outs) if many else spec,
        out_shape=[place(*out) for out in outs] if many else place(*outs),
        scratch_shapes=scratch,
        compiler_params=pltpu.CompilerParams(vmem_limit_bytes=24 << 20),
        name=name,
    )(*[value if index in apart else resident(value) for index, value in enumerate(values)])


def forward_kernel(weighted, factor, block_ref, table_ref, out_ref, rows_ref):
    length = block_ref.shape[0] * block_ref.shape[2]
    owners, rows, _ = out_ref.shape
    _, channels, _, width = block_ref.shape
    slots = M1 // owners
    for channel in range(channels):
        block = block_ref[:, channel].reshape(-1, width)
        spec_x = dot(table_ref[:, :length], block)
        if factor != 1.0:
            spec_x = spec_x * factor
        spec_x = spec_x.astype(BF)
        spec = dot(spec_x[:M1], table_ref[:, length : length + 2 * M2])
        spec = spec + dot(spec_x[M1:], table_ref[:, length + 2 * M2 :])
        spec = turn(spec, lax.axis_index("gy"), -1.0)
        if weighted:
            spec = spec * column_weight(M2)
        for slot in range(slots):
            for part in range(2):
                rows_ref[(channel * slots + slot) * 2 + part] = spec[
                    slot * owners : (slot + 1) * owners, part * M2 : (part + 1) * M2
                ]
    out_ref[...] = jnp.transpose(rows_ref[...], (1, 0, 2)).astype(BF)


def to_modes(block, weighted, factor, tables, owners):
    rows = block.shape[1] * (M1 // owners) * 2
    return on_chip(
        functools.partial(forward_kernel, weighted, factor),
        ((owners, rows, M2), BF),
        [pltpu.VMEM((rows, owners, M2), F32)],
        "to_modes",
        block,
        tables[0],
        place=jax.ShapeDtypeStruct,
    )


def inverse_kernel(weighted, factor, spec_ref, table_ref, out_ref, rows_ref):
    owners = spec_ref.shape[0]
    strips, channels, rows, width = out_ref.shape
    length = strips * rows
    slots = M1 // owners
    rows_ref[...] = jnp.transpose(spec_ref[...].astype(F32), (1, 0, 2))
    for channel in range(channels):
        spec = jnp.concatenate(
            [
                jnp.concatenate(
                    [rows_ref[(channel * slots + slot) * 2 + part] for part in range(2)], axis=1
                )
                for slot in range(slots)
            ],
            axis=0,
        )
        spec = turn(spec, lax.axis_index("gy"), 1.0)
        if weighted:
            spec = spec * column_weight(M2)
        spec = spec.astype(BF)
        over_y = [
            lax.dot_general(
                spec, table_ref[first : first + width], (((1,), (1,)), ((), ())), preferred_element_type=F32
            ).astype(BF)
            for first in (length, length + width)
        ]
        total = dot(table_ref[:length], jnp.concatenate(over_y, axis=0))
        if factor != 1.0:
            total = total * factor
        out_ref[:, channel] = total.astype(BF).reshape(strips, rows, width)


def to_field(spec, weighted, factor, tables, shape):
    owners, rows, _ = spec.shape
    return on_chip(
        functools.partial(inverse_kernel, weighted, factor),
        (shape, BF),
        [pltpu.VMEM((rows, owners, M2), F32)],
        "to_field",
        spec,
        tables[1],
    )


def mix_kernel(sign, parts_ref, weight_ref, out_ref, spec_ref, sum_ref, mixed_ref, place_ref):
    strips, rows, kept = spec_ref.shape
    pieces = parts_ref.shape[0] // strips
    slots, _, ins, outs, _ = weight_ref.shape
    share = ins // strips
    total = jnp.sum(parts_ref[...].reshape(strips, pieces, rows, kept).astype(F32), axis=1).astype(BF)
    spec_ref[...] = total
    sum_ref[...] = total.astype(F32)
    for slot in range(slots):
        real = jnp.zeros((outs, kept), F32)
        imag = jnp.zeros((outs, kept), F32)
        for channel in range(ins):
            strip, row = channel // share, (channel % share * slots + slot) * 2
            real_s = sum_ref[strip, row : row + 1, :]
            imag_s = sum_ref[strip, row + 1 : row + 2, :]
            real_w = weight_ref[slot, 0, channel].astype(F32)
            imag_w = weight_ref[slot, 1, channel].astype(F32)
            if sign > 0:
                real = real + (real_s * real_w - imag_s * imag_w)
                imag = imag + (real_s * imag_w + imag_s * real_w)
            else:
                real = real + (real_s * real_w + imag_s * imag_w)
                imag = imag + (imag_s * real_w - real_s * imag_w)
        mixed_ref[slot * 2] = real
        mixed_ref[slot * 2 + 1] = imag
    share = outs // strips
    for channel in range(share):
        for row in range(2 * slots):
            place_ref[:, channel * 2 * slots + row, :] = mixed_ref[
                row, pl.ds(channel, strips, stride=share), :
            ]
    placed = place_ref[...].astype(BF)
    out_ref[...] = jnp.broadcast_to(placed[:, None], (strips, pieces, rows, kept)).reshape(
        strips * pieces, rows, kept
    )


def mix(parts, weight, sign, strips):
    owners, rows, kept = parts.shape
    slots, _, _, outs, _ = weight.shape
    return on_chip(
        functools.partial(mix_kernel, sign),
        [((owners, rows, kept), BF), ((strips, rows, kept), BF)],
        [
            pltpu.VMEM((strips, rows, kept), F32),
            pltpu.VMEM((2 * slots, outs, kept), F32),
            pltpu.VMEM((strips, rows, kept), F32),
        ],
        "mix",
        parts,
        weight,
    )


def by_mode(rows, slots):
    strips, count, kept = rows.shape
    split = rows.reshape(strips, count // slots // 2, slots, 2, kept)
    return jnp.transpose(split, (2, 3, 0, 1, 4)).reshape(slots, 2, -1, kept)


CHUNK = 2


def gate_kernel(local_ref, field_ref, up_ref, grad_out, act_out, grad_ref, act_ref, sems):
    copies = []
    for place, first in enumerate(range(0, local_ref.shape[0], CHUNK)):
        piece = pl.ds(first, CHUNK)
        pre = field_ref[piece].astype(F32) + local_ref[piece]
        gate = 0.5 + 0.5 * jnp.tanh(0.5 * pre)
        grad_ref[piece] = (up_ref[piece].astype(F32) * gate * (1.0 + pre * (1.0 - gate))).astype(BF)
        act_ref[piece] = pre * gate
        for index, (ref, out) in enumerate(((grad_ref, grad_out), (act_ref, act_out))):
            copies.append(pltpu.make_async_copy(ref.at[piece], out.at[piece], sems.at[index, place]))
            copies[-1].start()
    for copy in copies:
        copy.wait()


def gate_both(local, field, upstream):
    shape = local.shape
    vmem, hbm = pl.BlockSpec(memory_space=pltpu.VMEM), pl.BlockSpec(memory_space=pltpu.HBM)
    return pl.pallas_call(
        gate_kernel,
        in_specs=[vmem] * 3,
        out_specs=[hbm] * 2,
        out_shape=[jax.ShapeDtypeStruct(shape, BF), jax.ShapeDtypeStruct(shape, F32)],
        scratch_shapes=[
            pltpu.VMEM(shape, BF),
            pltpu.VMEM(shape, F32),
            pltpu.SemaphoreType.DMA((2, shape[0] // CHUNK)),
        ],
        compiler_params=pltpu.CompilerParams(vmem_limit_bytes=24 << 20),
        name="gate_both",
    )(resident(local), resident(field), resident(upstream))


def add_kernel(local_ref, field_ref, out, out_ref, sems):
    copies = []
    for place, first in enumerate(range(0, local_ref.shape[0], CHUNK)):
        piece = pl.ds(first, CHUNK)
        out_ref[piece] = field_ref[piece].astype(F32) + local_ref[piece]
        copies.append(pltpu.make_async_copy(out_ref.at[piece], out.at[piece], sems.at[place]))
        copies[-1].start()
    for copy in copies:
        copy.wait()


def add_field(local, field):
    shape = local.shape
    vmem, hbm = pl.BlockSpec(memory_space=pltpu.VMEM), pl.BlockSpec(memory_space=pltpu.HBM)
    return pl.pallas_call(
        add_kernel,
        in_specs=[vmem, vmem],
        out_specs=hbm,
        out_shape=jax.ShapeDtypeStruct(shape, F32),
        scratch_shapes=[
            pltpu.VMEM(shape, F32),
            pltpu.SemaphoreType.DMA((shape[0] // CHUNK,)),
        ],
        compiler_params=pltpu.CompilerParams(vmem_limit_bytes=24 << 20),
        name="add_field",
    )(resident(local), resident(field))


CONV_ROWS = 4


def conv_matrix(weight):
    outs, ins = weight.shape[1:]
    band = jnp.transpose(weight.reshape(3, 3, outs, ins), (1, 2, 0, 3)).reshape(3 * outs, 3 * ins)
    return jnp.concatenate(
        [
            jnp.pad(band, ((0, 0), (row * ins, (CONV_ROWS - 1 - row) * ins)))
            for row in range(CONV_ROWS)
        ],
        axis=0,
    )


def conv_kernel(
    matrix_ref, main_hbm, side_hbm, above_ref, below_ref, bias_ref, out_ref, all_ref, sems
):
    ins = matrix_ref.shape[1] // (CONV_ROWS + 2)
    outs, rows, width = out_ref.shape
    full = all_ref.shape[1]
    window = (CONV_ROWS + 2) * ins
    tall = 2 * CONV_ROWS
    inner = pl.ds(ins, rows * ins)
    copies = [
        pltpu.make_async_copy(main_hbm, all_ref.at[inner, pl.ds(0, width)], sems.at[0]),
        pltpu.make_async_copy(side_hbm, all_ref.at[inner, pl.ds(width, full - width)], sems.at[1]),
    ]
    for copy in copies:
        copy.start()
    all_ref[:ins, :] = above_ref[...]
    all_ref[(rows + 1) * ins :, :] = below_ref[...]
    for copy in copies:
        copy.wait()

    @pl.loop(0, rows // tall)
    def _(step):
        pieces = []
        for part in range(tall // CONV_ROWS):
            start = pl.multiple_of((step * tall + part * CONV_ROWS) * ins, ins)
            taps = dot(matrix_ref[...], all_ref[pl.ds(start, window), :])
            for row in range(CONV_ROWS):
                base = row * 3 * outs
                low = pltpu.roll(taps[base : base + outs], 1, 1)[:, :width]
                mid = taps[base + outs : base + 2 * outs, :width]
                high = pltpu.roll(taps[base + 2 * outs : base + 3 * outs], full - 1, 1)[:, :width]
                pieces.append(low + mid + high + bias_ref[:, :1])
        first = pl.multiple_of(step * tall, tall)
        out_ref[:, pl.ds(first, tall), :] = jnp.transpose(jnp.stack(pieces, axis=0), (1, 0, 2))


def conv(matrix, main, side, above, below, bias):
    outs = matrix.shape[0] // (3 * CONV_ROWS)
    ins = above.shape[0]
    rows, width = main.shape[0] // ins, main.shape[1]
    vmem, hbm = pl.BlockSpec(memory_space=pltpu.VMEM), pl.BlockSpec(memory_space=pltpu.HBM)
    return pl.pallas_call(
        conv_kernel,
        in_specs=[vmem, hbm, hbm, vmem, vmem, vmem],
        out_specs=vmem,
        out_shape=pltpu.VMEM((outs, rows, width), F32),
        scratch_shapes=[
            pltpu.VMEM(((rows + 2) * ins, above.shape[1]), BF),
            pltpu.SemaphoreType.DMA((2,)),
        ],
        compiler_params=pltpu.CompilerParams(vmem_limit_bytes=24 << 20),
        name="conv",
    )(
        resident(matrix),
        pltpu.with_memory_space_constraint(main, pltpu.HBM),
        pltpu.with_memory_space_constraint(side, pltpu.HBM),
        resident(above),
        resident(below),
        resident(bias),
    )


def conv_stacked_kernel(matrix_ref, main_ref, side_ref, bias_ref, out_ref):
    ins = matrix_ref.shape[1] // (CONV_ROWS + 2)
    outs, rows, width = out_ref.shape
    window = (CONV_ROWS + 2) * ins
    tall = 2 * CONV_ROWS

    @pl.loop(0, rows // tall)
    def _(step):
        pieces = []
        for part in range(tall // CONV_ROWS):
            start = pl.multiple_of((step * tall + part * CONV_ROWS) * ins, ins)
            main = dot(matrix_ref[...], main_ref[pl.ds(start, window), :])
            side = dot(matrix_ref[...], side_ref[pl.ds(start, window), :])
            taps = jnp.concatenate([main, side], axis=1)
            full = taps.shape[1]
            for row in range(CONV_ROWS):
                base = row * 3 * outs
                low = pltpu.roll(taps[base : base + outs], 1, 1)[:, :width]
                mid = taps[base + outs : base + 2 * outs, :width]
                high = pltpu.roll(taps[base + 2 * outs : base + 3 * outs], full - 1, 1)[:, :width]
                pieces.append(low + mid + high + bias_ref[:, :1])
        first = pl.multiple_of(step * tall, tall)
        out_ref[:, pl.ds(first, tall), :] = jnp.transpose(jnp.stack(pieces, axis=0), (1, 0, 2))


def conv_stacked(matrix, main, side, bias, rows):
    outs = matrix.shape[0] // (3 * CONV_ROWS)
    return on_chip(
        conv_stacked_kernel,
        ((outs, rows, main.shape[1]), F32),
        [],
        "conv_stacked",
        matrix,
        pltpu.with_memory_space_constraint(main, pltpu.HBM),
        side,
        bias,
        apart=(1,),
    )


def swap(value, axis, back=False):
    count = lax.axis_size(axis)
    pairs = [(i, i + 1) for i in range(count - 1)]
    if back:
        pairs = [(b, a) for a, b in pairs]
    return lax.ppermute(value, axis, pairs)


def across_edges(field):
    return swap(field[:, -1], "gx"), swap(field[:, 0], "gx", back=True)


def stack_rows(field, above, below):
    channels, rows, width = field.shape
    main = jnp.concatenate([above[None], jnp.transpose(field, (1, 0, 2)), below[None]], axis=0)
    main = main.reshape((rows + 2) * channels, width)
    pick = np.zeros((2, width), np.float32)
    pick[0, 0] = pick[1, width - 1] = 1.0
    ends = jnp.einsum("ry,ny->rn", pick.astype(BF), main, preferred_element_type=F32).astype(BF)
    return main, ends


def by_rows(field):
    channels, rows, width = field.shape
    main = jnp.transpose(field, (1, 0, 2)).reshape(rows * channels, width)
    pick = np.zeros((2, width), np.float32)
    pick[0, 0] = pick[1, width - 1] = 1.0
    ends = jnp.einsum("ry,ny->rn", pick.astype(BF), main, preferred_element_type=F32).astype(BF)
    return main, ends


def edge_rows(main, side, channels):
    return (
        jnp.concatenate([main[:channels], side[:channels]], axis=1),
        jnp.concatenate([main[-channels:], side[-channels:]], axis=1),
    )


def across_rows(first, last):
    return swap(last, "gx"), swap(first, "gx", back=True)


def across_columns(ends):
    return swap(ends[:1], "gy", back=True), swap(ends[1:], "gy")


def side_slots():
    place = np.zeros((2, 128), np.float32)
    place[0, 0] = place[1, 127] = 1.0
    return place.astype(BF)


def place_columns(right, left, slots):
    return jnp.einsum(
        "rn,rk->nk", jnp.concatenate([right, left]), slots, preferred_element_type=F32
    ).astype(BF)


def exchange(value, axes):
    return lax.all_to_all(value, axes, split_axis=0, concat_axis=0, tiled=True)


def pdot(form, left, right):
    return jnp.einsum(form, left, right, preferred_element_type=F32)


def weight_grads(spec, dmixed):
    real_s, imag_s = (spec[:, 0], spec[:, 1])
    real_d, imag_d = (dmixed[:, 0], dmixed[:, 1])
    form_w = "mcq,mdq->cdmq"
    grad_real = pdot(form_w, real_s, real_d) + pdot(form_w, imag_s, imag_d)
    grad_imag = pdot(form_w, real_s, imag_d) - pdot(form_w, imag_s, real_d)
    return jnp.stack([grad_real, grad_imag], axis=2)


def body(field_in, spectral_weight, conv_weight, conv_bias, upstream):
    strips, pieces = lax.axis_size("gx"), lax.axis_size("gy")
    owners = strips * pieces
    _, channels, width_x, width_y = field_in.shape
    length_x, length_y = width_x * strips, width_y * pieces
    scale = 1.0 / (length_x * length_y)
    both = ("gx", "gy")
    share = (strips, channels // strips, width_x, width_y)
    whole = (channels, width_x, width_y)

    table_x, table_y = x_table(length_x, owners), y_table(length_y, width_y)
    hold = lax.optimization_barrier
    tables = [
        jnp.asarray(np.concatenate([table_x, table_y[:width_y], table_y[width_y:]], axis=1)),
        jnp.asarray(np.concatenate([table_x.T, table_y], axis=0)),
    ]

    field = field_in[0]
    bias = jnp.broadcast_to(conv_bias[:, None], (channels, 128))
    block = exchange(field.reshape(share), "gx")
    main, ends = by_rows(field)
    right, left = across_columns(ends)
    weight = jnp.transpose(spectral_weight, (3, 2, 0, 1, 4))
    matrix = conv_matrix(conv_weight)
    block, weight, matrix = hold((block, weight, matrix))
    parts = to_modes(block, False, 1.0, tables, owners)
    parts, right, left, places = hold((parts, right, left, side_slots()))
    parts = exchange(parts, both)
    side = place_columns(right, left, places)
    above, below = across_rows(*edge_rows(main, side, channels))
    mixed, spec = mix(parts, weight, 1, strips)
    mixed, above, below = hold((mixed, above, below))
    arrived = exchange(mixed, both)
    local = conv(matrix, main, side, above, below, bias)
    arrived, local = hold((arrived, local))
    back = to_field(arrived, True, scale, tables, share)
    spectral = exchange(back, "gx").reshape(whole)

    dpre, activation = gate_both(local, spectral, upstream[0])

    dblock = exchange(dpre.reshape(share), "gx")
    dabove, dbelow = across_edges(dpre)
    dparts = to_modes(dblock, True, scale, tables, owners)
    dparts, dhere, dabove, dbelow, taps, dweight = hold(
        (dparts, dpre, dabove, dbelow, conv_weight, spectral_weight)
    )
    dparts = exchange(dparts, both)
    dmatrix = conv_matrix(jnp.transpose(taps[::-1], (0, 2, 1)))
    dweight = jnp.transpose(dweight, (3, 2, 1, 0, 4))
    dmain, dends = stack_rows(dhere, dabove, dbelow)
    dparts, dends, dmain, dmatrix, dweight = hold((dparts, dends, dmain, dmatrix, dweight))
    dmixed, dspec = mix(dparts, dweight, -1, strips)
    darrived = exchange(dmixed, both)
    dright, dleft = across_columns(dends)
    dback = to_field(darrived, False, 1.0, tables, share)
    dback, dright, dleft, places, spec, dspec = hold((dback, dright, dleft, places, spec, dspec))
    dfield = exchange(dback, "gx").reshape(whole)
    back_local = conv_stacked(dmatrix, dmain, place_columns(dright, dleft, places), jnp.zeros_like(bias), width_x)
    slots = M1 // owners
    weight_grad = weight_grads(by_mode(spec, slots), by_mode(dspec, slots))
    dfield, back_local, weight_grad = hold((dfield, back_local, weight_grad))
    field_grad = add_field(back_local, dfield)
    return (activation[None], field_grad[None], weight_grad)


def solution(mesh):
    return jax.shard_map(
        body,
        mesh=mesh,
        in_specs=(
            P("dp", None, "gx", "gy"),
            P(None, None, None, ("gx", "gy"), None),
            P(),
            P(),
            P("dp", None, "gx", "gy"),
        ),
        out_specs=(
            P("dp", None, "gx", "gy"),
            P("dp", None, "gx", "gy"),
            P("dp", None, None, ("gx", "gy"), None),
        ),
        check_vma=False,
    )
```

```python
import functools
import math

import jax
import jax.numpy as jnp
import numpy as np
from jax import lax
from jax.experimental import pallas as pl
from jax.experimental.pallas import tpu as pltpu
from jax.sharding import PartitionSpec as P

M1 = 128
M2 = 128
BF = jnp.bfloat16
F32 = jnp.float32


def dot(left, right):
    return jnp.dot(left, right, preferred_element_type=F32)


@functools.lru_cache(maxsize=None)
def x_table(length, owners):
    slots = M1 // owners
    order = np.arange(M1).reshape(owners, slots).T.reshape(-1)
    modes = np.where(order < M1 // 2, order, order + length - M1)
    angle = (modes[:, None] * np.arange(length)[None, :] % length) * (2.0 * math.pi / length)
    table = np.concatenate([np.cos(angle), -np.sin(angle)], axis=0)
    return table.astype(np.float32).astype(jnp.bfloat16)


@functools.lru_cache(maxsize=None)
def y_table(length, width):
    angle = (np.arange(width)[:, None] * np.arange(M2)[None, :] % length) * (2.0 * math.pi / length)
    cosine, sine = np.cos(angle), np.sin(angle)
    table = np.concatenate(
        [np.concatenate([cosine, -sine], axis=1), np.concatenate([sine, cosine], axis=1)], axis=0
    )
    return table.astype(np.float32).astype(jnp.bfloat16)


def turn(values, quarter, sign):
    half = values.shape[1] // 2
    lane = lax.broadcasted_iota(jnp.int32, (1, 2 * half), 1)
    second = lane >= half
    q = jnp.where(second, lane - half, lane)
    step = lax.rem(q * quarter, 4)
    one = jnp.where(step == 0, 1.0, jnp.where(step == 2, -1.0, 0.0))
    imag = jnp.where(step == 1, 1.0, jnp.where(step == 3, -1.0, 0.0)) * sign
    swap = jnp.concatenate([values[:, half:], values[:, :half]], axis=1)
    return values * one + swap * jnp.where(second, imag, -imag)


def column_weight(half):
    lane = lax.broadcasted_iota(jnp.int32, (1, 2 * half), 1)
    return jnp.where((lane == 0) | (lane == half), 1.0, 2.0)


def resident(value):
    return pltpu.with_memory_space_constraint(value, pltpu.VMEM)


def on_chip(kernel, outs, scratch, name, *values, place=pltpu.VMEM, apart=()):
    spec = pl.BlockSpec(memory_space=pltpu.VMEM)
    many = isinstance(outs, list)
    return pl.pallas_call(
        kernel,
        in_specs=[spec] * len(values),
        out_specs=[spec] * len(outs) if many else spec,
        out_shape=[place(*out) for out in outs] if many else place(*outs),
        scratch_shapes=scratch,
        compiler_params=pltpu.CompilerParams(vmem_limit_bytes=24 << 20),
        name=name,
    )(*[value if index in apart else resident(value) for index, value in enumerate(values)])


def forward_kernel(weighted, factor, block_ref, table_ref, out_ref, rows_ref):
    length = block_ref.shape[0] * block_ref.shape[2]
    owners, rows, _ = out_ref.shape
    _, channels, _, width = block_ref.shape
    slots = M1 // owners
    for channel in range(channels):
        block = block_ref[:, channel].reshape(-1, width)
        spec_x = dot(table_ref[:, :length], block)
        if factor != 1.0:
            spec_x = spec_x * factor
        spec_x = spec_x.astype(BF)
        spec = dot(spec_x[:M1], table_ref[:, length : length + 2 * M2])
        spec = spec + dot(spec_x[M1:], table_ref[:, length + 2 * M2 :])
        spec = turn(spec, lax.axis_index("gy"), -1.0)
        if weighted:
            spec = spec * column_weight(M2)
        for slot in range(slots):
            for part in range(2):
                rows_ref[(channel * slots + slot) * 2 + part] = spec[
                    slot * owners : (slot + 1) * owners, part * M2 : (part + 1) * M2
                ]
    out_ref[...] = jnp.transpose(rows_ref[...], (1, 0, 2)).astype(BF)


def to_modes(block, weighted, factor, tables, owners):
    rows = block.shape[1] * (M1 // owners) * 2
    return on_chip(
        functools.partial(forward_kernel, weighted, factor),
        ((owners, rows, M2), BF),
        [pltpu.VMEM((rows, owners, M2), F32)],
        "to_modes",
        block,
        tables[0],
        place=jax.ShapeDtypeStruct,
    )


def inverse_kernel(weighted, factor, spec_ref, table_ref, out_ref, rows_ref):
    owners = spec_ref.shape[0]
    strips, channels, rows, width = out_ref.shape
    length = strips * rows
    slots = M1 // owners
    rows_ref[...] = jnp.transpose(spec_ref[...].astype(F32), (1, 0, 2))
    for channel in range(channels):
        spec = jnp.concatenate(
            [
                jnp.concatenate(
                    [rows_ref[(channel * slots + slot) * 2 + part] for part in range(2)], axis=1
                )
                for slot in range(slots)
            ],
            axis=0,
        )
        spec = turn(spec, lax.axis_index("gy"), 1.0)
        if weighted:
            spec = spec * column_weight(M2)
        spec = spec.astype(BF)
        over_y = [
            lax.dot_general(
                spec, table_ref[first : first + width], (((1,), (1,)), ((), ())), preferred_element_type=F32
            ).astype(BF)
            for first in (length, length + width)
        ]
        total = dot(table_ref[:length], jnp.concatenate(over_y, axis=0))
        if factor != 1.0:
            total = total * factor
        out_ref[:, channel] = total.astype(BF).reshape(strips, rows, width)


def to_field(spec, weighted, factor, tables, shape):
    owners, rows, _ = spec.shape
    return on_chip(
        functools.partial(inverse_kernel, weighted, factor),
        (shape, BF),
        [pltpu.VMEM((rows, owners, M2), F32)],
        "to_field",
        spec,
        tables[1],
    )


def mix_kernel(sign, parts_ref, weight_ref, out_ref, spec_ref, sum_ref, mixed_ref, place_ref):
    strips, rows, kept = spec_ref.shape
    pieces = parts_ref.shape[0] // strips
    slots, _, ins, outs, _ = weight_ref.shape
    share = ins // strips
    total = jnp.sum(parts_ref[...].reshape(strips, pieces, rows, kept).astype(F32), axis=1).astype(BF)
    spec_ref[...] = total
    sum_ref[...] = total.astype(F32)
    for slot in range(slots):
        real = jnp.zeros((outs, kept), F32)
        imag = jnp.zeros((outs, kept), F32)
        for channel in range(ins):
            strip, row = channel // share, (channel % share * slots + slot) * 2
            real_s = sum_ref[strip, row : row + 1, :]
            imag_s = sum_ref[strip, row + 1 : row + 2, :]
            real_w = weight_ref[slot, 0, channel].astype(F32)
            imag_w = weight_ref[slot, 1, channel].astype(F32)
            if sign > 0:
                real = real + (real_s * real_w - imag_s * imag_w)
                imag = imag + (real_s * imag_w + imag_s * real_w)
            else:
                real = real + (real_s * real_w + imag_s * imag_w)
                imag = imag + (imag_s * real_w - real_s * imag_w)
        mixed_ref[slot * 2] = real
        mixed_ref[slot * 2 + 1] = imag
    share = outs // strips
    for channel in range(share):
        for row in range(2 * slots):
            place_ref[:, channel * 2 * slots + row, :] = mixed_ref[
                row, pl.ds(channel, strips, stride=share), :
            ]
    placed = place_ref[...].astype(BF)
    out_ref[...] = jnp.broadcast_to(placed[:, None], (strips, pieces, rows, kept)).reshape(
        strips * pieces, rows, kept
    )


def mix(parts, weight, sign, strips):
    owners, rows, kept = parts.shape
    slots, _, _, outs, _ = weight.shape
    return on_chip(
        functools.partial(mix_kernel, sign),
        [((owners, rows, kept), BF), ((strips, rows, kept), BF)],
        [
            pltpu.VMEM((strips, rows, kept), F32),
            pltpu.VMEM((2 * slots, outs, kept), F32),
            pltpu.VMEM((strips, rows, kept), F32),
        ],
        "mix",
        parts,
        weight,
    )


def by_mode(rows, slots):
    strips, count, kept = rows.shape
    split = rows.reshape(strips, count // slots // 2, slots, 2, kept)
    return jnp.transpose(split, (2, 3, 0, 1, 4)).reshape(slots, 2, -1, kept)


CHUNK = 8


def gate_kernel(local_ref, field_ref, up_ref, grad_out, act_out, grad_ref, act_ref, sems):
    copies = []
    for place, first in enumerate(range(0, local_ref.shape[0], CHUNK)):
        piece = pl.ds(first, CHUNK)
        pre = field_ref[piece].astype(F32) + local_ref[piece]
        gate = 0.5 + 0.5 * jnp.tanh(0.5 * pre)
        grad_ref[piece] = (up_ref[piece].astype(F32) * gate * (1.0 + pre * (1.0 - gate))).astype(BF)
        act_ref[piece] = pre * gate
        for index, (ref, out) in enumerate(((grad_ref, grad_out), (act_ref, act_out))):
            copies.append(pltpu.make_async_copy(ref.at[piece], out.at[piece], sems.at[index, place]))
            copies[-1].start()
    for copy in copies:
        copy.wait()


def gate_both(local, field, upstream):
    shape = local.shape
    vmem, hbm = pl.BlockSpec(memory_space=pltpu.VMEM), pl.BlockSpec(memory_space=pltpu.HBM)
    return pl.pallas_call(
        gate_kernel,
        in_specs=[vmem] * 3,
        out_specs=[hbm] * 2,
        out_shape=[jax.ShapeDtypeStruct(shape, BF), jax.ShapeDtypeStruct(shape, F32)],
        scratch_shapes=[
            pltpu.VMEM(shape, BF),
            pltpu.VMEM(shape, F32),
            pltpu.SemaphoreType.DMA((2, shape[0] // CHUNK)),
        ],
        compiler_params=pltpu.CompilerParams(vmem_limit_bytes=24 << 20),
        name="gate_both",
    )(resident(local), resident(field), resident(upstream))


def add_kernel(local_ref, field_ref, out, out_ref, sems):
    copies = []
    for place, first in enumerate(range(0, local_ref.shape[0], CHUNK)):
        piece = pl.ds(first, CHUNK)
        out_ref[piece] = field_ref[piece].astype(F32) + local_ref[piece]
        copies.append(pltpu.make_async_copy(out_ref.at[piece], out.at[piece], sems.at[place]))
        copies[-1].start()
    for copy in copies:
        copy.wait()


def add_field(local, field):
    shape = local.shape
    vmem, hbm = pl.BlockSpec(memory_space=pltpu.VMEM), pl.BlockSpec(memory_space=pltpu.HBM)
    return pl.pallas_call(
        add_kernel,
        in_specs=[vmem, vmem],
        out_specs=hbm,
        out_shape=jax.ShapeDtypeStruct(shape, F32),
        scratch_shapes=[
            pltpu.VMEM(shape, F32),
            pltpu.SemaphoreType.DMA((shape[0] // CHUNK,)),
        ],
        compiler_params=pltpu.CompilerParams(vmem_limit_bytes=24 << 20),
        name="add_field",
    )(resident(local), resident(field))


CONV_ROWS = 4


def conv_matrix(weight):
    outs, ins = weight.shape[1:]
    band = jnp.transpose(weight.reshape(3, 3, outs, ins), (1, 2, 0, 3)).reshape(3 * outs, 3 * ins)
    return jnp.concatenate(
        [
            jnp.pad(band, ((0, 0), (row * ins, (CONV_ROWS - 1 - row) * ins)))
            for row in range(CONV_ROWS)
        ],
        axis=0,
    )


def conv_kernel(
    matrix_ref, main_hbm, side_hbm, above_ref, below_ref, bias_ref, out_ref, all_ref, sems
):
    ins = matrix_ref.shape[1] // (CONV_ROWS + 2)
    outs, rows, width = out_ref.shape
    full = all_ref.shape[1]
    window = (CONV_ROWS + 2) * ins
    tall = 2 * CONV_ROWS
    inner = pl.ds(ins, rows * ins)
    copies = [
        pltpu.make_async_copy(main_hbm, all_ref.at[inner, pl.ds(0, width)], sems.at[0]),
        pltpu.make_async_copy(side_hbm, all_ref.at[inner, pl.ds(width, full - width)], sems.at[1]),
    ]
    for copy in copies:
        copy.start()
    all_ref[:ins, :] = above_ref[...]
    all_ref[(rows + 1) * ins :, :] = below_ref[...]
    for copy in copies:
        copy.wait()

    @pl.loop(0, rows // tall)
    def _(step):
        pieces = []
        for part in range(tall // CONV_ROWS):
            start = pl.multiple_of((step * tall + part * CONV_ROWS) * ins, ins)
            taps = dot(matrix_ref[...], all_ref[pl.ds(start, window), :])
            for row in range(CONV_ROWS):
                base = row * 3 * outs
                low = pltpu.roll(taps[base : base + outs], 1, 1)[:, :width]
                mid = taps[base + outs : base + 2 * outs, :width]
                high = pltpu.roll(taps[base + 2 * outs : base + 3 * outs], full - 1, 1)[:, :width]
                pieces.append(low + mid + high + bias_ref[:, :1])
        first = pl.multiple_of(step * tall, tall)
        out_ref[:, pl.ds(first, tall), :] = jnp.transpose(jnp.stack(pieces, axis=0), (1, 0, 2))


def conv(matrix, main, side, above, below, bias):
    outs = matrix.shape[0] // (3 * CONV_ROWS)
    ins = above.shape[0]
    rows, width = main.shape[0] // ins, main.shape[1]
    vmem, hbm = pl.BlockSpec(memory_space=pltpu.VMEM), pl.BlockSpec(memory_space=pltpu.HBM)
    return pl.pallas_call(
        conv_kernel,
        in_specs=[vmem, hbm, hbm, vmem, vmem, vmem],
        out_specs=vmem,
        out_shape=pltpu.VMEM((outs, rows, width), F32),
        scratch_shapes=[
            pltpu.VMEM(((rows + 2) * ins, above.shape[1]), BF),
            pltpu.SemaphoreType.DMA((2,)),
        ],
        compiler_params=pltpu.CompilerParams(vmem_limit_bytes=24 << 20),
        name="conv",
    )(
        resident(matrix),
        pltpu.with_memory_space_constraint(main, pltpu.HBM),
        pltpu.with_memory_space_constraint(side, pltpu.HBM),
        resident(above),
        resident(below),
        resident(bias),
    )


def conv_stacked_kernel(matrix_ref, main_ref, side_ref, bias_ref, out_ref):
    ins = matrix_ref.shape[1] // (CONV_ROWS + 2)
    outs, rows, width = out_ref.shape
    window = (CONV_ROWS + 2) * ins
    tall = 2 * CONV_ROWS

    @pl.loop(0, rows // tall)
    def _(step):
        pieces = []
        for part in range(tall // CONV_ROWS):
            start = pl.multiple_of((step * tall + part * CONV_ROWS) * ins, ins)
            main = dot(matrix_ref[...], main_ref[pl.ds(start, window), :])
            side = dot(matrix_ref[...], side_ref[pl.ds(start, window), :])
            taps = jnp.concatenate([main, side], axis=1)
            full = taps.shape[1]
            for row in range(CONV_ROWS):
                base = row * 3 * outs
                low = pltpu.roll(taps[base : base + outs], 1, 1)[:, :width]
                mid = taps[base + outs : base + 2 * outs, :width]
                high = pltpu.roll(taps[base + 2 * outs : base + 3 * outs], full - 1, 1)[:, :width]
                pieces.append(low + mid + high + bias_ref[:, :1])
        first = pl.multiple_of(step * tall, tall)
        out_ref[:, pl.ds(first, tall), :] = jnp.transpose(jnp.stack(pieces, axis=0), (1, 0, 2))


def conv_stacked(matrix, main, side, bias, rows):
    outs = matrix.shape[0] // (3 * CONV_ROWS)
    return on_chip(
        conv_stacked_kernel,
        ((outs, rows, main.shape[1]), F32),
        [],
        "conv_stacked",
        matrix,
        pltpu.with_memory_space_constraint(main, pltpu.HBM),
        side,
        bias,
        apart=(1,),
    )


def swap(value, axis, back=False):
    count = lax.axis_size(axis)
    pairs = [(i, i + 1) for i in range(count - 1)]
    if back:
        pairs = [(b, a) for a, b in pairs]
    return lax.ppermute(value, axis, pairs)


def across_edges(field):
    return swap(field[:, -1], "gx"), swap(field[:, 0], "gx", back=True)


def stack_rows(field, above, below):
    channels, rows, width = field.shape
    main = jnp.concatenate([above[None], jnp.transpose(field, (1, 0, 2)), below[None]], axis=0)
    main = main.reshape((rows + 2) * channels, width)
    pick = np.zeros((2, width), np.float32)
    pick[0, 0] = pick[1, width - 1] = 1.0
    ends = jnp.einsum("ry,ny->rn", pick.astype(BF), main, preferred_element_type=F32).astype(BF)
    return main, ends


def by_rows(field):
    channels, rows, width = field.shape
    main = jnp.transpose(field, (1, 0, 2)).reshape(rows * channels, width)
    pick = np.zeros((2, width), np.float32)
    pick[0, 0] = pick[1, width - 1] = 1.0
    ends = jnp.einsum("ry,ny->rn", pick.astype(BF), main, preferred_element_type=F32).astype(BF)
    return main, ends


def edge_rows(main, side, channels):
    return (
        jnp.concatenate([main[:channels], side[:channels]], axis=1),
        jnp.concatenate([main[-channels:], side[-channels:]], axis=1),
    )


def across_rows(first, last):
    return swap(last, "gx"), swap(first, "gx", back=True)


def across_columns(ends):
    return swap(ends[:1], "gy", back=True), swap(ends[1:], "gy")


def side_slots():
    place = np.zeros((2, 128), np.float32)
    place[0, 0] = place[1, 127] = 1.0
    return place.astype(BF)


def place_columns(right, left, slots):
    return jnp.einsum(
        "rn,rk->nk", jnp.concatenate([right, left]), slots, preferred_element_type=F32
    ).astype(BF)


def exchange(value, axes):
    return lax.all_to_all(value, axes, split_axis=0, concat_axis=0, tiled=True)


def pdot(form, left, right):
    return jnp.einsum(form, left, right, preferred_element_type=F32)


def weight_grads(spec, dmixed):
    real_s, imag_s = (spec[:, 0], spec[:, 1])
    real_d, imag_d = (dmixed[:, 0], dmixed[:, 1])
    form_w = "mcq,mdq->cdmq"
    grad_real = pdot(form_w, real_s, real_d) + pdot(form_w, imag_s, imag_d)
    grad_imag = pdot(form_w, real_s, imag_d) - pdot(form_w, imag_s, real_d)
    return jnp.stack([grad_real, grad_imag], axis=2)


def body(field_in, spectral_weight, conv_weight, conv_bias, upstream):
    strips, pieces = lax.axis_size("gx"), lax.axis_size("gy")
    owners = strips * pieces
    _, channels, width_x, width_y = field_in.shape
    length_x, length_y = width_x * strips, width_y * pieces
    scale = 1.0 / (length_x * length_y)
    both = ("gx", "gy")
    share = (strips, channels // strips, width_x, width_y)
    whole = (channels, width_x, width_y)

    table_x, table_y = x_table(length_x, owners), y_table(length_y, width_y)
    hold = lax.optimization_barrier
    tables = [
        jnp.asarray(np.concatenate([table_x, table_y[:width_y], table_y[width_y:]], axis=1)),
        jnp.asarray(np.concatenate([table_x.T, table_y], axis=0)),
    ]

    field = field_in[0]
    bias = jnp.broadcast_to(conv_bias[:, None], (channels, 128))
    block = exchange(field.reshape(share), "gx")
    main, ends = by_rows(field)
    right, left = across_columns(ends)
    weight = jnp.transpose(spectral_weight, (3, 2, 0, 1, 4))
    matrix = conv_matrix(conv_weight)
    block, weight, matrix = hold((block, weight, matrix))
    parts = to_modes(block, False, 1.0, tables, owners)
    parts, right, left, places = hold((parts, right, left, side_slots()))
    parts = exchange(parts, both)
    side = place_columns(right, left, places)
    above, below = across_rows(*edge_rows(main, side, channels))
    mixed, spec = mix(parts, weight, 1, strips)
    mixed, above, below = hold((mixed, above, below))
    arrived = exchange(mixed, both)
    local = conv(matrix, main, side, above, below, bias)
    arrived, local = hold((arrived, local))
    back = to_field(arrived, True, scale, tables, share)
    spectral = exchange(back, "gx").reshape(whole)

    dpre, activation = gate_both(local, spectral, upstream[0])

    dblock = exchange(dpre.reshape(share), "gx")
    dabove, dbelow = across_edges(dpre)
    dparts = to_modes(dblock, True, scale, tables, owners)
    dparts, dhere, dabove, dbelow, taps, dweight = hold(
        (dparts, dpre, dabove, dbelow, conv_weight, spectral_weight)
    )
    dparts = exchange(dparts, both)
    dmatrix = conv_matrix(jnp.transpose(taps[::-1], (0, 2, 1)))
    dweight = jnp.transpose(dweight, (3, 2, 1, 0, 4))
    dmain, dends = stack_rows(dhere, dabove, dbelow)
    dparts, dends, dmain, dmatrix, dweight = hold((dparts, dends, dmain, dmatrix, dweight))
    dmixed, dspec = mix(dparts, dweight, -1, strips)
    darrived = exchange(dmixed, both)
    dright, dleft = across_columns(dends)
    dback = to_field(darrived, False, 1.0, tables, share)
    dback, dright, dleft, places, spec, dspec = hold((dback, dright, dleft, places, spec, dspec))
    dfield = exchange(dback, "gx").reshape(whole)
    back_local = conv_stacked(dmatrix, dmain, place_columns(dright, dleft, places), jnp.zeros_like(bias), width_x)
    slots = M1 // owners
    weight_grad = weight_grads(by_mode(spec, slots), by_mode(dspec, slots))
    dfield, back_local, weight_grad = hold((dfield, back_local, weight_grad))
    field_grad = add_field(back_local, dfield)
    return (activation[None], field_grad[None], weight_grad)


def solution(mesh):
    return jax.shard_map(
        body,
        mesh=mesh,
        in_specs=(
            P("dp", None, "gx", "gy"),
            P(None, None, None, ("gx", "gy"), None),
            P(),
            P(),
            P("dp", None, "gx", "gy"),
        ),
        out_specs=(
            P("dp", None, "gx", "gy"),
            P("dp", None, "gx", "gy"),
            P("dp", None, None, ("gx", "gy"), None),
        ),
        check_vma=False,
    )
```
